32 devices in a mesh: seq: 4 (over y, core), dp: 8 (over z, x).
Axes of the slice: x: 2, y: 2, z: 4, core: 2. Of those that a mesh axis runs over, the one named last changes fastest.
Arguments:
- tokens: bfloat16 [8, 2048, 768], P('dp', 'seq'), may hold values from -6 to 6
- lengths: int32 [8, 8], P('dp'), may hold values from 16 to 1536, as said below
- classes: bfloat16 [150, 768], replicated, may hold values from -6 to 6
- norm_gains: bfloat16 [5, 768], replicated, may hold values from 0.5 to 1.5
- mask_gain: bfloat16 [150], replicated, may hold values from 0.5 to 1.5
- enc_qkv: bfloat16 [768, 2304], P('dp'), may hold values from -0.21875 to 0.21875
- enc_out: bfloat16 [768, 768], P('dp'), may hold values from -3 to 3
- enc_up: bfloat16 [768, 3072], P('dp'), may hold values from -0.21875 to 0.21875
- enc_down: bfloat16 [3072, 768], P('dp'), may hold values from -0.109375 to 0.109375
- dec_qkv: bfloat16 [768, 2304], P('dp'), may hold values from -0.21875 to 0.21875
- dec_out: bfloat16 [768, 768], P('dp'), may hold values from -3 to 3
- dec_up: bfloat16 [768, 3072], P('dp'), may hold values from -0.21875 to 0.21875
- dec_down: bfloat16 [3072, 768], P('dp'), may hold values from -0.109375 to 0.109375
- patch_proj: bfloat16 [768, 768], P('dp'), may hold values from -0.21875 to 0.21875
- class_proj: bfloat16 [768, 768], P('dp'), may hold values from -0.21875 to 0.21875
- mask_cot: float32 [8, 2048, 150], P('dp', 'seq'), may hold values from -6 to 6
Outputs:
- masks: float32 [8, 2048, 150], P('dp', 'seq')
- grad_tokens: float32 [8, 2048, 768], P('dp', 'seq')
- grad_classes: float32 [150, 768], replicated
- grad_gains: float32 [5, 768], replicated
- grad_mask_gain: float32 [150], replicated
- grad_enc_qkv: float32 [768, 2304], P('dp')
- grad_enc_out: float32 [768, 768], P('dp')
- grad_enc_up: float32 [768, 3072], P('dp')
- grad_enc_down: float32 [3072, 768], P('dp')
- grad_dec_qkv: float32 [768, 2304], P('dp')
- grad_dec_out: float32 [768, 768], P('dp')
- grad_dec_up: float32 [768, 3072], P('dp')
- grad_dec_down: float32 [3072, 768], P('dp')
- grad_patch_proj: float32 [768, 768], P('dp')
- grad_class_proj: float32 [768, 768], P('dp')
The draws below stay inside these ranges and needn't reach their ends.
Inputs may be any that keep to these rules, and one draw needn't show every extreme that they name: Each row holds the lengths of 8 images in packing order; they sum to 1984, the positions after them being padding; one image of each row has exactly 1536 patches.
All inputs are finite; a program needn't handle non-finite values.
Results may differ from the reference program's by a relative error of at most 0.03.
Values may be sent and summed in bfloat16 or wider, within the bound.
No kernel may reach another device: no remote copies, remote signals or barrier semaphores. Data moves between devices by JAX's collectives and lax.ppermute only.
A program may use at most 320 MiB of HBM per device.

```python
import math
import jax
import jax.numpy as jnp
from jax import lax

D = 768
HEADS = 12
HD = 64
MLP = 3072
CLASSES = 150
SEQ_DEV = 512
IMGS = 8
MIN_IMG = 16
SEQ_LEN = 2048
SEQS = 8


def draw_lengths(key, part):
    key_short, key_long = jax.random.split(jax.random.fold_in(key, 7))
    quota = SEQ_DEV // IMGS
    raw = jax.random.randint(key_short, (SEQS, IMGS - 1), 0, quota - MIN_IMG + 1)
    shorts = quota + raw - jnp.roll(raw, 1, axis=1)
    long_slot = jax.random.randint(key_long, (SEQS, 1), 0, IMGS)
    slots = jnp.arange(IMGS, dtype=jnp.int32)[None, :]
    is_long = slots == long_slot
    short_index = jnp.clip(slots - (slots > long_slot).astype(jnp.int32), 0, IMGS - 2)
    placed = jnp.take_along_axis(shorts, short_index, axis=1)
    longest = SEQ_LEN - SEQ_DEV
    return jnp.where(is_long, longest, placed).astype(jnp.int32)


def block_scale(key, extent, cuts, least, largest):
    factor_of = 1.0
    for position, blocks in cuts:
        draws = jax.random.uniform(jax.random.fold_in(jax.random.fold_in(key, 6), position), (blocks,), jnp.float32, least / len(cuts), largest / len(cuts))
        factor_of = factor_of * jnp.repeat(jnp.exp(draws), extent[position] // blocks).reshape((-1,) + (1,) * (len(extent) - 1 - position))
    return factor_of


def centred(key, shape, spread, reach, cuts=(), held_as=jnp.bfloat16):
    level = block_scale(key, shape, cuts, -0.22, 0.18) if cuts else 1.0
    entries = jax.random.normal(key, shape, jnp.float32) * spread * level
    return jnp.minimum(jnp.maximum(entries, -reach), reach).astype(held_as)


def setup_inputs(seed: int = 0) -> dict:
    keys = jax.random.split(jax.random.key(seed), 17)
    return {
        "tokens": centred(keys[0], (SEQS, SEQ_LEN, D), 1.0, 6.0, ((0, 8), (1, 4))),
        "lengths": draw_lengths(jax.random.fold_in(keys[16], 71), 0),
        "classes": centred(keys[2], (CLASSES, D), 1.0, 6.0),
        "norm_gains": jnp.clip(1.0 + 0.1 * jax.random.normal(keys[3], (5, D), jnp.float32), 0.5, 1.5).astype(jnp.bfloat16),
        "mask_gain": jnp.clip(1.0 + 0.1 * jax.random.normal(keys[4], (CLASSES,), jnp.float32), 0.5, 1.5).astype(jnp.bfloat16),
        "enc_qkv": centred(keys[5], (D, 3 * D), D ** -0.5, 0.21875, ((0, 8),)),
        "enc_out": centred(keys[6], (D, D), 4 ** -0.5, 3.0, ((0, 8),)),
        "enc_up": centred(keys[7], (D, MLP), D ** -0.5, 0.21875, ((0, 8),)),
        "enc_down": centred(keys[8], (MLP, D), MLP ** -0.5, 0.109375, ((0, 8),)),
        "dec_qkv": centred(keys[9], (D, 3 * D), D ** -0.5, 0.21875, ((0, 8),)),
        "dec_out": centred(keys[10], (D, D), 4 ** -0.5, 3.0, ((0, 8),)),
        "dec_up": centred(keys[11], (D, MLP), D ** -0.5, 0.21875, ((0, 8),)),
        "dec_down": centred(keys[12], (MLP, D), MLP ** -0.5, 0.109375, ((0, 8),)),
        "patch_proj": centred(keys[13], (D, D), D ** -0.5, 0.21875, ((0, 8),)),
        "class_proj": centred(keys[14], (D, D), D ** -0.5, 0.21875, ((0, 8),)),
        "mask_cot": centred(keys[15], (SEQS, SEQ_LEN, CLASSES), 1.0, 6.0, ((0, 8), (1, 4)), jnp.float32),
    }


NEG_FILL = -1e+30
PRECISE = lax.Precision.HIGHEST

@jax.custom_vjp
def low(v):
    return lax.optimization_barrier(v.astype(jnp.bfloat16)).astype(jnp.float32)

@jax.custom_vjp
def low_back(v):
    return v

def low_keep(v):
    return (low(v), None)

def low_pass(kept, grad):
    return (grad,)

def back_keep(v):
    return (v, None)

def back_low(kept, grad):
    return (low(grad),)
low.defvjp(low_keep, low_pass)
low_back.defvjp(back_keep, back_low)

def matmul_high(left, right):
    return jnp.dot(left, right, precision=PRECISE, preferred_element_type=jnp.float32)

def norm_rows(values, gain_row):
    centre = values - lax.optimization_barrier(jnp.mean(values, axis=-1, keepdims=True))
    return centre * lax.rsqrt(lax.optimization_barrier(jnp.mean(centre * centre, axis=-1, keepdims=True)) + 1e-06) * gain_row

def class_norm(logits, gain_row):
    centre = logits - lax.optimization_barrier(jnp.mean(logits, axis=-1, keepdims=True))
    return centre * lax.rsqrt(lax.optimization_barrier(jnp.mean(centre * centre, axis=-1, keepdims=True)) + 1e-05) * gain_row

def unit_rows(values):
    return values * lax.rsqrt(lax.optimization_barrier(jnp.sum(values * values, axis=-1, keepdims=True)) + 1e-06)

def segments(seq_lengths, row_count):
    boundary = jnp.cumsum(seq_lengths)
    places = jnp.arange(row_count, dtype=jnp.int32)
    return lax.optimization_barrier(jnp.sum((places[:, None] >= boundary[None, :]).astype(jnp.int32), axis=1)).astype(jnp.int32)

def attention(queries, keys_all, values_all, seg_query, seg_key):
    row_count = queries.shape[0]
    block_rows = math.gcd(row_count, 512)
    block_count = row_count // block_rows
    key_heads = keys_all.reshape(-1, HEADS, HD)
    value_heads = values_all.reshape(-1, HEADS, HD)

    def query_block(inputs):
        query_rows, seg_rows = inputs
        scores = jnp.einsum('qhd,khd->hqk', query_rows, key_heads, precision=PRECISE) * (1.0 / math.sqrt(HD))
        scores = low_back(scores)
        permit = ((seg_rows[:, None] == seg_key[None, :]) | (seg_key[None, :] < 0))[None]
        scores = jnp.where(permit, scores, NEG_FILL)
        row_top = lax.optimization_barrier(jnp.max(scores, axis=-1, keepdims=True))
        log_total = row_top + jnp.log(lax.optimization_barrier(jnp.sum(jnp.exp(scores - row_top), axis=-1, keepdims=True)))
        weights = jnp.exp(scores - log_total)
        return jnp.einsum('hqk,khd->qhd', low(weights), value_heads, precision=PRECISE)
    result = lax.map(jax.checkpoint(query_block), (queries.reshape(block_count, block_rows, HEADS, HD), seg_query.reshape(block_count, block_rows)))
    return result.reshape(row_count, D)

def layer_block(hidden, gain_a, gain_b, w_qkv, w_out, w_up, w_down, segment_ids, class_kv):
    normed = low(norm_rows(hidden, gain_a))
    projected = low(low_back(matmul_high(normed, w_qkv)))
    queries = projected[:, :D]
    keys_all = projected[:, D:2 * D]
    values_all = projected[:, 2 * D:]
    seg_key = segment_ids
    if class_kv is not None:
        keys_all = jnp.concatenate([class_kv[:, :D], keys_all], axis=0)
        values_all = jnp.concatenate([class_kv[:, D:], values_all], axis=0)
        seg_key = jnp.concatenate([jnp.full((class_kv.shape[0],), -1, jnp.int32), segment_ids], axis=0)
    attended = low(low_back(attention(queries, keys_all, values_all, segment_ids, seg_key)))
    middle = hidden + low_back(matmul_high(attended, w_out))
    second = low(norm_rows(middle, gain_b))
    upward = low_back(matmul_high(second, w_up))
    active = low(jax.nn.gelu(upward))
    return middle + low_back(matmul_high(active, w_down))

def reference(tokens, lengths, classes, norm_gains, mask_gain, enc_qkv, enc_out, enc_up, enc_down, dec_qkv, dec_out, dec_up, dec_down, patch_proj, class_proj, mask_cot):
    floats = tuple((item.astype(jnp.float32) for item in (tokens, classes, norm_gains, mask_gain, enc_qkv, enc_out, enc_up, enc_down, dec_qkv, dec_out, dec_up, dec_down, patch_proj, class_proj)))

    def forward(tokens_f, classes_f, gains_f, mask_gain_f, eq_w, eo_w, eu_w, ed_w, dq_w, do_w, du_w, dd_w, patch_w, class_w):
        class_kv = low(matmul_high(low(norm_rows(classes_f, gains_f[2])), dq_w[:, D:]))
        class_unit = low(unit_rows(matmul_high(classes_f, class_w)))

        def one_sequence(inputs):
            hidden, seq_lengths = inputs
            segment_ids = segments(seq_lengths, SEQ_LEN)
            valid_rows = (segment_ids < IMGS).astype(jnp.float32)
            hidden = layer_block(hidden, gains_f[0], gains_f[1], eq_w, eo_w, eu_w, ed_w, segment_ids, None)
            hidden = layer_block(hidden, gains_f[2], gains_f[3], dq_w, do_w, du_w, dd_w, segment_ids, class_kv)
            patches = low(low_back(matmul_high(low(norm_rows(hidden, gains_f[4])), patch_w)))
            logits = low_back(matmul_high(patches, class_unit.T))
            return class_norm(logits, mask_gain_f) * valid_rows[:, None]
        return lax.map(one_sequence, (tokens_f, lengths))
    mask_out, pullback = jax.vjp(forward, *floats)
    gradients = pullback(mask_cot)
    return (mask_out, gradients[0], gradients[1], gradients[2], gradients[3], gradients[4], gradients[5], gradients[6], gradients[7], gradients[8], gradients[9], gradients[10], gradients[11], gradients[12], gradients[13])
```

```python
import jax, jax.numpy as jnp
from jax import lax
from jax.experimental import pallas as pl
from jax.experimental.pallas import tpu as pltpu
from jax.sharding import PartitionSpec as P
HD=64
KB=256
LSE_LANE=10
NEG=-1e30
NT=(((1,),(1,)),((),()))
NN=(((1,),(0,)),((),()))

def split3(v):
    hi=v.astype(jnp.bfloat16).astype(jnp.float32)
    mid=(v-hi).astype(jnp.bfloat16).astype(jnp.float32)
    return hi,mid,v-hi-mid

def fwd_kernel(idx_ref,q_ref,k_ref,v_ref,fq_ref,fk_ref,o_ref,ol_ref,qa_ref,ka,va,s_ref,m_ref,acc_ref):
    rows=q_ref.shape[0]
    cnt=idx_ref[0]
    lane=lax.broadcasted_iota(jnp.int32,(1,128),1)
    low=lane<HD
    q2=q_ref[...]*jnp.bfloat16(0.125)
    fq=fq_ref[...]
    qs=(jnp.where(low,q2,fq),jnp.where(low,fq,q2))
    k2=k_ref[...];v2=v_ref[...];fk=fk_ref[...]
    ka[0]=jnp.where(low,k2,fk);ka[1]=jnp.where(low,fk,k2)
    va[0]=jnp.where(low,v2,fk);va[1]=jnp.where(low,fk,v2)
    m_ref[...]=jnp.full(m_ref.shape,2*NEG,jnp.float32)
    def first(i,_):
        r=pl.ds(pl.multiple_of(idx_ref[i+1]*KB,KB),KB)
        for h in range(2):
            s=lax.dot_general(qs[h],ka[h,r,:],NT,preferred_element_type=jnp.float32)
            s_ref[h,i]=s
            m_ref[h]=jnp.maximum(m_ref[h],jnp.maximum(s[:,:128],s[:,128:]))
        return 0
    lax.fori_loop(0,cnt,first,0)
    tops=[jnp.max(m_ref[h],axis=1,keepdims=True) for h in range(2)]
    acc_ref[...]=jnp.zeros(acc_ref.shape,jnp.float32)
    def second(i,_):
        r=pl.ds(pl.multiple_of(idx_ref[i+1]*KB,KB),KB)
        for h in range(2):
            p=jnp.exp(s_ref[h,i]-tops[h]).astype(jnp.bfloat16)
            acc_ref[h]+=lax.dot_general(p,va[h,r,:],NN,preferred_element_type=jnp.float32)
        return 0
    lax.fori_loop(0,cnt,second,0)
    outs=[]
    for h in range(2):
        base=HD+LSE_LANE if h==0 else LSE_LANE
        acc=acc_ref[h]
        total=acc[:,base:base+1]
        outs.append(acc/total)
        hi,mid,lo=split3(-(tops[h]+jnp.log(total)))
        qa=qs[h].astype(jnp.float32)
        for j,t in enumerate((hi,mid,lo)):
            qa=jnp.where(lane==base+j,t,qa)
        qa_ref[h]=qa.astype(jnp.bfloat16)
    o=jnp.where(low,outs[0],outs[1])
    o_ref[...]=o
    ol_ref[...]=o.astype(jnp.bfloat16)

def attend(q,kv,idx,fq,fk,heads=12):
    rows,d=q.shape
    nk=kv.shape[0]
    pairs=heads//2
    nb=nk//KB
    spec=pltpu.PrefetchScalarGridSpec(num_scalar_prefetch=1,grid=(pairs,),
        in_specs=[pl.BlockSpec((rows,128),lambda p,i:(0,p)),
                  pl.BlockSpec((nk,128),lambda p,i:(0,p)),
                  pl.BlockSpec((nk,128),lambda p,i:(0,p+pairs)),
                  pl.BlockSpec((rows,128),lambda p,i:(0,0)),
                  pl.BlockSpec((nk,128),lambda p,i:(0,0))],
        out_specs=[pl.BlockSpec((rows,128),lambda p,i:(0,p)),
                   pl.BlockSpec((rows,128),lambda p,i:(0,p)),
                   pl.BlockSpec((2,rows,128),lambda p,i:(p,0,0))],
        scratch_shapes=[pltpu.VMEM((2,nk,128),jnp.bfloat16),pltpu.VMEM((2,nk,128),jnp.bfloat16),
                        pltpu.VMEM((2,nb,rows,KB),jnp.float32),pltpu.VMEM((2,rows,128),jnp.float32),
                        pltpu.VMEM((2,rows,128),jnp.float32)])
    return pl.pallas_call(fwd_kernel,grid_spec=spec,
        out_shape=[jax.ShapeDtypeStruct((rows,d),jnp.float32),jax.ShapeDtypeStruct((rows,d),jnp.bfloat16),
                   jax.ShapeDtypeStruct((heads,rows,128),jnp.bfloat16)],
        compiler_params=pltpu.CompilerParams(vmem_limit_bytes=60<<20),
        cost_estimate=pl.CostEstimate(flops=2*2*rows*nk*256*heads,bytes_accessed=nk*d*4+rows*d*10,transcendentals=rows*nk*heads),
        name="attend")(idx,q,kv,kv,fq,fk)

def bwd_kernel(idx_ref,qa_ref,k_ref,v_ref,fk_ref,g_ref,o_ref,dq_ref,dk_ref,dv_ref,dqt):
    cnt=idx_ref[0]
    lane=lax.broadcasted_iota(jnp.int32,(1,128),1)
    low=lane<HD
    g=g_ref[...].astype(jnp.float32)
    prod=g*o_ref[...]
    gs=[]
    for h in range(2):
        own=low if h==0 else jnp.logical_not(low)
        base=HD+LSE_LANE if h==0 else LSE_LANE
        delta=jnp.sum(jnp.where(own,prod,0.0),axis=1,keepdims=True)
        hi,mid,lo=split3(-delta)
        ga=jnp.where(own,g,0.0)
        for j,t in enumerate((hi,mid,lo)):
            ga=jnp.where(lane==base+j,t,ga)
        gs.append(ga.astype(jnp.bfloat16))
    dk_ref[...]=jnp.zeros(dk_ref.shape,dk_ref.dtype)
    dv_ref[...]=jnp.zeros(dv_ref.shape,dv_ref.dtype)
    dqt[...]=jnp.zeros(dqt.shape,jnp.float32)
    qs=(qa_ref[0],qa_ref[1])
    def step(i,_):
        r=pl.ds(pl.multiple_of(idx_ref[i+1]*KB,KB),KB)
        k2=k_ref[r,:];v2=v_ref[r,:];fk=fk_ref[r,:]
        dks=[];dvs=[]
        for h in range(2):
            ka=jnp.where(low,k2,fk) if h==0 else jnp.where(low,fk,k2)
            va=jnp.where(low,v2,fk) if h==0 else jnp.where(low,fk,v2)
            st=lax.dot_general(ka,qs[h],NT,preferred_element_type=jnp.float32)
            dpt=lax.dot_general(va,gs[h],NT,preferred_element_type=jnp.float32)
            pt=jnp.exp(st)
            ds=(pt*dpt).astype(jnp.bfloat16)
            dvs.append(lax.dot_general(pt.astype(jnp.bfloat16),gs[h],NN,preferred_element_type=jnp.float32))
            dks.append(lax.dot_general(ds,qs[h],NN,preferred_element_type=jnp.float32))
            dqt[h]+=lax.dot_general(ka.T,ds,NN,preferred_element_type=jnp.float32)
        dk_ref[r,:]=jnp.where(low,dks[0],dks[1]).astype(dk_ref.dtype)
        dv_ref[r,:]=jnp.where(low,dvs[0],dvs[1]).astype(dv_ref.dtype)
        return 0
    lax.fori_loop(0,cnt,step,0)
    dq_ref[...]=(jnp.where(low,dqt[0].T,dqt[1].T)*0.125).astype(dq_ref.dtype)

def attend_back(qa,kv,idx,fk,g,o,heads=12):
    rows,d=g.shape
    nk=kv.shape[0]
    pairs=heads//2
    spec=pltpu.PrefetchScalarGridSpec(num_scalar_prefetch=1,grid=(pairs,),
        in_specs=[pl.BlockSpec((2,rows,128),lambda p,i:(p,0,0)),
                  pl.BlockSpec((nk,128),lambda p,i:(0,p)),
                  pl.BlockSpec((nk,128),lambda p,i:(0,p+pairs)),
                  pl.BlockSpec((nk,128),lambda p,i:(0,0)),
                  pl.BlockSpec((rows,128),lambda p,i:(0,p)),
                  pl.BlockSpec((rows,128),lambda p,i:(0,p))],
        out_specs=[pl.BlockSpec((rows,128),lambda p,i:(0,p)),
                   pl.BlockSpec((nk,128),lambda p,i:(0,p)),
                   pl.BlockSpec((nk,128),lambda p,i:(0,p))],
        scratch_shapes=[pltpu.VMEM((2,128,rows),jnp.float32)])
    return pl.pallas_call(bwd_kernel,grid_spec=spec,
        out_shape=[jax.ShapeDtypeStruct((rows,d),jnp.bfloat16),jax.ShapeDtypeStruct((nk,d),jnp.bfloat16),
                   jax.ShapeDtypeStruct((nk,d),jnp.bfloat16)],
        compiler_params=pltpu.CompilerParams(vmem_limit_bytes=60<<20),
        cost_estimate=pl.CostEstimate(flops=5*2*rows*nk*256*heads,bytes_accessed=nk*d*8+rows*d*10,transcendentals=rows*nk*heads),
        name="attend_back")(idx,qa,kv,kv,fk,g,o)

def features(seg_query,seg_key):
    j=jnp.arange(128,dtype=jnp.int32)[None,:]%HD
    fq=jnp.where((j<10)&(j!=seg_query[:,None]),NEG,0.0).astype(jnp.bfloat16)
    fk=(((j<10)&(j==seg_key[:,None]))|((j>=LSE_LANE)&(j<LSE_LANE+3))).astype(jnp.bfloat16)
    return fq,fk

def active(seg_query,seg_key):
    nb=seg_key.shape[0]//KB
    lo=jnp.min(seg_query);hi=jnp.max(seg_query)
    sk=seg_key.reshape(nb,KB)
    use=jnp.any((sk<0)|((sk>=lo)&(sk<=hi)),axis=1)
    slot=jnp.arange(nb,dtype=jnp.int32)
    rank=jnp.sum((use[None,:]&(slot[None,:]<slot[:,None])).astype(jnp.int32),axis=1)
    order=jnp.sum(jnp.where(use[None,:]&(rank[None,:]==slot[:,None]),slot[None,:],0),axis=1)
    return jnp.concatenate([jnp.sum(use.astype(jnp.int32))[None],order]).astype(jnp.int32)


D = 768
HEADS = 12
IMGS = 8
CLASS_ROWS = 256
WIDE = 384


def norm_rows(values, gain_row):
    centre = values - jnp.mean(values, axis=-1, keepdims=True)
    return centre * lax.rsqrt(jnp.mean(centre * centre, axis=-1, keepdims=True) + 1e-06) * gain_row


def class_norm(logits, gain_row):
    centre = logits - jnp.mean(logits, axis=-1, keepdims=True)
    return centre * lax.rsqrt(jnp.mean(centre * centre, axis=-1, keepdims=True) + 1e-05) * gain_row


def unit_rows(values):
    return values * lax.rsqrt(jnp.sum(values * values, axis=-1, keepdims=True) + 1e-06)


def dot(left, right):
    return jnp.dot(left, right, preferred_element_type=jnp.float32)


def dot_rows(left, right):
    return lax.dot_general(left, right, (((0,), (0,)), ((), ())), preferred_element_type=jnp.float32)


def dot_turned(left, right):
    return lax.dot_general(left, right, (((1,), (1,)), ((), ())), preferred_element_type=jnp.float32)


def low(values):
    return values.astype(jnp.bfloat16)


def bits_of(axis):
    return [1 << i for i in range(lax.axis_size(axis).bit_length() - 1)]


def swap(values, axis, bit):
    count = lax.axis_size(axis)
    return lax.ppermute(values, axis, [(i, i ^ bit) for i in range(count)])


def own_bit(axis, bit):
    return (lax.axis_index(axis) // bit) % 2


def gather_rows(rows):
    for bit in reversed(bits_of("seq")):
        rows = jnp.concatenate([rows, swap(rows, "seq", bit)], axis=0)
    return rows


def relative():
    order = [0]
    for bit in reversed(bits_of("seq")):
        order = order + [i ^ bit for i in order]
    return order


def scatter_rows(rows):
    for bit in bits_of("seq"):
        half = rows.shape[0] // 2
        rows = rows[:half] + swap(low(rows[half:]), "seq", bit).astype(jnp.float32)
    return rows


def segment_of(places, seq_lengths):
    count = seq_lengths.shape[0]
    before = jnp.arange(count)[None, :] <= jnp.arange(count)[:, None]
    boundary = jnp.sum(jnp.where(before, seq_lengths[None, :], 0), axis=1)
    return jnp.sum((places[:, None] >= boundary[None, :]).astype(jnp.int32), axis=1)


def bundle(shards):
    count, index = lax.axis_size("seq"), lax.axis_index("seq")
    pieces = []
    for shard in shards:
        rows = shard.shape[0] // count
        part = lax.dynamic_slice_in_dim(shard, index * rows, rows, 0)
        pieces += [part[:, i : i + D] for i in range(0, shard.shape[1], D)]
    return jnp.concatenate(pieces, axis=0)


def unbundle(gathered, shards):
    count = lax.axis_size("seq")
    devices = gathered.shape[0]
    weights, at = [], 0
    for shard in shards:
        rows, wide = shard.shape[0] // count, shard.shape[1] // D
        part = gathered[:, at : at + rows * wide].reshape(devices, wide, rows, D)
        weights.append(part.transpose(0, 2, 1, 3).reshape(devices * rows, wide * D))
        at += rows * wide
    return weights


def gather_weights(shards):
    return unbundle(lax.all_gather(bundle(shards), ("dp", "seq"), axis=0), shards)


def core_half(left, right):
    core = own_bit("seq", 1)
    half = right.shape[1] // 2
    send = lax.dynamic_slice_in_dim(right, (1 - core) * half, half, 1)
    keep = lax.dynamic_slice_in_dim(right, core * half, half, 1)
    arrived = swap(low(dot_rows(left, send)), "seq", 1)
    total = low(dot_rows(left, keep) + arrived.astype(jnp.float32))
    return [total[:, i : i + WIDE] for i in range(0, half, WIDE)]


def halve(values, dim, axis, bit):
    own = own_bit(axis, bit)
    arrived = swap(lax.dynamic_index_in_dim(values, 1 - own, dim), axis, bit)
    kept = lax.dynamic_index_in_dim(values, own, dim)
    return low(kept.astype(jnp.float32) + arrived.astype(jnp.float32))


def double(values, dim, axis, bit):
    own = own_bit(axis, bit)
    arrived = swap(values, axis, bit)
    return jnp.concatenate(
        [jnp.where(own == 0, values, arrived), jnp.where(own == 0, arrived, values)], axis=dim
    )


def reduce_weights(products):
    dp_bits, y_bits = bits_of("dp"), bits_of("seq")[1:]
    devices, y_count = lax.axis_size("dp"), lax.axis_size("seq") // 2
    pieces, shape = [], []
    for left, right in products:
        mine = core_half(left, right)
        rows = left.shape[1] // (devices * y_count)
        pieces += [t.reshape(devices, y_count, rows, WIDE) for t in mine]
        shape.append((rows, len(mine)))
    total = jnp.concatenate(pieces, axis=2)
    steps = [("dp", b, len(dp_bits) - 1 - i) for i, b in enumerate(dp_bits)]
    y_steps = [("seq", b, len(dp_bits) + len(y_bits) - 1 - i) for i, b in enumerate(y_bits)]
    cut = total.shape[2] // 2
    done = []
    for part, order in (
        (total[:, :, :cut], y_steps + steps),
        (total[:, :, cut:], steps[:1] + y_steps + steps[1:]),
    ):
        part = part.reshape((2,) * (len(dp_bits) + len(y_bits)) + part.shape[2:])
        for axis, bit, dim in order:
            part = halve(part, dim, axis, bit)
        done.append(part.reshape((1,) + part.shape[-2:]))
    mine = jnp.concatenate(done, axis=1)
    for bit in y_bits:
        mine = double(mine, 0, "seq", bit)
    other = swap(mine, "seq", 1)
    core = own_bit("seq", 1)
    sides = [jnp.where(core == 0, mine, other), jnp.where(core == 0, other, mine)]
    results, at = [], 0
    for rows, wide in shape:
        columns = [
            side[:, at + i * rows : at + (i + 1) * rows].reshape(y_count * rows, WIDE)
            for side in sides
            for i in range(wide)
        ]
        results.append(jnp.concatenate(columns, axis=1).astype(jnp.float32))
        at += rows * wide
    return results


def sum_everywhere(values):
    steps = [("seq", b) for b in bits_of("seq")] + [("dp", b) for b in bits_of("dp")]
    parts = 1 << len(steps)
    rows = values.shape[0]
    total = jnp.pad(values, ((0, -rows % parts), (0, 0)))
    if rows >= parts:
        for axis, bit in steps:
            own, half = own_bit(axis, bit), total.shape[0] // 2
            kept = lax.dynamic_slice_in_dim(total, own * half, half, 0)
            total = kept + swap(lax.dynamic_slice_in_dim(total, (1 - own) * half, half, 0), axis, bit)
        for axis, bit in reversed(steps):
            total = double(total, 0, axis, bit)
    else:
        total = values
        for axis, bit in steps:
            total = total + swap(total, axis, bit)
    return total[:rows]


def block_forward(hidden, gain_a, gain_b, weights, mask, class_normed):
    w_qkv, w_out, w_up, w_down = weights
    idx, feature_q, feature_k = mask
    normed = low(norm_rows(hidden, gain_a))
    rows_all = gather_rows(normed)
    if class_normed is not None:
        rows_all = jnp.concatenate([rows_all, class_normed], axis=0)
    queries = low(dot(normed, w_qkv[:, :D]))
    keyval = low(dot(rows_all, w_qkv[:, D:]))
    attended, attended_low, kept_q = attend(queries, keyval, idx, feature_q, feature_k)
    middle = hidden + dot(attended_low, w_out)
    second = low(norm_rows(middle, gain_b))
    upward = dot(second, w_up)
    active_rows = low(jax.nn.gelu(upward))
    result = middle + dot(active_rows, w_down)
    return result, (normed, rows_all, keyval, attended, attended_low, kept_q, middle, second, upward, active_rows)


def block_backward(grad_result, hidden, kept, gain_a, gain_b, weights, mask):
    w_qkv, w_out, w_up, w_down = weights
    idx, _, feature_k = mask
    normed, rows_all, keyval, attended, attended_low, kept_q, middle, second, upward, active_rows = kept
    grad_branch = low(grad_result)
    grad_active = dot_turned(grad_branch, w_down)
    _, gelu_back = jax.vjp(jax.nn.gelu, upward)
    grad_upward = low(gelu_back(grad_active)[0])
    mlp_products = [(second, grad_upward), (active_rows, grad_branch)]
    grad_second = dot_turned(grad_upward, w_up)
    _, second_back = jax.vjp(norm_rows, middle, gain_b)
    grad_middle, grad_gain_b = second_back(grad_second)
    grad_middle = grad_middle + grad_result
    grad_attn = low(grad_middle)
    grad_attended = low(dot_turned(grad_attn, w_out))
    grad_query, grad_key, grad_value = attend_back(kept_q, keyval, idx, feature_k, grad_attended, attended)
    grad_keyval = jnp.concatenate([grad_key, grad_value], axis=1)
    grad_all = dot_turned(grad_keyval, w_qkv[:, D:])
    token_rows = rows_all.shape[0] // hidden.shape[0] * hidden.shape[0]
    grad_class_normed = grad_all[token_rows:]
    grad_normed = dot_turned(grad_query, w_qkv[:, :D]) + scatter_rows(grad_all[:token_rows])
    attn_products = [(normed, grad_query), (rows_all, grad_keyval), (attended_low, grad_attn)]
    _, first_back = jax.vjp(norm_rows, hidden, gain_a)
    grad_hidden, grad_gain_a = first_back(grad_normed)
    return grad_hidden + grad_middle, mlp_products, attn_products, grad_gain_a, grad_gain_b, grad_class_normed


def local(
    tokens,
    lengths,
    classes,
    norm_gains,
    mask_gain,
    enc_qkv,
    enc_out,
    enc_up,
    enc_down,
    dec_qkv,
    dec_out,
    dec_up,
    dec_down,
    patch_proj,
    class_proj,
    mask_cot,
):
    enc_weights = gather_weights((enc_qkv, enc_out, enc_up, enc_down))
    *dec_weights, w_patch, w_class = gather_weights(
        (dec_qkv, dec_out, dec_up, dec_down, patch_proj, class_proj)
    )
    row_count = tokens.shape[1]
    index = lax.axis_index("seq")
    seq_lengths = lengths[0]
    inputs_f = tokens[0].astype(jnp.float32)
    gains_f = norm_gains.astype(jnp.float32)
    classes_f = classes.astype(jnp.float32)
    class_count = classes.shape[0]
    mask_gain_f = mask_gain.astype(jnp.float32)
    steps = jnp.arange(row_count, dtype=jnp.int32)
    seg_query = segment_of(index * row_count + steps, seq_lengths)
    starts = jnp.stack([(index ^ r) * row_count for r in relative()])
    seg_rows = segment_of((starts[:, None] + steps[None, :]).reshape(-1), seq_lengths)
    class_slots = jnp.arange(CLASS_ROWS, dtype=jnp.int32)
    seg_key = jnp.concatenate([seg_rows, jnp.where(class_slots < class_count, -1, IMGS + 1)])
    feature_q, feature_k = features(seg_query, seg_key)
    enc_mask = (active(seg_query, seg_rows), feature_q, feature_k[: seg_rows.shape[0]])
    dec_mask = (active(seg_query, seg_key), feature_q, feature_k)
    valid_rows = (seg_query < IMGS).astype(jnp.float32)[:, None]
    encoded, enc_kept = block_forward(inputs_f, gains_f[0], gains_f[1], enc_weights, enc_mask, None)
    class_normed = low(norm_rows(classes_f, gains_f[2]))
    class_padded = jnp.pad(class_normed, ((0, CLASS_ROWS - class_count), (0, 0)))
    decoded, dec_kept = block_forward(
        encoded, gains_f[2], gains_f[3], dec_weights, dec_mask, class_padded
    )
    final_normed = low(norm_rows(decoded, gains_f[4]))
    patch_rows = low(dot(final_normed, w_patch))
    class_rows = dot(classes, w_class)
    class_unit = low(unit_rows(class_rows))
    logits = dot_turned(patch_rows, class_unit)
    mask_out = class_norm(logits, mask_gain_f) * valid_rows
    _, head_back = jax.vjp(class_norm, logits, mask_gain_f)
    grad_logits, grad_mask_gain = head_back(mask_cot[0] * valid_rows)
    grad_logits_low = low(grad_logits)
    grad_patch_rows = low(dot(grad_logits_low, class_unit))
    grad_unit = dot_rows(grad_logits_low, patch_rows)
    grad_final = dot_turned(grad_patch_rows, w_patch)
    _, final_back = jax.vjp(norm_rows, decoded, gains_f[4])
    grad_decoded, grad_gain_last = final_back(grad_final)
    _, unit_back = jax.vjp(unit_rows, class_rows)
    grad_class_rows = low(unit_back(grad_unit)[0])
    grad_classes = dot_turned(grad_class_rows, w_class)
    grad_encoded, dec_mlp, dec_attn, grad_gain_two, grad_gain_three, grad_class_normed = block_backward(
        grad_decoded, encoded, dec_kept, gains_f[2], gains_f[3], dec_weights, dec_mask
    )
    _, class_back = jax.vjp(norm_rows, classes_f, gains_f[2])
    grad_classes_kv, grad_gain_class = class_back(grad_class_normed[:class_count])
    early = [grad_gain_two + grad_gain_class, grad_gain_three, grad_gain_last]
    padded_mask_gain = jnp.pad(grad_mask_gain, (0, D - class_count))
    shared = sum_everywhere(
        jnp.concatenate([grad_classes + grad_classes_kv, jnp.stack(early + [padded_mask_gain])], axis=0)
    )
    dec_up_down = reduce_weights(
        dec_mlp + [(final_normed, grad_patch_rows), (classes, grad_class_rows)]
    )
    dec_proj = reduce_weights(dec_attn)
    grad_inputs, enc_mlp, enc_attn, grad_gain_zero, grad_gain_one, _ = block_backward(
        grad_encoded, inputs_f, enc_kept, gains_f[0], gains_f[1], enc_weights, enc_mask
    )
    enc_up_down = reduce_weights(enc_mlp)
    enc_proj = reduce_weights(enc_attn)
    late = sum_everywhere(jnp.stack([grad_gain_zero, grad_gain_one]))
    gain_sums = jnp.concatenate([late, shared[class_count : class_count + 3]], axis=0)
    return (
        mask_out[None],
        grad_inputs[None],
        shared[:class_count],
        gain_sums,
        shared[class_count + 3, :class_count],
        jnp.concatenate(enc_proj[:2], axis=1),
        enc_proj[2],
        enc_up_down[0],
        enc_up_down[1],
        jnp.concatenate(dec_proj[:2], axis=1),
        dec_proj[2],
        dec_up_down[0],
        dec_up_down[1],
        dec_up_down[2],
        dec_up_down[3],
    )


def solution(mesh):
    placed = (
        P("dp", "seq", None),
        P("dp", None),
        P(),
        P(),
        P(),
        P("dp", None),
        P("dp", None),
        P("dp", None),
        P("dp", None),
        P("dp", None),
        P("dp", None),
        P("dp", None),
        P("dp", None),
        P("dp", None),
        P("dp", None),
        P("dp", "seq", None),
    )
    return jax.shard_map(
        local,
        mesh=mesh,
        in_specs=placed,
        out_specs=(
            P("dp", "seq", None),
            P("dp", "seq", None),
            P(),
            P(),
            P(),
            P("dp", None),
            P("dp", None),
            P("dp", None),
            P("dp", None),
            P("dp", None),
            P("dp", None),
            P("dp", None),
            P("dp", None),
            P("dp", None),
            P("dp", None),
        ),
        check_vma=False,
    )
```

```python
import functools
import math

import jax
import jax.numpy as jnp
from jax import lax
from jax.experimental import pallas as pl
from jax.experimental.pallas import tpu as pltpu
from jax.sharding import PartitionSpec as P
HD=64
KB=256
LSE_LANE=10
NEG=-1e30
NT=(((1,),(1,)),((),()))
NN=(((1,),(0,)),((),()))

def split3(v):
    hi=v.astype(jnp.bfloat16).astype(jnp.float32)
    mid=(v-hi).astype(jnp.bfloat16).astype(jnp.float32)
    return hi,mid,v-hi-mid

def fwd_kernel(idx_ref,q_ref,k_ref,v_ref,fq_ref,fk_ref,o_ref,ol_ref,qa_ref,ka,va,s_ref,m_ref,acc_ref):
    rows=q_ref.shape[0]
    cnt=idx_ref[0]
    lane=lax.broadcasted_iota(jnp.int32,(1,128),1)
    low=lane<HD
    q2=q_ref[...]*jnp.bfloat16(0.125)
    fq=fq_ref[...]
    qs=(jnp.where(low,q2,fq),jnp.where(low,fq,q2))
    k2=k_ref[...];v2=v_ref[...];fk=fk_ref[...]
    ka[0]=jnp.where(low,k2,fk);ka[1]=jnp.where(low,fk,k2)
    va[0]=jnp.where(low,v2,fk);va[1]=jnp.where(low,fk,v2)
    m_ref[...]=jnp.full(m_ref.shape,2*NEG,jnp.float32)
    def first(i,_):
        r=pl.ds(pl.multiple_of(idx_ref[i+1]*KB,KB),KB)
        for h in range(2):
            s=lax.dot_general(qs[h],ka[h,r,:],NT,preferred_element_type=jnp.float32)
            s_ref[h,i]=s
            m_ref[h]=jnp.maximum(m_ref[h],jnp.maximum(s[:,:128],s[:,128:]))
        return 0
    lax.fori_loop(0,cnt,first,0)
    tops=[jnp.max(m_ref[h],axis=1,keepdims=True) for h in range(2)]
    acc_ref[...]=jnp.zeros(acc_ref.shape,jnp.float32)
    def second(i,_):
        r=pl.ds(pl.multiple_of(idx_ref[i+1]*KB,KB),KB)
        for h in range(2):
            p=jnp.exp(s_ref[h,i]-tops[h]).astype(jnp.bfloat16)
            acc_ref[h]+=lax.dot_general(p,va[h,r,:],NN,preferred_element_type=jnp.float32)
        return 0
    lax.fori_loop(0,cnt,second,0)
    outs=[]
    for h in range(2):
        base=HD+LSE_LANE if h==0 else LSE_LANE
        acc=acc_ref[h]
        total=acc[:,base:base+1]
        outs.append(acc/total)
        hi,mid,lo=split3(-(tops[h]+jnp.log(total)))
        qa=qs[h].astype(jnp.float32)
        for j,t in enumerate((hi,mid,lo)):
            qa=jnp.where(lane==base+j,t,qa)
        qa_ref[h]=qa.astype(jnp.bfloat16)
    o=jnp.where(low,outs[0],outs[1])
    o_ref[...]=o
    ol_ref[...]=o.astype(jnp.bfloat16)

def attend(q,kv,idx,fq,fk,heads=12):
    rows,d=q.shape
    nk=kv.shape[0]
    pairs=heads//2
    nb=nk//KB
    spec=pltpu.PrefetchScalarGridSpec(num_scalar_prefetch=1,grid=(pairs,),
        in_specs=[pl.BlockSpec((rows,128),lambda p,i:(0,p)),
                  pl.BlockSpec((nk,128),lambda p,i:(0,p)),
                  pl.BlockSpec((nk,128),lambda p,i:(0,p+pairs)),
                  pl.BlockSpec((rows,128),lambda p,i:(0,0)),
                  pl.BlockSpec((nk,128),lambda p,i:(0,0))],
        out_specs=[pl.BlockSpec((rows,128),lambda p,i:(0,p)),
                   pl.BlockSpec((rows,128),lambda p,i:(0,p)),
                   pl.BlockSpec((2,rows,128),lambda p,i:(p,0,0))],
        scratch_shapes=[pltpu.VMEM((2,nk,128),jnp.bfloat16),pltpu.VMEM((2,nk,128),jnp.bfloat16),
                        pltpu.VMEM((2,nb,rows,KB),jnp.float32),pltpu.VMEM((2,rows,128),jnp.float32),
                        pltpu.VMEM((2,rows,128),jnp.float32)])
    return pl.pallas_call(fwd_kernel,grid_spec=spec,
        out_shape=[jax.ShapeDtypeStruct((rows,d),jnp.float32),jax.ShapeDtypeStruct((rows,d),jnp.bfloat16),
                   jax.ShapeDtypeStruct((heads,rows,128),jnp.bfloat16)],
        compiler_params=pltpu.CompilerParams(vmem_limit_bytes=60<<20),
        cost_estimate=pl.CostEstimate(flops=rows*nk,bytes_accessed=rows*d,transcendentals=0),
        name="attend")(idx,q,kv,kv,fq,fk)

def bwd_kernel(idx_ref,qa_ref,k_ref,v_ref,fk_ref,g_ref,o_ref,dq_ref,dk_ref,dv_ref,dqt):
    cnt=idx_ref[0]
    lane=lax.broadcasted_iota(jnp.int32,(1,128),1)
    low=lane<HD
    g=g_ref[...].astype(jnp.float32)
    prod=g*o_ref[...]
    gs=[]
    for h in range(2):
        own=low if h==0 else jnp.logical_not(low)
        base=HD+LSE_LANE if h==0 else LSE_LANE
        delta=jnp.sum(jnp.where(own,prod,0.0),axis=1,keepdims=True)
        hi,mid,lo=split3(-delta)
        ga=jnp.where(own,g,0.0)
        for j,t in enumerate((hi,mid,lo)):
            ga=jnp.where(lane==base+j,t,ga)
        gs.append(ga.astype(jnp.bfloat16))
    dk_ref[...]=jnp.zeros(dk_ref.shape,dk_ref.dtype)
    dv_ref[...]=jnp.zeros(dv_ref.shape,dv_ref.dtype)
    dqt[...]=jnp.zeros(dqt.shape,jnp.float32)
    qs=(qa_ref[0],qa_ref[1])
    def step(i,_):
        r=pl.ds(pl.multiple_of(idx_ref[i+1]*KB,KB),KB)
        k2=k_ref[r,:];v2=v_ref[r,:];fk=fk_ref[r,:]
        dks=[];dvs=[]
        for h in range(2):
            ka=jnp.where(low,k2,fk) if h==0 else jnp.where(low,fk,k2)
            va=jnp.where(low,v2,fk) if h==0 else jnp.where(low,fk,v2)
            st=lax.dot_general(ka,qs[h],NT,preferred_element_type=jnp.float32)
            dpt=lax.dot_general(va,gs[h],NT,preferred_element_type=jnp.float32)
            pt=jnp.exp(st)
            ds=(pt*dpt).astype(jnp.bfloat16)
            dvs.append(lax.dot_general(pt.astype(jnp.bfloat16),gs[h],NN,preferred_element_type=jnp.float32))
            dks.append(lax.dot_general(ds,qs[h],NN,preferred_element_type=jnp.float32))
            dqt[h]+=lax.dot_general(ka.T,ds,NN,preferred_element_type=jnp.float32)
        dk_ref[r,:]=jnp.where(low,dks[0],dks[1]).astype(dk_ref.dtype)
        dv_ref[r,:]=jnp.where(low,dvs[0],dvs[1]).astype(dv_ref.dtype)
        return 0
    lax.fori_loop(0,cnt,step,0)
    dq_ref[...]=(jnp.where(low,dqt[0].T,dqt[1].T)*0.125).astype(dq_ref.dtype)

def attend_back(qa,kv,idx,fk,g,o,first,count,heads=12):
    rows,d=g.shape
    nk=kv.shape[0]
    pairs=heads//2
    spec=pltpu.PrefetchScalarGridSpec(num_scalar_prefetch=1,grid=(count,),
        in_specs=[pl.BlockSpec((2,rows,128),lambda p,i:(p+first,0,0)),
                  pl.BlockSpec((nk,128),lambda p,i:(0,p+first)),
                  pl.BlockSpec((nk,128),lambda p,i:(0,p+first+pairs)),
                  pl.BlockSpec((nk,128),lambda p,i:(0,0)),
                  pl.BlockSpec((rows,128),lambda p,i:(0,p+first)),
                  pl.BlockSpec((rows,128),lambda p,i:(0,p+first))],
        out_specs=[pl.BlockSpec((rows,128),lambda p,i:(0,p)),
                   pl.BlockSpec((nk,128),lambda p,i:(0,p)),
                   pl.BlockSpec((nk,128),lambda p,i:(0,p))],
        scratch_shapes=[pltpu.VMEM((2,128,rows),jnp.float32)])
    return pl.pallas_call(bwd_kernel,grid_spec=spec,
        out_shape=[jax.ShapeDtypeStruct((rows,128*count),jnp.bfloat16),jax.ShapeDtypeStruct((nk,128*count),jnp.bfloat16),
                   jax.ShapeDtypeStruct((nk,128*count),jnp.bfloat16)],
        compiler_params=pltpu.CompilerParams(vmem_limit_bytes=60<<20),
        cost_estimate=pl.CostEstimate(flops=rows*nk,bytes_accessed=rows*d,transcendentals=0),
        name="attend_back")(idx,qa,kv,kv,fk,g,o)

def features(seg_query,seg_key):
    j=jnp.arange(128,dtype=jnp.int32)[None,:]%HD
    fq=jnp.where((j<10)&(j!=seg_query[:,None]),NEG,0.0).astype(jnp.bfloat16)
    fk=(((j<10)&(j==seg_key[:,None]))|((j>=LSE_LANE)&(j<LSE_LANE+3))).astype(jnp.bfloat16)
    return fq,fk

def active(seg_query,seg_key):
    nb=seg_key.shape[0]//KB
    lo=jnp.min(seg_query);hi=jnp.max(seg_query)
    sk=seg_key.reshape(nb,KB)
    use=jnp.any((sk<0)|((sk>=lo)&(sk<=hi)),axis=1)
    slot=jnp.arange(nb,dtype=jnp.int32)
    rank=jnp.sum((use[None,:]&(slot[None,:]<slot[:,None])).astype(jnp.int32),axis=1)
    order=jnp.sum(jnp.where(use[None,:]&(rank[None,:]==slot[:,None]),slot[None,:],0),axis=1)
    return jnp.concatenate([jnp.sum(use.astype(jnp.int32))[None],order]).astype(jnp.int32)


D = 768
HEADS = 12
IMGS = 8
CLASS_ROWS = 256
WIDE = 384


def norm_rows(values, gain_row):
    centre = values - jnp.mean(values, axis=-1, keepdims=True)
    return centre * lax.rsqrt(jnp.mean(centre * centre, axis=-1, keepdims=True) + 1e-06) * gain_row


def class_norm(logits, gain_row):
    centre = logits - jnp.mean(logits, axis=-1, keepdims=True)
    return centre * lax.rsqrt(jnp.mean(centre * centre, axis=-1, keepdims=True) + 1e-05) * gain_row


def unit_rows(values):
    return values * lax.rsqrt(jnp.sum(values * values, axis=-1, keepdims=True) + 1e-06)


def dot(left, right):
    return jnp.dot(left, right, preferred_element_type=jnp.float32)


def dot_rows(left, right):
    return lax.dot_general(left, right, (((0,), (0,)), ((), ())), preferred_element_type=jnp.float32)


def dot_turned(left, right):
    return lax.dot_general(left, right, (((1,), (1,)), ((), ())), preferred_element_type=jnp.float32)


def low(values):
    return values.astype(jnp.bfloat16)


BOTH = ("dp", "seq")


def bits_of(count):
    return [1 << i for i in range(count.bit_length() - 1)]


def seq_bits():
    return bits_of(lax.axis_size("seq"))


def chip_bits():
    return bits_of(lax.axis_size("seq") * lax.axis_size("dp"))[1:]


def swap(values, mask):
    inner, outer = lax.axis_size("seq"), lax.axis_size("dp")
    place = [(i % inner) * outer + i // inner for i in range(inner * outer)]
    pairs = [(place[i], place[i ^ mask]) for i in range(inner * outer)]
    return lax.ppermute(values, ("seq", "dp"), pairs)


def own_bit(bit):
    return (lax.axis_index(BOTH) // bit) % 2


def masks_of(bits):
    masks = [0]
    for bit in bits:
        masks = masks + [m | bit for m in masks]
    return masks


def groups_of(bits):
    return [bits[i : i + 2] for i in range(0, len(bits), 2)]


def absolute(pieces, bits):
    for i, bit in enumerate(bits):
        same = own_bit(bit) == 0
        pieces = [jnp.where(same, p, pieces[k ^ (1 << i)]) for k, p in enumerate(pieces)]
    return pieces


def gather_rows(rows):
    for bit in reversed(seq_bits()):
        rows = jnp.concatenate([rows, swap(rows, bit)], axis=0)
    return rows


def relative():
    return masks_of(seq_bits()[::-1])


def segment_of(places, seq_lengths):
    count = seq_lengths.shape[0]
    before = jnp.arange(count)[None, :] <= jnp.arange(count)[:, None]
    boundary = jnp.sum(jnp.where(before, seq_lengths[None, :], 0), axis=1)
    return jnp.sum((places[:, None] >= boundary[None, :]).astype(jnp.int32), axis=1)


def from_sequence(mine):
    bits = seq_bits()
    return absolute([mine if m == 0 else swap(mine, m) for m in masks_of(bits)], bits)


def share_low(total, group, width):
    values = total.reshape((total.shape[0] // width, width) + total.shape[1:])
    own = lax.axis_index(BOTH)
    pieces = []
    for m in masks_of(group):
        place = ((own ^ m) // group[0]) % width
        piece = lax.dynamic_index_in_dim(values, place, 1, keepdims=False)
        pieces.append(piece if m == 0 else swap(piece, m))
    return sum(p.astype(jnp.float32) for p in pieces).astype(total.dtype)


BLOCKS = 16
PIECE = 48
TALL = 192
TN = (((0,), (0,)), ((), ()))


def cheap(rows):
    return pl.CostEstimate(flops=rows, bytes_accessed=rows, transcendentals=0)


def dot_nn(left, right):
    return lax.dot_general(left, right, NN, preferred_element_type=jnp.float32)


def dot_nt(left, right):
    return lax.dot_general(left, right, NT, preferred_element_type=jnp.float32)


def mat(chunk):
    return chunk.reshape(-1, WIDE)


def columns(c):
    return slice(c * WIDE, (c + 1) * WIDE)


def gelu_parts(u):
    root = math.sqrt(2.0 / math.pi)
    t = jnp.tanh(root * (u + 0.044715 * (u * u * u)))
    return 0.5 * (1.0 + t), 0.5 * u * (1.0 - t * t) * (root * (1.0 + (3 * 0.044715) * (u * u)))


def qkv_kernel(rows_ref, w_ref, kv_ref, q_ref):
    step = pl.program_id(0)
    weight = mat(w_ref[:, 0])

    @pl.when(step < 4)
    def _():
        kv_ref[...] = dot_nn(rows_ref[...], weight).astype(kv_ref.dtype)

    @pl.when(step >= 4)
    def _():
        q_ref[...] = dot_nn(rows_ref[: q_ref.shape[0]], weight).astype(q_ref.dtype)


def project(rows_all, own, weights, first):
    count = rows_all.shape[0]
    return pl.pallas_call(
        qkv_kernel,
        grid=(6,),
        in_specs=[
            pl.BlockSpec((count, D), lambda t: (0, 0)),
            pl.BlockSpec(
                (BLOCKS, 1, PIECE, WIDE),
                lambda t: (0, t % 2, jnp.where(t < 4, first + 1 + t // 2, first), 0),
            ),
        ],
        out_specs=[
            pl.BlockSpec((count, WIDE), lambda t: (0, jnp.minimum(t, 3))),
            pl.BlockSpec((own, WIDE), lambda t: (0, jnp.maximum(t - 4, 0))),
        ],
        out_shape=[
            jax.ShapeDtypeStruct((count, 2 * D), jnp.bfloat16),
            jax.ShapeDtypeStruct((own, D), jnp.bfloat16),
        ],
        compiler_params=pltpu.CompilerParams(vmem_limit_bytes=60 << 20),
        cost_estimate=cheap(own),
        name="project",
    )(rows_all, weights)


def mlp_kernel(h_ref, o_ref, gain_ref, next_ref, wo_ref, wu_ref, wd_ref, mid_ref, sec_ref, u_ref, act_ref, res_ref, nrm_ref):
    step = pl.program_id(0)

    @pl.when(step == 0)
    def _():
        for c in range(2):
            part = dot_nn(o_ref[...], mat(wo_ref[:, c]))
            mid_ref[:, columns(c)] = h_ref[:, columns(c)].astype(jnp.float32) + part
        middle = mid_ref[...]
        sec_ref[...] = norm_rows(middle, gain_ref[...]).astype(sec_ref.dtype)
        res_ref[...] = middle

    for p in range(2):
        u = dot_nn(sec_ref[...], mat(wu_ref[:, 0, p * PIECE : (p + 1) * PIECE]))
        u_ref[:, columns(p)] = u.astype(u_ref.dtype)
        act_ref[:, columns(p)] = (u * gelu_parts(u)[0]).astype(act_ref.dtype)
    for c in range(2):
        res_ref[:, columns(c)] += dot_nn(act_ref[...], mat(wd_ref[:, c]))

    @pl.when(step == 3)
    def _():
        nrm_ref[...] = norm_rows(res_ref[...], next_ref[...]).astype(nrm_ref.dtype)


def mlp_specs(out_piece):
    return [
        pl.BlockSpec((BLOCKS, 2, PIECE, WIDE), lambda t: (0, 0, out_piece, 0)),
        pl.BlockSpec((BLOCKS, 1, 2 * PIECE, WIDE), lambda t: (0, t // 2, 2 + t % 2, 0)),
        pl.BlockSpec((BLOCKS // 4, 2, TALL, WIDE), lambda t: (t, 0, 0, 0)),
    ]


def whole(shape):
    return pl.BlockSpec(shape, lambda t: (0,) * len(shape))


def feed_forward(hidden, attended, gain, next_gain, w_out, out_piece, w_mlp):
    rows = hidden.shape[0]
    full, tile = (rows, D), pl.BlockSpec((rows, D), lambda t: (0, t))
    return pl.pallas_call(
        mlp_kernel,
        grid=(4,),
        in_specs=[whole(full), whole(full), whole((1, D)), whole((1, D)), *mlp_specs(out_piece)],
        out_specs=[whole(full), whole(full), tile, tile, whole(full), whole(full)],
        out_shape=[
            jax.ShapeDtypeStruct(full, jnp.float32),
            jax.ShapeDtypeStruct(full, jnp.bfloat16),
            jax.ShapeDtypeStruct((rows, 4 * D), jnp.bfloat16),
            jax.ShapeDtypeStruct((rows, 4 * D), jnp.bfloat16),
            jax.ShapeDtypeStruct(full, jnp.float32),
            jax.ShapeDtypeStruct(full, jnp.bfloat16),
        ],
        compiler_params=pltpu.CompilerParams(vmem_limit_bytes=60 << 20),
        cost_estimate=cheap(rows),
        name="feed_forward",
    )(hidden, attended, gain[None], next_gain[None], w_out, w_mlp, w_mlp)


def norm_back(grad, values, gain):
    centre = values - jnp.mean(values, axis=-1, keepdims=True)
    scale = lax.rsqrt(jnp.mean(centre * centre, axis=-1, keepdims=True) + 1e-06)
    unit = centre * scale
    inner = grad * gain
    inner = inner - jnp.mean(inner, axis=-1, keepdims=True) - unit * jnp.mean(inner * unit, axis=-1, keepdims=True)
    return inner * scale, grad * unit


def mlp_back_kernel(g_ref, u_ref, mid_ref, gain_ref, wo_ref, wu_ref, wd_ref, gb_ref, gu_ref, gm_ref, ga_ref, gat_ref, gg_ref, acc):
    step = pl.program_id(0)

    @pl.when(step == 0)
    def _():
        gb_ref[...] = g_ref[...].astype(gb_ref.dtype)
        acc[...] = jnp.zeros(acc.shape, jnp.float32)

    low_grad = gb_ref[...]
    for p in range(2):
        part = slice(p * 2, p * 2 + 2)
        grad = sum(dot_nt(low_grad[:, columns(c)], mat(wd_ref[part, c])) for c in range(2))
        u = u_ref[:, columns(p)].astype(jnp.float32)
        gu = (grad * sum(gelu_parts(u))).astype(gu_ref.dtype)
        gu_ref[:, columns(p)] = gu
        acc[...] += dot_nt(gu, mat(wu_ref[:, 0, p * PIECE : (p + 1) * PIECE]))

    @pl.when(step == 3)
    def _():
        back, gain_rows = norm_back(acc[...], mid_ref[...], gain_ref[...])
        middle = back + g_ref[...]
        gm_ref[...] = middle
        gg_ref[...] = jnp.sum(gain_rows, axis=0, keepdims=True)
        low_middle = middle.astype(ga_ref.dtype)
        ga_ref[...] = low_middle
        gat_ref[...] = sum(dot_nt(low_middle[:, columns(c)], mat(wo_ref[:, c])) for c in range(2)).astype(gat_ref.dtype)


def feed_forward_back(grad, upward, middle, gain, w_out, out_piece, w_mlp):
    rows = grad.shape[0]
    full, tile = (rows, D), pl.BlockSpec((rows, D), lambda t: (0, t))
    return pl.pallas_call(
        mlp_back_kernel,
        grid=(4,),
        in_specs=[whole(full), tile, whole(full), whole((1, D)), *mlp_specs(out_piece)],
        out_specs=[whole(full), tile, whole(full), whole(full), whole(full), whole((1, D))],
        out_shape=[
            jax.ShapeDtypeStruct(full, jnp.bfloat16),
            jax.ShapeDtypeStruct((rows, 4 * D), jnp.bfloat16),
            jax.ShapeDtypeStruct(full, jnp.float32),
            jax.ShapeDtypeStruct(full, jnp.bfloat16),
            jax.ShapeDtypeStruct(full, jnp.bfloat16),
            jax.ShapeDtypeStruct((1, D), jnp.float32),
        ],
        scratch_shapes=[pltpu.VMEM(full, jnp.float32)],
        compiler_params=pltpu.CompilerParams(vmem_limit_bytes=60 << 20),
        cost_estimate=cheap(rows),
        name="feed_forward_back",
    )(grad, upward, middle, gain[None], w_out, w_mlp, w_mlp)


def rows_back_kernel(own, dk0, dk1, dv0, dv1, dq0, dq1, wq_ref, wk_ref, wv_ref, out_ref):
    total = sum(
        dot_nt(d[...], mat(w[:, c]))
        for d, w, c in ((dk0, wk_ref, 0), (dk1, wk_ref, 1), (dv0, wv_ref, 0), (dv1, wv_ref, 1))
    )
    out_ref[...] = total

    @pl.when(pl.program_id(0) < own)
    def _():
        out_ref[...] += sum(dot_nt(d[...], mat(wq_ref[:, c])) for d, c in ((dq0, 0), (dq1, 1)))


def rows_back(one, two, weights, first):
    count, own = one[1].shape[0], one[0].shape[0] // KB
    tile = pl.BlockSpec((KB, WIDE), lambda t: (t, 0))
    query = pl.BlockSpec((KB, WIDE), lambda t: (jnp.minimum(t, own - 1), 0))
    piece = lambda i: pl.BlockSpec((BLOCKS, 2, PIECE, WIDE), lambda t: (0, 0, first + i, 0))
    return pl.pallas_call(
        functools.partial(rows_back_kernel, own),
        grid=(count // KB,),
        in_specs=[tile, tile, tile, tile, query, query, piece(0), piece(1), piece(2)],
        out_specs=pl.BlockSpec((KB, D), lambda t: (t, 0)),
        out_shape=jax.ShapeDtypeStruct((count, D), jnp.float32),
        compiler_params=pltpu.CompilerParams(vmem_limit_bytes=60 << 20),
        cost_estimate=cheap(count),
        name="rows_back",
    )(one[1], two[1], one[2], two[2], one[0], two[0], weights, weights, weights)


def products_kernel(plan, *refs):
    *ins, out_ref, turned = refs
    held = None
    for left, column, count, right, at_column, block, half, at, tall in plan:
        if held != (left, column):
            turned[:, :count] = ins[left][:, column : column + D].T
            held = (left, column)
        part = dot_nn(turned[:, :count], ins[right][:, at_column : at_column + WIDE]).astype(out_ref.dtype)
        if tall:
            out_ref[block : block + 4, half, at : at + TALL] = part.reshape(4, TALL, WIDE)
        else:
            out_ref[:, half, at : at + PIECE] = part.reshape(BLOCKS, PIECE, WIDE)


def products(wanted):
    arrays, plan, at = [], [], 0

    def place(array):
        for i, known in enumerate(arrays):
            if known is array:
                return i
        arrays.append(array)
        return len(arrays) - 1

    for left, rights in wanted:
        pieces = [(place(r), i) for r in rights for i in range(0, r.shape[1], WIDE)]
        index, count = place(left), left.shape[0]
        if left.shape[1] == D:
            wide = len(pieces) // 2
            for n, (right, column) in enumerate(pieces):
                plan.append((index, 0, count, right, column, 0, n // wide, at + n % wide * PIECE, False))
            at += wide * PIECE
        else:
            for block in range(4):
                for half, (right, column) in enumerate(pieces):
                    plan.append((index, block * D, count, right, column, block * 4, half, at, True))
            at += TALL
    longest = max(left.shape[0] for left, _ in wanted)
    return pl.pallas_call(
        functools.partial(products_kernel, plan),
        out_shape=jax.ShapeDtypeStruct((BLOCKS, 2, at, WIDE), jnp.bfloat16),
        scratch_shapes=[pltpu.VMEM((D, longest), jnp.bfloat16)],
        compiler_params=pltpu.CompilerParams(vmem_limit_bytes=60 << 20),
        cost_estimate=cheap(longest),
        name="products",
    )(*arrays)


def to_blocks(gathered, sizes):
    places = gathered.shape[0] // 2
    chunks = gathered.reshape(places, 2, -1, WIDE)
    if places == BLOCKS:
        return chunks
    pieces, at = [], 0
    for size in sizes:
        rows = size * BLOCKS // places
        part = chunks[:, :, at : at + rows].reshape(BLOCKS, -1, 2, rows, WIDE)
        pieces.append(part.transpose(0, 2, 1, 3, 4).reshape(BLOCKS, 2, size, WIDE))
        at += rows
    return jnp.concatenate(pieces, axis=2)


def from_blocks(chunks, sizes):
    places = 1 << len(chip_bits())
    if places == BLOCKS:
        return chunks
    pieces, at = [], 0
    for size in sizes:
        rows = size * BLOCKS // places
        part = chunks[:, :, at : at + size].reshape(BLOCKS, 2, -1, rows, WIDE)
        pieces.append(part.transpose(0, 2, 1, 3, 4).reshape(places, 2, rows, WIDE))
        at += size
    return jnp.concatenate(pieces, axis=2)


def bundle(shards):
    chips, index = lax.axis_size("seq") // 2, lax.axis_index("seq")
    pieces = []
    for shard in shards:
        rows, half = shard.shape[0] // chips, shard.shape[1] // 2
        part = lax.dynamic_slice(shard, (index // 2 * rows, index % 2 * half), (rows, half))
        pieces += [part[:, i : i + WIDE] for i in range(0, half, WIDE)]
    return jnp.concatenate(pieces, axis=0)


def sizes_of(shards):
    tall = lambda s: s.shape[0] * lax.axis_size("dp") // BLOCKS
    return [tall(s) for s in shards for _ in range(0, s.shape[1] // 2, WIDE)]


def thirds_of(shard):
    return [shard[:, i : i + D] for i in range(0, 3 * D, D)]


def gather_weights(shards):
    return lax.all_gather(bundle(shards), BOTH, axis=0)


def gather_first(shards, after):
    values = bundle(shards)
    rows = values.shape[0]
    values = values[None]
    for step, group in enumerate(reversed(groups_of(chip_bits()))):
        pieces = [values if m == 0 else swap(values, m) for m in masks_of(group)]
        if step == 0:
            pieces, after = lax.optimization_barrier((pieces, after))
        values = jnp.stack(absolute(pieces, group), axis=1).reshape(-1, rows, WIDE)
    values = jnp.stack(absolute([values, swap(values, 1)], [1]), axis=1)
    return to_blocks(values.reshape(-1, rows, WIDE), sizes_of(shards)), after


def collect(mine, wanted):
    shares = from_sequence(mine)
    places = 1 << len(chip_bits())
    results, at = [], 0
    for height, width in wanted:
        rows, wide = height // places, width // (2 * WIDE)
        parts = [
            jnp.concatenate([s[at + i * rows : at + (i + 1) * rows] for s in shares[core::2]], axis=0)
            for core in range(2)
            for i in range(wide)
        ]
        results.append(jnp.concatenate(parts, axis=1).astype(jnp.float32))
        at += rows * wide
    return results


def scatter_sums(chunks):
    return lax.psum_scatter(chunks.reshape((-1,) + chunks.shape[2:]), BOTH, scatter_dimension=0)


def stepped_sums(chunks):
    core = own_bit(1)
    arrived = swap(lax.dynamic_index_in_dim(chunks, 1 - core, 1, keepdims=False), 1)
    kept = lax.dynamic_index_in_dim(chunks, core, 1, keepdims=False)
    total = (yield [low(kept.astype(jnp.float32) + arrived.astype(jnp.float32))])[0]
    for group in groups_of(chip_bits()):
        total = (yield [share_low(total, group, 1 << len(group))])[0]
    return total[0]


def everywhere(values):
    groups = groups_of([1] + chip_bits())
    parts = 2 << len(chip_bits())
    rows, wide = values.shape
    if rows < parts:
        for group in groups:
            values = sum(values if m == 0 else swap(values, m) for m in masks_of(group))
            values = (yield [values])[0]
        return values
    total = jnp.pad(values, ((0, -rows % (8 * parts)), (0, 0))).reshape(parts, -1, wide)
    for group in groups:
        total = share_low(total, group, 1 << len(group))
        total = (yield [total])[0]
    for group in reversed(groups):
        pieces = absolute([total if m == 0 else swap(total, m) for m in masks_of(group)], group)
        total = jnp.stack(pieces, axis=1).reshape((-1,) + total.shape[1:])
        total = (yield [total])[0]
    return total.reshape(-1, wide)[:rows]


class Running:
    def __init__(self, steps):
        self.steps, self.values, self.result = steps, None, None
        self.go(None)

    def go(self, values):
        try:
            self.values = self.steps.send(values)
        except StopIteration as end:
            self.values, self.result = [], end.value

    def finish(self):
        while self.result is None:
            self.go(self.values)
        return self.result


def tie(values, *running):
    values, held = lax.optimization_barrier((values, [r.values for r in running]))
    for r, h in zip(running, held):
        if r.result is None:
            r.go(h)
    return values


def attention_backward(grad_attended, kept, mask, between):
    idx, _, feature_k = mask
    keyval, attended, kept_q = kept
    pairs = HEADS // 2
    cut = pairs // 2
    one = attend_back(kept_q, keyval, idx, feature_k, grad_attended, attended, 0, cut)
    one, grad_attended = between((one, grad_attended))
    two = attend_back(kept_q, keyval, idx, feature_k, grad_attended, attended, cut, pairs - cut)
    return one, two


def summed_rows(grad_all):
    rows = grad_all
    for bit in seq_bits()[:-1]:
        half = rows.shape[0] // 2
        rows = rows[:half] + swap(low(rows[half:]), bit).astype(jnp.float32)
    half = rows.shape[0] // 2
    return rows[:half], swap(low(rows[half:]), seq_bits()[-1])


def local(
    tokens,
    lengths,
    classes,
    norm_gains,
    mask_gain,
    enc_qkv,
    enc_out,
    enc_up,
    enc_down,
    dec_qkv,
    dec_out,
    dec_up,
    dec_down,
    patch_proj,
    class_proj,
    mask_cot,
):
    w_first, (tokens, lengths) = gather_first(thirds_of(enc_qkv), (tokens, lengths))
    middle_shards = (enc_down, enc_up, enc_out, *thirds_of(dec_qkv), dec_out)
    last_shards = (dec_down, dec_up, patch_proj, class_proj)
    w_middle = to_blocks(gather_weights(middle_shards), sizes_of(middle_shards))
    gathered_last = gather_weights(last_shards)
    row_count = tokens.shape[1]
    index = lax.axis_index("seq")
    seq_lengths = lengths[0]
    inputs_f = tokens[0].astype(jnp.float32)
    gains_f = norm_gains.astype(jnp.float32)
    classes_f = classes.astype(jnp.float32)
    class_count = classes.shape[0]
    mask_gain_f = mask_gain.astype(jnp.float32)
    steps = jnp.arange(row_count, dtype=jnp.int32)
    seg_query = segment_of(index * row_count + steps, seq_lengths)
    starts = jnp.stack([(index ^ r) * row_count for r in relative()])
    seg_rows = segment_of((starts[:, None] + steps[None, :]).reshape(-1), seq_lengths)
    class_slots = jnp.arange(CLASS_ROWS, dtype=jnp.int32)
    seg_key = jnp.concatenate([seg_rows, jnp.where(class_slots < class_count, -1, IMGS + 1)])
    feature_q, feature_k = features(seg_query, seg_key)
    enc_mask = (active(seg_query, seg_rows), feature_q, feature_k[: seg_rows.shape[0]])
    dec_mask = (active(seg_query, seg_key), feature_q, feature_k)
    valid_rows = (seg_query < IMGS).astype(jnp.float32)[:, None]
    enc_normed = low(norm_rows(inputs_f, gains_f[0]))
    enc_rows = gather_rows(enc_normed)
    keyval, queries = project(enc_rows, row_count, w_first, 0)
    attended, attended_low, kept_q = attend(queries, keyval, *enc_mask)
    enc_attn = (keyval, attended, kept_q)
    enc_low = attended_low
    enc_middle, enc_second, enc_upward, enc_active, encoded, dec_normed = feed_forward(
        tokens[0], attended_low, gains_f[1], gains_f[2], w_middle, 8, w_middle
    )
    class_normed = low(norm_rows(classes_f, gains_f[2]))
    class_padded = jnp.pad(class_normed, ((0, CLASS_ROWS - class_count), (0, 0)))
    dec_rows = jnp.concatenate([gather_rows(dec_normed), class_padded], axis=0)
    keyval, queries = project(dec_rows, row_count, w_middle, 9)
    attended, dec_low, kept_q = attend(queries, keyval, *dec_mask)
    dec_attn = (keyval, attended, kept_q)
    gathered_last, dec_low = lax.optimization_barrier((gathered_last, dec_low))
    w_last = to_blocks(gathered_last, sizes_of(last_shards))
    dec_middle, dec_second, dec_upward, dec_active, decoded, final_normed = feed_forward(
        encoded, dec_low, gains_f[3], gains_f[4], w_middle, 12, w_last
    )
    w_patch, w_class = (
        jnp.concatenate([w_last[:, c, at : at + PIECE].reshape(D, WIDE) for c in range(2)], axis=1)
        for at in (2 * TALL, 2 * TALL + PIECE)
    )
    patch_rows = low(dot(final_normed, w_patch))
    class_rows = dot(classes, w_class)
    class_unit = low(unit_rows(class_rows))
    logits = dot_turned(patch_rows, class_unit)
    mask_out = class_norm(logits, mask_gain_f) * valid_rows
    _, head_back = jax.vjp(class_norm, logits, mask_gain_f)
    grad_logits, grad_mask_gain = head_back(mask_cot[0] * valid_rows)
    grad_logits_low = low(grad_logits)
    grad_patch_rows = low(dot(grad_logits_low, class_unit))
    grad_unit = dot_rows(grad_logits_low, patch_rows)
    grad_final = dot_turned(grad_patch_rows, w_patch)
    _, final_back = jax.vjp(norm_rows, decoded, gains_f[4])
    grad_decoded, grad_gain_last = final_back(grad_final)
    _, unit_back = jax.vjp(unit_rows, class_rows)
    grad_class_rows = low(unit_back(grad_unit)[0])
    grad_classes = dot_turned(grad_class_rows, w_class)
    grad_branch, grad_upward, grad_middle, grad_attn, grad_attended, grad_gain_three = feed_forward_back(
        grad_decoded, dec_upward, dec_middle, gains_f[3], w_middle, 12, w_last
    )
    pad_classes = ((0, CLASS_ROWS - class_count), (0, 0))
    dec_chunks = products(
        [
            (dec_active, [grad_branch]),
            (dec_second, [grad_upward]),
            (dec_low, [grad_attn]),
            (final_normed, [grad_patch_rows]),
            (jnp.pad(classes, pad_classes), [jnp.pad(grad_class_rows, pad_classes)]),
        ]
    )
    dec_chunks, grad_attended = lax.optimization_barrier((dec_chunks, grad_attended))
    dec_sum = scatter_sums(from_blocks(dec_chunks, [TALL] + 7 * [PIECE]))
    one, two = attention_backward(grad_attended, dec_attn, dec_mask, lambda v: v)
    grad_all = rows_back(one, two, w_middle, 9)
    token_rows = row_count * lax.axis_size("seq")
    here, coming = summed_rows(grad_all[:token_rows])
    dec_qkv_chunks = products(
        [(dec_normed, [one[0], two[0]]), (dec_rows, [one[1], two[1]]), (dec_rows, [one[2], two[2]])]
    )
    _, class_back = jax.vjp(norm_rows, classes_f, gains_f[2])
    grad_classes_kv, grad_gain_class = class_back(grad_all[token_rows : token_rows + class_count])
    back, gain_rows = norm_back(here + coming.astype(jnp.float32), encoded, gains_f[2])
    grad_encoded = back + grad_middle
    padded_mask_gain = jnp.pad(grad_mask_gain, (0, D - class_count))
    shared = jnp.concatenate(
        [
            grad_classes + grad_classes_kv,
            jnp.stack(
                [jnp.sum(gain_rows, axis=0) + grad_gain_class, grad_gain_three[0], grad_gain_last, padded_mask_gain]
            ),
        ],
        axis=0,
    )
    shared = Running(everywhere(shared))
    dec_proj = Running(stepped_sums(from_blocks(dec_qkv_chunks, 3 * [PIECE])))
    grad_encoded = tie(grad_encoded, dec_proj, shared)
    grad_branch, grad_upward, grad_middle, grad_attn, grad_attended, grad_gain_one = feed_forward_back(
        grad_encoded, enc_upward, enc_middle, gains_f[1], w_middle, 8, w_middle
    )
    enc_chunks = products(
        [(enc_active, [grad_branch]), (enc_second, [grad_upward]), (enc_low, [grad_attn])]
    )
    enc_chunks, grad_attended, dec_sum = lax.optimization_barrier((enc_chunks, grad_attended, dec_sum))
    enc_sum = scatter_sums(from_blocks(enc_chunks, [TALL] + 5 * [PIECE]))
    grad_attended = tie(grad_attended, dec_proj, shared)
    one, two = attention_backward(
        grad_attended, enc_attn, enc_mask, lambda v: tie(v, dec_proj, shared)
    )
    one, two = tie((one, two), dec_proj, shared)
    grad_all = rows_back(one, two, w_first, 0)
    here, coming = summed_rows(grad_all)
    grad_all, one, two = lax.optimization_barrier((grad_all, one, two))
    enc_qkv_chunks = products(
        [(enc_normed, [one[0], two[0]]), (enc_rows, [one[1], two[1]]), (enc_rows, [one[2], two[2]])]
    )
    enc_proj = Running(stepped_sums(from_blocks(enc_qkv_chunks, 3 * [PIECE])))
    here, coming = tie((here, coming), enc_proj, shared)
    back, gain_rows = norm_back(here + coming.astype(jnp.float32), inputs_f, gains_f[0])
    grad_inputs = back + grad_middle
    late = Running(everywhere(jnp.stack([jnp.sum(gain_rows, axis=0), grad_gain_one[0]])))
    square, wide, tall = (D, D), (D, 4 * D), (4 * D, D)
    thirds = [square] * 3
    out_enc_qkv = jnp.concatenate(collect(enc_proj.finish(), thirds), axis=1)
    late = late.finish()
    out_dec_qkv = jnp.concatenate(collect(dec_proj.finish(), thirds), axis=1)
    shared = shared.finish()
    out_dec = collect(dec_sum, [tall, wide, square, square, square])
    out_enc = collect(enc_sum, [tall, wide, square])
    gain_sums = jnp.concatenate([late, shared[class_count : class_count + 3]], axis=0)
    return (
        mask_out[None],
        grad_inputs[None],
        shared[:class_count],
        gain_sums,
        shared[class_count + 3, :class_count],
        out_enc_qkv,
        out_enc[2],
        out_enc[1],
        out_enc[0],
        out_dec_qkv,
        out_dec[2],
        out_dec[1],
        out_dec[0],
        out_dec[3],
        out_dec[4],
    )


def solution(mesh):
    placed = (
        P("dp", "seq", None),
        P("dp", None),
        P(),
        P(),
        P(),
        P("dp", None),
        P("dp", None),
        P("dp", None),
        P("dp", None),
        P("dp", None),
        P("dp", None),
        P("dp", None),
        P("dp", None),
        P("dp", None),
        P("dp", None),
        P("dp", "seq", None),
    )
    return jax.shard_map(
        local,
        mesh=mesh,
        in_specs=placed,
        out_specs=(
            P("dp", "seq", None),
            P("dp", "seq", None),
            P(),
            P(),
            P(),
            P("dp", None),
            P("dp", None),
            P("dp", None),
            P("dp", None),
            P("dp", None),
            P("dp", None),
            P("dp", None),
            P("dp", None),
            P("dp", None),
            P("dp", None),
        ),
        check_vma=False,
    )
```

```python
import functools
import math

import jax
import jax.numpy as jnp
from jax import lax
from jax.experimental import pallas as pl
from jax.experimental.pallas import tpu as pltpu
from jax.sharding import PartitionSpec as P
HD=64
KB=256
LSE_LANE=10
NEG=-1e30
NT=(((1,),(1,)),((),()))
NN=(((1,),(0,)),((),()))

def split3(v):
    hi=v.astype(jnp.bfloat16).astype(jnp.float32)
    mid=(v-hi).astype(jnp.bfloat16).astype(jnp.float32)
    return hi,mid,v-hi-mid

def fwd_kernel(q_ref, k_ref, v_ref, fq_ref, fk_ref, o_ref, ol_ref, qa_ref):
    lane = lax.broadcasted_iota(jnp.int32, (1, 128), 1)
    low = lane < HD
    fk, k2, v2 = fk_ref[...], k_ref[...], v_ref[...]
    keys = (jnp.where(low, k2, fk), jnp.where(low, fk, k2))
    values = (jnp.where(low, v2, fk), jnp.where(low, fk, v2))
    size = q_ref.shape[0] // 2
    for t in range(2):
        r = slice(t * size, (t + 1) * size)
        q2, fq = q_ref[r] * jnp.bfloat16(0.125), fq_ref[r]
        outs = []
        for h, qs in enumerate((jnp.where(low, q2, fq), jnp.where(low, fq, q2))):
            s = lax.dot_general(qs, keys[h], NT, preferred_element_type=jnp.float32)
            top = jnp.max(s, axis=1, keepdims=True)
            p = jnp.exp(s - top).astype(jnp.bfloat16)
            acc = lax.dot_general(p, values[h], NN, preferred_element_type=jnp.float32)
            base = HD + LSE_LANE if h == 0 else LSE_LANE
            total = acc[:, base : base + 1]
            outs.append(acc / total)
            qa = qs.astype(jnp.float32)
            for j, x in enumerate(split3(-(top + jnp.log(total)))):
                qa = jnp.where(lane == base + j, x, qa)
            qa_ref[h, r] = qa.astype(jnp.bfloat16)
        o = jnp.where(low, outs[0], outs[1])
        o_ref[r] = o
        ol_ref[r] = o.astype(jnp.bfloat16)


def attend(q, kv, fq, fk, heads=12):
    rows, d = q.shape
    nk, pairs = kv.shape[0], heads // 2
    row = pl.BlockSpec((rows, 128), lambda p: (0, p))
    return pl.pallas_call(
        fwd_kernel,
        grid=(pairs,),
        in_specs=[
            row,
            pl.BlockSpec((nk, 128), lambda p: (0, p)),
            pl.BlockSpec((nk, 128), lambda p: (0, p + pairs)),
            pl.BlockSpec((rows, 128), lambda p: (0, 0)),
            pl.BlockSpec((nk, 128), lambda p: (0, 0)),
        ],
        out_specs=[row, row, pl.BlockSpec((2, rows, 128), lambda p: (p, 0, 0))],
        out_shape=[
            jax.ShapeDtypeStruct((rows, d), jnp.float32),
            jax.ShapeDtypeStruct((rows, d), jnp.bfloat16),
            jax.ShapeDtypeStruct((heads, rows, 128), jnp.bfloat16),
        ],
        compiler_params=pltpu.CompilerParams(vmem_limit_bytes=60 << 20),
        cost_estimate=pl.CostEstimate(flops=rows, bytes_accessed=rows, transcendentals=0),
        name="attend",
    )(q, kv, kv, fq, fk)


def bwd_kernel(qa_ref, k_ref, v_ref, fk_ref, g_ref, o_ref, dq_ref, dk_ref, dv_ref, ds_ref):
    nk = k_ref.shape[0]
    lane = lax.broadcasted_iota(jnp.int32, (1, 128), 1)
    low = lane < HD
    g = g_ref[...].astype(jnp.float32)
    prod = g * o_ref[...]
    gs = []
    for h in range(2):
        own = low if h == 0 else jnp.logical_not(low)
        base = HD + LSE_LANE if h == 0 else LSE_LANE
        delta = jnp.sum(jnp.where(own, prod, 0.0), axis=1, keepdims=True)
        ga = jnp.where(own, g, 0.0)
        for j, t in enumerate(split3(-delta)):
            ga = jnp.where(lane == base + j, t, ga)
        gs.append(ga.astype(jnp.bfloat16))
    for at in range(0, nk, 3 * KB):
        r = slice(at, min(at + 3 * KB, nk))
        k2, v2, fk = k_ref[r], v_ref[r], fk_ref[r]
        dks, dvs = [], []
        for h in range(2):
            ka = jnp.where(low, k2, fk) if h == 0 else jnp.where(low, fk, k2)
            va = jnp.where(low, v2, fk) if h == 0 else jnp.where(low, fk, v2)
            pt = jnp.exp(lax.dot_general(ka, qa_ref[h], NT, preferred_element_type=jnp.float32))
            dpt = lax.dot_general(va, gs[h], NT, preferred_element_type=jnp.float32)
            ds = (pt * dpt).astype(jnp.bfloat16)
            ds_ref[h, r] = ds
            dvs.append(lax.dot_general(pt.astype(jnp.bfloat16), gs[h], NN, preferred_element_type=jnp.float32))
            dks.append(lax.dot_general(ds, qa_ref[h], NN, preferred_element_type=jnp.float32))
        dk_ref[r] = jnp.where(low, dks[0], dks[1]).astype(dk_ref.dtype)
        dv_ref[r] = jnp.where(low, dvs[0], dvs[1]).astype(dv_ref.dtype)
    kt = k_ref[...].T
    dqs = [lax.dot_general(kt, ds_ref[h], NN, preferred_element_type=jnp.float32) for h in range(2)]
    top = lax.broadcasted_iota(jnp.int32, (128, 1), 0) < HD
    dq_ref[...] = (jnp.where(top, dqs[0], dqs[1]).T * 0.125).astype(dq_ref.dtype)


def attend_back(qa, kv, fk, g, o, first, count, heads=12):
    rows, nk, pairs = g.shape[0], kv.shape[0], heads // 2
    row = pl.BlockSpec((rows, 128), lambda p: (0, p + first))
    key = pl.BlockSpec((nk, 128), lambda p: (0, p))
    return pl.pallas_call(
        bwd_kernel,
        grid=(count,),
        in_specs=[
            pl.BlockSpec((2, rows, 128), lambda p: (p + first, 0, 0)),
            pl.BlockSpec((nk, 128), lambda p: (0, p + first)),
            pl.BlockSpec((nk, 128), lambda p: (0, p + first + pairs)),
            pl.BlockSpec((nk, 128), lambda p: (0, 0)),
            row,
            row,
        ],
        out_specs=[pl.BlockSpec((rows, 128), lambda p: (0, p)), key, key],
        out_shape=[jax.ShapeDtypeStruct((n, 128 * count), jnp.bfloat16) for n in (rows, nk, nk)],
        scratch_shapes=[pltpu.VMEM((2, nk, rows), jnp.bfloat16)],
        compiler_params=pltpu.CompilerParams(vmem_limit_bytes=60 << 20),
        cost_estimate=pl.CostEstimate(flops=rows, bytes_accessed=rows, transcendentals=0),
        name="attend_back",
    )(qa, kv, kv, fk, g, o)


def features(seg_query,seg_key):
    j=jnp.arange(128,dtype=jnp.int32)[None,:]%HD
    fq=jnp.where((j<10)&(j!=seg_query[:,None]),NEG,0.0).astype(jnp.bfloat16)
    fk=(((j<10)&(j==seg_key[:,None]))|((j>=LSE_LANE)&(j<LSE_LANE+3))).astype(jnp.bfloat16)
    return fq,fk


D = 768
HEADS = 12
IMGS = 8
CLASS_ROWS = 256
WIDE = 384


def norm_rows(values, gain_row):
    centre = values - jnp.mean(values, axis=-1, keepdims=True)
    return centre * lax.rsqrt(jnp.mean(centre * centre, axis=-1, keepdims=True) + 1e-06) * gain_row


def class_norm(logits, gain_row):
    centre = logits - jnp.mean(logits, axis=-1, keepdims=True)
    return centre * lax.rsqrt(jnp.mean(centre * centre, axis=-1, keepdims=True) + 1e-05) * gain_row


def unit_rows(values):
    return values * lax.rsqrt(jnp.sum(values * values, axis=-1, keepdims=True) + 1e-06)


def dot(left, right):
    return jnp.dot(left, right, preferred_element_type=jnp.float32)


def dot_rows(left, right):
    return lax.dot_general(left, right, (((0,), (0,)), ((), ())), preferred_element_type=jnp.float32)


def dot_turned(left, right):
    return lax.dot_general(left, right, (((1,), (1,)), ((), ())), preferred_element_type=jnp.float32)


def low(values):
    return values.astype(jnp.bfloat16)


BOTH = ("dp", "seq")


def bits_of(count):
    return [1 << i for i in range(count.bit_length() - 1)]


def seq_bits():
    return bits_of(lax.axis_size("seq"))


def chip_bits():
    return bits_of(lax.axis_size("seq") * lax.axis_size("dp"))[1:]


def swap(values, mask):
    inner, outer = lax.axis_size("seq"), lax.axis_size("dp")
    place = [(i % inner) * outer + i // inner for i in range(inner * outer)]
    pairs = [(place[i], place[i ^ mask]) for i in range(inner * outer)]
    return lax.ppermute(values, ("seq", "dp"), pairs)


def own_bit(bit):
    return (lax.axis_index(BOTH) // bit) % 2


def masks_of(bits):
    masks = [0]
    for bit in bits:
        masks = masks + [m | bit for m in masks]
    return masks


def groups_of(bits):
    return [bits[i : i + 2] for i in range(0, len(bits), 2)]


def absolute(pieces, bits):
    for i, bit in enumerate(bits):
        same = own_bit(bit) == 0
        pieces = [jnp.where(same, p, pieces[k ^ (1 << i)]) for k, p in enumerate(pieces)]
    return pieces


def gather_rows(rows):
    for bit in reversed(seq_bits()):
        rows = jnp.concatenate([rows, swap(rows, bit)], axis=0)
    return rows


def relative():
    return masks_of(seq_bits()[::-1])


def segment_of(places, seq_lengths):
    count = seq_lengths.shape[0]
    before = jnp.arange(count)[None, :] <= jnp.arange(count)[:, None]
    boundary = jnp.sum(jnp.where(before, seq_lengths[None, :], 0), axis=1)
    return jnp.sum((places[:, None] >= boundary[None, :]).astype(jnp.int32), axis=1)


def from_sequence(mine):
    bits = seq_bits()
    return absolute([mine if m == 0 else swap(mine, m) for m in masks_of(bits)], bits)


def share_low(total, group, width):
    values = total.reshape((total.shape[0] // width, width) + total.shape[1:])
    own = lax.axis_index(BOTH)
    pieces = []
    for m in masks_of(group):
        place = ((own ^ m) // group[0]) % width
        piece = lax.dynamic_index_in_dim(values, place, 1, keepdims=False)
        pieces.append(piece if m == 0 else swap(piece, m))
    return sum(p.astype(jnp.float32) for p in pieces).astype(total.dtype)


BLOCKS = 16
PIECE = 48
TALL = 192
TN = (((0,), (0,)), ((), ()))


def cheap(rows):
    return pl.CostEstimate(flops=rows, bytes_accessed=rows, transcendentals=0)


def dot_nn(left, right):
    return lax.dot_general(left, right, NN, preferred_element_type=jnp.float32)


def dot_nt(left, right):
    return lax.dot_general(left, right, NT, preferred_element_type=jnp.float32)


def mat(chunk):
    return chunk.reshape(-1, WIDE)


def columns(c):
    return slice(c * WIDE, (c + 1) * WIDE)


def joined(chunk):
    return jnp.concatenate([mat(chunk[:, 0]), mat(chunk[:, 1])], axis=1)


def gelu_parts(u):
    root = math.sqrt(2.0 / math.pi)
    t = jnp.tanh(root * (u + 0.044715 * (u * u * u)))
    return 0.5 * (1.0 + t), 0.5 * u * (1.0 - t * t) * (root * (1.0 + (3 * 0.044715) * (u * u)))


def qkv_kernel(rows_ref, w_ref, kv_ref, q_ref):
    step = pl.program_id(0)
    weight = joined(w_ref[...])

    @pl.when(step < 2)
    def _():
        kv_ref[...] = dot_nn(rows_ref[...], weight).astype(kv_ref.dtype)

    @pl.when(step == 2)
    def _():
        q_ref[...] = dot_nn(rows_ref[: q_ref.shape[0]], weight).astype(q_ref.dtype)


def project(rows_all, own, weights, first):
    count = rows_all.shape[0]
    return pl.pallas_call(
        qkv_kernel,
        grid=(3,),
        in_specs=[
            pl.BlockSpec((count, D), lambda t: (0, 0)),
            pl.BlockSpec((BLOCKS, 2, PIECE, WIDE), lambda t: (0, 0, jnp.where(t < 2, first + 1 + t, first), 0)),
        ],
        out_specs=[
            pl.BlockSpec((count, D), lambda t: (0, jnp.minimum(t, 1))),
            pl.BlockSpec((own, D), lambda t: (0, 0)),
        ],
        out_shape=[
            jax.ShapeDtypeStruct((count, 2 * D), jnp.bfloat16),
            jax.ShapeDtypeStruct((own, D), jnp.bfloat16),
        ],
        compiler_params=pltpu.CompilerParams(vmem_limit_bytes=60 << 20),
        cost_estimate=cheap(own),
        name="project",
    )(rows_all, weights)


def halves(ref):
    half = ref.shape[0] // 2
    return (slice(0, half), slice(half, 2 * half))


def mlp_kernel(h_ref, o_ref, gain_ref, next_ref, wo_ref, wu_ref, wd_ref, mid_ref, sec_ref, u_ref, act_ref, res_ref, nrm_ref):
    step = pl.program_id(0)

    @pl.when(step == 0)
    def _():
        middle = h_ref[...].astype(jnp.float32) + dot_nn(o_ref[...], joined(wo_ref[...]))
        mid_ref[...] = middle
        sec_ref[...] = norm_rows(middle, gain_ref[...]).astype(sec_ref.dtype)
        res_ref[...] = middle

    up = jnp.concatenate([mat(wu_ref[:, 0, :PIECE]), mat(wu_ref[:, 0, PIECE:])], axis=1)
    down = joined(wd_ref[...])
    for part in halves(sec_ref):
        u = dot_nn(sec_ref[part], up)
        u_ref[part] = u.astype(u_ref.dtype)
        active_part = (u * gelu_parts(u)[0]).astype(act_ref.dtype)
        act_ref[part] = active_part
        res_ref[part] += dot_nn(active_part, down)

    @pl.when(step == 3)
    def _():
        nrm_ref[...] = norm_rows(res_ref[...], next_ref[...]).astype(nrm_ref.dtype)


def mlp_specs(out_piece):
    return [
        pl.BlockSpec((BLOCKS, 2, PIECE, WIDE), lambda t: (0, 0, out_piece, 0)),
        pl.BlockSpec((BLOCKS, 1, 2 * PIECE, WIDE), lambda t: (0, t // 2, 2 + t % 2, 0)),
        pl.BlockSpec((BLOCKS // 4, 2, TALL, WIDE), lambda t: (t, 0, 0, 0)),
    ]


def whole(shape):
    return pl.BlockSpec(shape, lambda t: (0,) * len(shape))


def feed_forward(hidden, attended, gain, next_gain, w_out, out_piece, w_mlp):
    rows = hidden.shape[0]
    full, tile = (rows, D), pl.BlockSpec((rows, D), lambda t: (0, t))
    return pl.pallas_call(
        mlp_kernel,
        grid=(4,),
        in_specs=[whole(full), whole(full), whole((1, D)), whole((1, D)), *mlp_specs(out_piece)],
        out_specs=[whole(full), whole(full), tile, tile, whole(full), whole(full)],
        out_shape=[
            jax.ShapeDtypeStruct(full, jnp.float32),
            jax.ShapeDtypeStruct(full, jnp.bfloat16),
            jax.ShapeDtypeStruct((rows, 4 * D), jnp.bfloat16),
            jax.ShapeDtypeStruct((rows, 4 * D), jnp.bfloat16),
            jax.ShapeDtypeStruct(full, jnp.float32),
            jax.ShapeDtypeStruct(full, jnp.bfloat16),
        ],
        compiler_params=pltpu.CompilerParams(vmem_limit_bytes=60 << 20),
        cost_estimate=cheap(rows),
        name="feed_forward",
    )(hidden, attended, gain[None], next_gain[None], w_out, w_mlp, w_mlp)


def norm_back(grad, values, gain):
    centre = values - jnp.mean(values, axis=-1, keepdims=True)
    scale = lax.rsqrt(jnp.mean(centre * centre, axis=-1, keepdims=True) + 1e-06)
    unit = centre * scale
    inner = grad * gain
    inner = inner - jnp.mean(inner, axis=-1, keepdims=True) - unit * jnp.mean(inner * unit, axis=-1, keepdims=True)
    return inner * scale, grad * unit


def mlp_back_kernel(g_ref, u_ref, mid_ref, gain_ref, wo_ref, wu_ref, wd_ref, gb_ref, gu_ref, gm_ref, ga_ref, gat_ref, gg_ref, acc):
    step = pl.program_id(0)

    @pl.when(step == 0)
    def _():
        gb_ref[...] = g_ref[...].astype(gb_ref.dtype)
        acc[...] = jnp.zeros(acc.shape, jnp.float32)

    up = jnp.concatenate([mat(wu_ref[:, 0, :PIECE]), mat(wu_ref[:, 0, PIECE:])], axis=1)
    down = joined(wd_ref[...])
    for part in halves(gb_ref):
        grad = dot_nt(gb_ref[part], down)
        gu = (grad * sum(gelu_parts(u_ref[part].astype(jnp.float32)))).astype(gu_ref.dtype)
        gu_ref[part] = gu
        acc[part] += dot_nt(gu, up)

    @pl.when(step == 3)
    def _():
        back, gain_rows = norm_back(acc[...], mid_ref[...], gain_ref[...])
        middle = back + g_ref[...]
        gm_ref[...] = middle
        gg_ref[...] = jnp.sum(gain_rows, axis=0, keepdims=True)
        low_middle = middle.astype(ga_ref.dtype)
        ga_ref[...] = low_middle
        gat_ref[...] = dot_nt(low_middle, joined(wo_ref[...])).astype(gat_ref.dtype)


def feed_forward_back(grad, upward, middle, gain, w_out, out_piece, w_mlp):
    rows = grad.shape[0]
    full, tile = (rows, D), pl.BlockSpec((rows, D), lambda t: (0, t))
    return pl.pallas_call(
        mlp_back_kernel,
        grid=(4,),
        in_specs=[whole(full), tile, whole(full), whole((1, D)), *mlp_specs(out_piece)],
        out_specs=[whole(full), tile, whole(full), whole(full), whole(full), whole((1, D))],
        out_shape=[
            jax.ShapeDtypeStruct(full, jnp.bfloat16),
            jax.ShapeDtypeStruct((rows, 4 * D), jnp.bfloat16),
            jax.ShapeDtypeStruct(full, jnp.float32),
            jax.ShapeDtypeStruct(full, jnp.bfloat16),
            jax.ShapeDtypeStruct(full, jnp.bfloat16),
            jax.ShapeDtypeStruct((1, D), jnp.float32),
        ],
        scratch_shapes=[pltpu.VMEM(full, jnp.float32)],
        compiler_params=pltpu.CompilerParams(vmem_limit_bytes=60 << 20),
        cost_estimate=cheap(rows),
        name="feed_forward_back",
    )(grad, upward, middle, gain[None], w_out, w_mlp, w_mlp)


def rows_back_kernel(steps, half, dk0, dk1, dv0, dv1, dq0, dq1, wq_ref, wk_ref, wv_ref, near_ref, far_ref, full):
    step = pl.program_id(0)

    @pl.when(step == 0)
    def _():
        full[:, :D] = joined(wk_ref[...])
        full[:, D:] = joined(wv_ref[...])

    rows = jnp.concatenate([dk0[...], dk1[...], dv0[...], dv1[...]], axis=1)
    total = dot_nt(rows, full[...])
    away = (step >= half) & (step < 2 * half)

    @pl.when(away)
    def _():
        far_ref[...] = total.astype(far_ref.dtype)

    @pl.when(jnp.logical_not(away))
    def _():
        near_ref[...] = total

    @pl.when(step < steps)
    def _():
        near_ref[...] += dot_nt(jnp.concatenate([dq0[...], dq1[...]], axis=1), joined(wq_ref[...]))


def rows_back(one, two, weights, first):
    count, size = one[1].shape[0], one[0].shape[0]
    tokens = count // size * size
    if count != tokens:
        size = math.gcd(count, size)
    steps, half = one[0].shape[0] // size, tokens // (2 * size)
    tile = pl.BlockSpec((size, WIDE), lambda t: (t, 0))
    query = pl.BlockSpec((size, WIDE), lambda t: (jnp.minimum(t, steps - 1), 0))
    piece = lambda i: pl.BlockSpec((BLOCKS, 2, PIECE, WIDE), lambda t: (0, 0, first + i, 0))
    near = lambda t: (jnp.where(t < half, t, jnp.where(t < 2 * half, half, t - half)), 0)
    far = lambda t: (jnp.clip(t - half, 0, half - 1), 0)
    rest = count - half * size
    spare = rest + size if count == tokens else rest
    return pl.pallas_call(
        functools.partial(rows_back_kernel, steps, half),
        grid=(count // size,),
        in_specs=[tile, tile, tile, tile, query, query, piece(0), piece(1), piece(2)],
        out_specs=[pl.BlockSpec((size, D), near), pl.BlockSpec((size, D), far)],
        out_shape=[
            jax.ShapeDtypeStruct((spare, D), jnp.float32),
            jax.ShapeDtypeStruct((half * size, D), jnp.bfloat16),
        ],
        scratch_shapes=[pltpu.VMEM((D, 2 * D), jnp.bfloat16)],
        compiler_params=pltpu.CompilerParams(vmem_limit_bytes=60 << 20),
        cost_estimate=cheap(size),
        name="rows_back",
    )(one[1], two[1], one[2], two[2], one[0], two[0], weights, weights, weights)


def products_kernel(plan, count_in, *refs):
    ins, (out_ref, turned) = refs[:count_in], refs[-2:]
    step = pl.program_id(0)
    for left, rights, begin, tiles, tall in plan:
        count = ins[left].shape[0]

        @pl.when(step == begin)
        def _():
            for i in range(0, ins[left].shape[1], D):
                part = ins[left][:, i : i + D].T
                if tall:
                    turned[i // TALL : (i + D) // TALL, :, :count] = part.reshape(D // TALL, TALL, count)
                else:
                    turned[:, :PIECE, :count] = part.reshape(BLOCKS, PIECE, count)

        @pl.when((step >= begin) & (step < begin + tiles))
        def _():
            n = step - begin
            if tall:
                at = pl.multiple_of(n * PIECE, PIECE)
                rows = turned[:, pl.ds(at, PIECE), :count].reshape(D, count)
            else:
                rows = turned[:, :PIECE, :count].reshape(D, count)
            if len(rights) == 2:
                right = jnp.concatenate([ins[r][...] for r in rights], axis=1)
            elif tall or tiles == 1:
                right = ins[rights[0]][...]
            else:
                half = tiles * WIDE
                parts = [
                    ins[rights[0]][:, pl.ds(pl.multiple_of(n * WIDE + c * half, WIDE), WIDE)] for c in range(2)
                ]
                right = jnp.concatenate(parts, axis=1)
            part = dot_nn(rows, right).astype(out_ref.dtype)
            for c in range(2):
                out_ref[:, c] = part[:, columns(c)].reshape(BLOCKS, PIECE, WIDE)


def products(wanted, into=None, first=0, pieces=None):
    arrays, plan, steps = [], [], 0

    def place(array):
        for i, known in enumerate(arrays):
            if known is array:
                return i
        arrays.append(array)
        return len(arrays) - 1

    for left, rights in wanted:
        tall = left.shape[1] != D
        tiles = left.shape[1] // D if tall else sum(r.shape[1] for r in rights) // D
        plan.append((place(left), [place(r) for r in rights], steps, tiles, tall))
        steps += tiles
    given = [] if into is None else [into]
    longest = max(left.shape[0] for left, _ in wanted)
    height = TALL if any(p[4] for p in plan) else PIECE
    return pl.pallas_call(
        functools.partial(products_kernel, plan, len(arrays)),
        grid=(steps,),
        in_specs=[pl.BlockSpec(a.shape, lambda t: (0, 0), pipeline_mode=pl.Buffered(1)) for a in arrays]
        + [pl.BlockSpec(memory_space=pl.ANY)] * len(given),
        out_specs=pl.BlockSpec((BLOCKS, 2, PIECE, WIDE), lambda t: (0, 0, first + t, 0)),
        out_shape=jax.ShapeDtypeStruct((BLOCKS, 2, (pieces or steps) * PIECE, WIDE), jnp.bfloat16),
        input_output_aliases={len(arrays): 0} if given else {},
        scratch_shapes=[pltpu.VMEM((BLOCKS, height, longest), jnp.bfloat16)],
        compiler_params=pltpu.CompilerParams(vmem_limit_bytes=60 << 20),
        cost_estimate=cheap(longest),
        name="products",
    )(*arrays, *given)


def to_blocks(gathered, sizes):
    places = gathered.shape[0] // 2
    chunks = gathered.reshape(places, 2, -1, WIDE)
    if places == BLOCKS:
        return chunks
    pieces, at = [], 0
    for size in sizes:
        rows = size * BLOCKS // places
        part = chunks[:, :, at : at + rows].reshape(BLOCKS, -1, 2, rows, WIDE)
        pieces.append(part.transpose(0, 2, 1, 3, 4).reshape(BLOCKS, 2, size, WIDE))
        at += rows
    return jnp.concatenate(pieces, axis=2)


def from_blocks(chunks, sizes):
    places = 1 << len(chip_bits())
    if places == BLOCKS:
        return chunks
    pieces, at = [], 0
    for size in sizes:
        rows = size * BLOCKS // places
        part = chunks[:, :, at : at + size].reshape(BLOCKS, 2, -1, rows, WIDE)
        pieces.append(part.transpose(0, 2, 1, 3, 4).reshape(places, 2, rows, WIDE))
        at += size
    return jnp.concatenate(pieces, axis=2)


def bundle(shards):
    chips, index = lax.axis_size("seq") // 2, lax.axis_index("seq")
    pieces = []
    for shard in shards:
        rows, half = shard.shape[0] // chips, shard.shape[1] // 2
        part = lax.dynamic_slice(shard, (index // 2 * rows, index % 2 * half), (rows, half))
        pieces += [part[:, i : i + WIDE] for i in range(0, half, WIDE)]
    return jnp.concatenate(pieces, axis=0)


def sizes_of(shards):
    tall = lambda s: s.shape[0] * lax.axis_size("dp") // BLOCKS
    return [tall(s) for s in shards for _ in range(0, s.shape[1] // 2, WIDE)]


def thirds_of(shard):
    return [shard[:, i : i + D] for i in range(0, 3 * D, D)]


def gather_weights(shards):
    return lax.all_gather(bundle(shards), BOTH, axis=0)


def gather_first(shards, after):
    values = bundle(shards)
    rows = values.shape[0]
    values = values[None]
    for step, group in enumerate(reversed(groups_of(chip_bits()))):
        pieces = [values if m == 0 else swap(values, m) for m in masks_of(group)]
        if step == 0:
            pieces, after = lax.optimization_barrier((pieces, after))
        values = jnp.stack(absolute(pieces, group), axis=1).reshape(-1, rows, WIDE)
    values = jnp.stack(absolute([values, swap(values, 1)], [1]), axis=1)
    return to_blocks(values.reshape(-1, rows, WIDE), sizes_of(shards)), after


def collect_kernel(plan, own_ref, *refs):
    count = len(refs) - len({p[3] for p in plan})
    ins, outs = refs[:count], refs[count:]
    for own in range(count):

        @pl.when(own_ref[0] == own)
        def _():
            for device in range(count):
                y, core = device // 2, device % 2
                for half, at, rows, out, column in plan:
                    if half == core:
                        part = ins[device ^ own][at : at + rows].astype(jnp.float32)
                        outs[out][y * rows : (y + 1) * rows, column : column + WIDE] = part


def collect(mine, wanted, outs):
    bits = seq_bits()
    held = {0: mine}
    for bit in reversed(bits):
        held.update({m | bit: swap(t, bit) for m, t in list(held.items())})
    pieces = [held[m] for m in masks_of(bits)]
    places = 1 << len(chip_bits())
    plan, shapes, at = [], {}, 0
    for (height, width), out in zip(wanted, outs):
        rows, half = height // places, width // 2
        begin = shapes.get(out, (0, 0))[1]
        for i in range(0, half, WIDE):
            plan += [(core, at, rows, out, begin + core * half + i) for core in range(2)]
            at += rows
        shapes[out] = (height // lax.axis_size("dp"), begin + width)
    if any(p[2] % 16 for p in plan):
        shares = absolute(pieces, bits)
        results = [jnp.zeros(shape, jnp.float32) for shape in shapes.values()]
        for core, at, rows, out, column in plan:
            for y, share in enumerate(shares[core::2]):
                part = share[at : at + rows].astype(jnp.float32)
                results[out] = results[out].at[y * rows : (y + 1) * rows, column : column + WIDE].set(part)
        return results, pieces
    spec = pltpu.PrefetchScalarGridSpec(
        num_scalar_prefetch=1,
        grid=(1,),
        in_specs=[pl.BlockSpec(mine.shape, lambda t, own: (0, 0)) for _ in pieces],
        out_specs=[pl.BlockSpec(shape, lambda t, own: (0, 0)) for shape in shapes.values()],
    )
    results = pl.pallas_call(
        functools.partial(collect_kernel, plan),
        grid_spec=spec,
        out_shape=[jax.ShapeDtypeStruct(shape, jnp.float32) for shape in shapes.values()],
        compiler_params=pltpu.CompilerParams(vmem_limit_bytes=40 << 20),
        cost_estimate=cheap(D),
        name="collect",
    )(lax.axis_index("seq").reshape(1), *pieces)
    return results, pieces


def across(pieces):
    shares = absolute(pieces, seq_bits())
    rows = jnp.concatenate([jnp.concatenate(shares[i : i + 2], axis=1) for i in range(0, len(shares), 2)], axis=0)
    total = rows[None]
    for group in groups_of(chip_bits()[len(seq_bits()) - 1 :]):
        total = jnp.stack(absolute([total if m == 0 else swap(total, m) for m in masks_of(group)], group), axis=0)
        total = total.reshape((-1,) + rows.shape)
    return total.reshape(-1, rows.shape[1])


def scatter_sums(chunks):
    return lax.psum_scatter(chunks.reshape((-1,) + chunks.shape[2:]), BOTH, scatter_dimension=0)


def stepped_sums(chunks):
    core = own_bit(1)
    arrived = swap(lax.dynamic_index_in_dim(chunks, 1 - core, 1, keepdims=False), 1)
    kept = lax.dynamic_index_in_dim(chunks, core, 1, keepdims=False)
    total = (yield [low(kept.astype(jnp.float32) + arrived.astype(jnp.float32))])[0]
    for group in groups_of(chip_bits()):
        total = (yield [share_low(total, group, 1 << len(group))])[0]
    return total[0]


def everywhere(values):
    for group in groups_of([1] + chip_bits()):
        values = sum(values if m == 0 else swap(values, m) for m in masks_of(group))
        values = (yield [values])[0]
    return values


def waited(values):
    return (yield [values])[0]


class Running:
    def __init__(self, steps):
        self.steps, self.values, self.result = steps, None, None
        self.go(None)

    def go(self, values):
        try:
            self.values = self.steps.send(values)
        except StopIteration as end:
            self.values, self.result = [], end.value

    def finish(self):
        while self.result is None:
            self.go(self.values)
        return self.result


def tie(values, *running):
    values, held = lax.optimization_barrier((values, [r.values for r in running]))
    for r, h in zip(running, held):
        if r.result is None:
            r.go(h)
    return values


def attention_backward(grad_attended, kept, mask, between):
    feature_k = mask[1]
    keyval, attended, kept_q = kept
    pairs = HEADS // 2
    cut = pairs // 2
    one = attend_back(kept_q, keyval, feature_k, grad_attended, attended, 0, cut)
    one, grad_attended = between((one, grad_attended))
    two = attend_back(kept_q, keyval, feature_k, grad_attended, attended, cut, pairs - cut)
    return one, two


def summed_rows(near, far):
    rows = near[: far.shape[0]] + swap(far, 1).astype(jnp.float32)
    for bit in seq_bits()[1:-1]:
        half = rows.shape[0] // 2
        rows = rows[:half] + swap(low(rows[half:]), bit).astype(jnp.float32)
    half = rows.shape[0] // 2
    return rows[:half], low(rows[half:])


def local(
    tokens,
    lengths,
    classes,
    norm_gains,
    mask_gain,
    enc_qkv,
    enc_out,
    enc_up,
    enc_down,
    dec_qkv,
    dec_out,
    dec_up,
    dec_down,
    patch_proj,
    class_proj,
    mask_cot,
):
    w_first, (tokens, lengths) = gather_first(thirds_of(enc_qkv), (tokens, lengths))
    middle_shards = (enc_down, enc_up, enc_out, *thirds_of(dec_qkv), dec_out)
    last_shards = (dec_down, dec_up, patch_proj, class_proj)
    w_middle = to_blocks(gather_weights(middle_shards), sizes_of(middle_shards))
    gathered_last = gather_weights(last_shards)
    row_count = tokens.shape[1]
    index = lax.axis_index("seq")
    seq_lengths = lengths[0]
    inputs_f = tokens[0].astype(jnp.float32)
    gains_f = norm_gains.astype(jnp.float32)
    classes_f = classes.astype(jnp.float32)
    class_count = classes.shape[0]
    mask_gain_f = mask_gain.astype(jnp.float32)
    steps = jnp.arange(row_count, dtype=jnp.int32)
    seg_query = segment_of(index * row_count + steps, seq_lengths)
    starts = jnp.stack([(index ^ r) * row_count for r in relative()])
    seg_rows = segment_of((starts[:, None] + steps[None, :]).reshape(-1), seq_lengths)
    class_slots = jnp.arange(CLASS_ROWS, dtype=jnp.int32)
    seg_key = jnp.concatenate([seg_rows, jnp.where(class_slots < class_count, -1, IMGS + 1)])
    feature_q, feature_k = features(seg_query, seg_key)
    enc_mask = (feature_q, feature_k[: seg_rows.shape[0]])
    dec_mask = (feature_q, feature_k)
    valid_rows = (seg_query < IMGS).astype(jnp.float32)[:, None]
    enc_normed = low(norm_rows(inputs_f, gains_f[0]))
    enc_rows = gather_rows(enc_normed)
    keyval, queries = project(enc_rows, row_count, w_first, 0)
    attended, attended_low, kept_q = attend(queries, keyval, *enc_mask)
    enc_attn = (keyval, attended, kept_q)
    enc_low = attended_low
    enc_middle, enc_second, enc_upward, enc_active, encoded, dec_normed = feed_forward(
        tokens[0], attended_low, gains_f[1], gains_f[2], w_middle, 8, w_middle
    )
    class_normed = low(norm_rows(classes_f, gains_f[2]))
    class_padded = jnp.pad(class_normed, ((0, CLASS_ROWS - class_count), (0, 0)))
    dec_rows = jnp.concatenate([gather_rows(dec_normed), class_padded], axis=0)
    keyval, queries = project(dec_rows, row_count, w_middle, 9)
    attended, dec_low, kept_q = attend(queries, keyval, *dec_mask)
    dec_attn = (keyval, attended, kept_q)
    gathered_last, dec_low = lax.optimization_barrier((gathered_last, dec_low))
    w_last = to_blocks(gathered_last, sizes_of(last_shards))
    dec_middle, dec_second, dec_upward, dec_active, decoded, final_normed = feed_forward(
        encoded, dec_low, gains_f[3], gains_f[4], w_middle, 12, w_last
    )
    w_patch, w_class = (
        jnp.concatenate([w_last[:, c, at : at + PIECE].reshape(D, WIDE) for c in range(2)], axis=1)
        for at in (2 * TALL, 2 * TALL + PIECE)
    )
    patch_rows = low(dot(final_normed, w_patch))
    class_rows = dot(classes, w_class)
    class_unit = low(unit_rows(class_rows))
    logits = dot_turned(patch_rows, class_unit)
    mask_out = class_norm(logits, mask_gain_f) * valid_rows
    _, head_back = jax.vjp(class_norm, logits, mask_gain_f)
    grad_logits, grad_mask_gain = head_back(mask_cot[0] * valid_rows)
    grad_logits_low = low(grad_logits)
    grad_patch_rows = low(dot(grad_logits_low, class_unit))
    grad_unit = dot_rows(grad_logits_low, patch_rows)
    grad_final = dot_turned(grad_patch_rows, w_patch)
    _, final_back = jax.vjp(norm_rows, decoded, gains_f[4])
    grad_decoded, grad_gain_last = final_back(grad_final)
    _, unit_back = jax.vjp(unit_rows, class_rows)
    grad_class_rows = low(unit_back(grad_unit)[0])
    grad_classes = dot_turned(grad_class_rows, w_class)
    grad_branch, grad_upward, grad_middle, grad_attn, grad_attended, grad_gain_three = feed_forward_back(
        grad_decoded, dec_upward, dec_middle, gains_f[3], w_middle, 12, w_last
    )
    pad_classes = ((0, CLASS_ROWS - class_count), (0, 0))
    dec_chunks = products(
        [
            (dec_active, [grad_branch]),
            (dec_second, [grad_upward]),
            (dec_low, [grad_attn]),
            (final_normed, [grad_patch_rows]),
            (jnp.pad(classes, pad_classes), [jnp.pad(grad_class_rows, pad_classes)]),
        ]
    )
    dec_chunks, grad_attended = lax.optimization_barrier((dec_chunks, grad_attended))
    dec_sum = scatter_sums(from_blocks(dec_chunks, [TALL] + 7 * [PIECE]))
    one, two = attention_backward(grad_attended, dec_attn, dec_mask, lambda v: v)
    near, far = rows_back(one, two, w_middle, 9)
    here, going = summed_rows(near, far)
    going, one, two = lax.optimization_barrier((going, one, two))
    coming = swap(going, seq_bits()[-1])
    dec_qkv_chunks = products(
        [(dec_normed, [one[0], two[0]]), (dec_rows, [one[1], two[1]]), (dec_rows, [one[2], two[2]])],
        first=9,
        pieces=12,
    )
    _, class_back = jax.vjp(norm_rows, classes_f, gains_f[2])
    grad_classes_kv, grad_gain_class = class_back(near[far.shape[0] : far.shape[0] + class_count])
    coming, dec_qkv_chunks = lax.optimization_barrier((coming, dec_qkv_chunks))
    back, gain_rows = norm_back(here + coming.astype(jnp.float32), encoded, gains_f[2])
    grad_encoded = back + grad_middle
    padded_mask_gain = jnp.pad(grad_mask_gain, (0, D - class_count))
    shared = jnp.concatenate(
        [
            grad_classes + grad_classes_kv,
            jnp.stack(
                [jnp.sum(gain_rows, axis=0) + grad_gain_class, grad_gain_three[0], grad_gain_last, padded_mask_gain]
            ),
        ],
        axis=0,
    )
    per_block = CLASS_ROWS // BLOCKS
    shared = low(jnp.pad(shared, ((0, CLASS_ROWS - shared.shape[0]), (0, 0))))
    shared = shared.reshape(BLOCKS, per_block, 2, WIDE).transpose(0, 2, 1, 3)
    grad_branch, grad_upward, grad_middle, grad_attn, grad_attended, grad_gain_one = feed_forward_back(
        grad_encoded, enc_upward, enc_middle, gains_f[1], w_middle, 8, w_middle
    )
    enc_chunks = products(
        [(enc_active, [grad_branch]), (enc_second, [grad_upward]), (enc_low, [grad_attn])],
        into=dec_qkv_chunks,
        pieces=12,
    )
    enc_chunks, grad_attended = lax.optimization_barrier((enc_chunks, grad_attended))
    enc_sum = scatter_sums(from_blocks(enc_chunks, [TALL] + 8 * [PIECE]))
    dec_sum = Running(waited(dec_sum))
    one, two = attention_backward(grad_attended, enc_attn, enc_mask, lambda v: tie(v, dec_sum))
    here, going = summed_rows(*rows_back(one, two, w_first, 0))
    going, one, two = lax.optimization_barrier((going, one, two))
    coming = swap(going, seq_bits()[-1])
    enc_qkv_chunks = products(
        [(enc_normed, [one[0], two[0]]), (enc_rows, [one[1], two[1]]), (enc_rows, [one[2], two[2]])]
    )
    enc_qkv_chunks = jnp.concatenate([enc_qkv_chunks, shared], axis=2)
    enc_proj = Running(stepped_sums(from_blocks(enc_qkv_chunks, 3 * [PIECE] + [per_block])))
    here, coming = tie((here, coming), enc_proj)
    back, gain_rows = norm_back(here + coming.astype(jnp.float32), inputs_f, gains_f[0])
    grad_inputs = back + grad_middle
    late = Running(everywhere(jnp.stack([jnp.sum(gain_rows, axis=0), grad_gain_one[0]])))
    square, wide, tall = (D, D), (D, 4 * D), (4 * D, D)
    qkv = [square, square, square]
    (out_enc_qkv,), shares = collect(enc_proj.finish(), qkv, [0, 0, 0])
    dec_sum, shares = lax.optimization_barrier((dec_sum.finish(), shares))
    shared = across([t[-(per_block * BLOCKS >> len(chip_bits())) :] for t in shares]).astype(jnp.float32)
    late = late.finish()
    out_dec, _ = collect(dec_sum, [tall, wide, square, square, square], range(5))
    out_enc, _ = collect(enc_sum, [tall, wide, square] + qkv, [0, 1, 2, 3, 3, 3])
    out_dec_qkv = out_enc[3]
    gain_sums = jnp.concatenate([late, shared[class_count : class_count + 3]], axis=0)
    return (
        mask_out[None],
        grad_inputs[None],
        shared[:class_count],
        gain_sums,
        shared[class_count + 3, :class_count],
        out_enc_qkv,
        out_enc[2],
        out_enc[1],
        out_enc[0],
        out_dec_qkv,
        out_dec[2],
        out_dec[1],
        out_dec[0],
        out_dec[3],
        out_dec[4],
    )


def solution(mesh):
    placed = (
        P("dp", "seq", None),
        P("dp", None),
        P(),
        P(),
        P(),
        P("dp", None),
        P("dp", None),
        P("dp", None),
        P("dp", None),
        P("dp", None),
        P("dp", None),
        P("dp", None),
        P("dp", None),
        P("dp", None),
        P("dp", None),
        P("dp", "seq", None),
    )
    return jax.shard_map(
        local,
        mesh=mesh,
        in_specs=placed,
        out_specs=(
            P("dp", "seq", None),
            P("dp", "seq", None),
            P(),
            P(),
            P(),
            P("dp", None),
            P("dp", None),
            P("dp", None),
            P("dp", None),
            P("dp", None),
            P("dp", None),
            P("dp", None),
            P("dp", None),
            P("dp", None),
            P("dp", None),
        ),
        check_vma=False,
    )
```

```python
import functools
import math

import jax
import jax.numpy as jnp
from jax import lax
from jax.experimental import pallas as pl
from jax.experimental.pallas import tpu as pltpu
from jax.sharding import PartitionSpec as P
HD=64
KB=256
LSE_LANE=10
NEG=-1e30
NT=(((1,),(1,)),((),()))
NN=(((1,),(0,)),((),()))

def split3(v):
    hi=v.astype(jnp.bfloat16).astype(jnp.float32)
    mid=(v-hi).astype(jnp.bfloat16).astype(jnp.float32)
    return hi,mid,v-hi-mid

def fwd_kernel(q_ref, k_ref, v_ref, fq_ref, fk_ref, o_ref, ol_ref, qa_ref):
    lane = lax.broadcasted_iota(jnp.int32, (1, 128), 1)
    low = lane < HD
    fk, k2, v2 = fk_ref[...], k_ref[...], v_ref[...]
    keys = (jnp.where(low, k2, fk), jnp.where(low, fk, k2))
    values = (jnp.where(low, v2, fk), jnp.where(low, fk, v2))
    size = q_ref.shape[0] // 2
    for t in range(2):
        r = slice(t * size, (t + 1) * size)
        q2, fq = q_ref[r] * jnp.bfloat16(0.125), fq_ref[r]
        outs = []
        for h, qs in enumerate((jnp.where(low, q2, fq), jnp.where(low, fq, q2))):
            s = lax.dot_general(qs, keys[h], NT, preferred_element_type=jnp.float32)
            top = jnp.max(s, axis=1, keepdims=True)
            p = jnp.exp(s - top).astype(jnp.bfloat16)
            acc = lax.dot_general(p, values[h], NN, preferred_element_type=jnp.float32)
            base = HD + LSE_LANE if h == 0 else LSE_LANE
            total = acc[:, base : base + 1]
            outs.append(acc / total)
            qa = qs.astype(jnp.float32)
            for j, x in enumerate(split3(-(top + jnp.log(total)))):
                qa = jnp.where(lane == base + j, x, qa)
            qa_ref[h, r] = qa.astype(jnp.bfloat16)
        o = jnp.where(low, outs[0], outs[1])
        o_ref[r] = o
        ol_ref[r] = o.astype(jnp.bfloat16)


def attend(q, kv, fq, fk, heads=12):
    rows, d = q.shape
    nk, pairs = kv.shape[0], heads // 2
    row = pl.BlockSpec((rows, 128), lambda p: (0, p))
    return pl.pallas_call(
        fwd_kernel,
        grid=(pairs,),
        in_specs=[
            row,
            pl.BlockSpec((nk, 128), lambda p: (0, p)),
            pl.BlockSpec((nk, 128), lambda p: (0, p + pairs)),
            pl.BlockSpec((rows, 128), lambda p: (0, 0)),
            pl.BlockSpec((nk, 128), lambda p: (0, 0)),
        ],
        out_specs=[row, row, pl.BlockSpec((2, rows, 128), lambda p: (p, 0, 0))],
        out_shape=[
            jax.ShapeDtypeStruct((rows, d), jnp.float32),
            jax.ShapeDtypeStruct((rows, d), jnp.bfloat16),
            jax.ShapeDtypeStruct((heads, rows, 128), jnp.bfloat16),
        ],
        compiler_params=pltpu.CompilerParams(vmem_limit_bytes=60 << 20),
        cost_estimate=pl.CostEstimate(flops=rows, bytes_accessed=rows, transcendentals=0),
        name="attend",
    )(q, kv, kv, fq, fk)


def bwd_kernel(qa_ref, k_ref, v_ref, fk_ref, g_ref, o_ref, dq_ref, dk_ref, dv_ref, ds_ref):
    nk = k_ref.shape[0]
    lane = lax.broadcasted_iota(jnp.int32, (1, 128), 1)
    low = lane < HD
    g = g_ref[...].astype(jnp.float32)
    prod = g * o_ref[...]
    gs = []
    for h in range(2):
        own = low if h == 0 else jnp.logical_not(low)
        base = HD + LSE_LANE if h == 0 else LSE_LANE
        delta = jnp.sum(jnp.where(own, prod, 0.0), axis=1, keepdims=True)
        ga = jnp.where(own, g, 0.0)
        for j, t in enumerate(split3(-delta)):
            ga = jnp.where(lane == base + j, t, ga)
        gs.append(ga.astype(jnp.bfloat16))
    for at in range(0, nk, 3 * KB):
        r = slice(at, min(at + 3 * KB, nk))
        k2, v2, fk = k_ref[r], v_ref[r], fk_ref[r]
        dks, dvs = [], []
        for h in range(2):
            ka = jnp.where(low, k2, fk) if h == 0 else jnp.where(low, fk, k2)
            va = jnp.where(low, v2, fk) if h == 0 else jnp.where(low, fk, v2)
            pt = jnp.exp(lax.dot_general(ka, qa_ref[h], NT, preferred_element_type=jnp.float32))
            dpt = lax.dot_general(va, gs[h], NT, preferred_element_type=jnp.float32)
            ds = (pt * dpt).astype(jnp.bfloat16)
            ds_ref[h, r] = ds
            dvs.append(lax.dot_general(pt.astype(jnp.bfloat16), gs[h], NN, preferred_element_type=jnp.float32))
            dks.append(lax.dot_general(ds, qa_ref[h], NN, preferred_element_type=jnp.float32))
        dk_ref[r] = jnp.where(low, dks[0], dks[1]).astype(dk_ref.dtype)
        dv_ref[r] = jnp.where(low, dvs[0], dvs[1]).astype(dv_ref.dtype)
    kt = k_ref[...].T
    dqs = [lax.dot_general(kt, ds_ref[h], NN, preferred_element_type=jnp.float32) for h in range(2)]
    top = lax.broadcasted_iota(jnp.int32, (128, 1), 0) < HD
    dq_ref[...] = (jnp.where(top, dqs[0], dqs[1]).T * 0.125).astype(dq_ref.dtype)


def attend_back(qa, kv, fk, g, o, first, count, heads=12):
    rows, nk, pairs = g.shape[0], kv.shape[0], heads // 2
    row = pl.BlockSpec((rows, 128), lambda p: (0, p + first))
    key = pl.BlockSpec((nk, 128), lambda p: (0, p))
    return pl.pallas_call(
        bwd_kernel,
        grid=(count,),
        in_specs=[
            pl.BlockSpec((2, rows, 128), lambda p: (p + first, 0, 0)),
            pl.BlockSpec((nk, 128), lambda p: (0, p + first)),
            pl.BlockSpec((nk, 128), lambda p: (0, p + first + pairs)),
            pl.BlockSpec((nk, 128), lambda p: (0, 0)),
            row,
            row,
        ],
        out_specs=[pl.BlockSpec((rows, 128), lambda p: (0, p)), key, key],
        out_shape=[jax.ShapeDtypeStruct((n, 128 * count), jnp.bfloat16) for n in (rows, nk, nk)],
        scratch_shapes=[pltpu.VMEM((2, nk, rows), jnp.bfloat16)],
        compiler_params=pltpu.CompilerParams(vmem_limit_bytes=60 << 20),
        cost_estimate=pl.CostEstimate(flops=rows, bytes_accessed=rows, transcendentals=0),
        name="attend_back",
    )(qa, kv, kv, fk, g, o)


def features(seg_query,seg_key):
    j=jnp.arange(128,dtype=jnp.int32)[None,:]%HD
    fq=jnp.where((j<10)&(j!=seg_query[:,None]),NEG,0.0).astype(jnp.bfloat16)
    fk=(((j<10)&(j==seg_key[:,None]))|((j>=LSE_LANE)&(j<LSE_LANE+3))).astype(jnp.bfloat16)
    return fq,fk


D = 768
HEADS = 12
IMGS = 8
CLASS_ROWS = 256
WIDE = 384


def norm_rows(values, gain_row):
    centre = values - jnp.mean(values, axis=-1, keepdims=True)
    return centre * lax.rsqrt(jnp.mean(centre * centre, axis=-1, keepdims=True) + 1e-06) * gain_row


def class_norm(logits, gain_row):
    centre = logits - jnp.mean(logits, axis=-1, keepdims=True)
    return centre * lax.rsqrt(jnp.mean(centre * centre, axis=-1, keepdims=True) + 1e-05) * gain_row


def unit_rows(values):
    return values * lax.rsqrt(jnp.sum(values * values, axis=-1, keepdims=True) + 1e-06)


def dot(left, right):
    return jnp.dot(left, right, preferred_element_type=jnp.float32)


def dot_rows(left, right):
    return lax.dot_general(left, right, (((0,), (0,)), ((), ())), preferred_element_type=jnp.float32)


def dot_turned(left, right):
    return lax.dot_general(left, right, (((1,), (1,)), ((), ())), preferred_element_type=jnp.float32)


def low(values):
    return values.astype(jnp.bfloat16)


BOTH = ("dp", "seq")


def bits_of(count):
    return [1 << i for i in range(count.bit_length() - 1)]


def seq_bits():
    return bits_of(lax.axis_size("seq"))


def chip_bits():
    return bits_of(lax.axis_size("seq") * lax.axis_size("dp"))[1:]


def swap(values, mask):
    inner, outer = lax.axis_size("seq"), lax.axis_size("dp")
    place = [(i % inner) * outer + i // inner for i in range(inner * outer)]
    pairs = [(place[i], place[i ^ mask]) for i in range(inner * outer)]
    return lax.ppermute(values, ("seq", "dp"), pairs)


def own_bit(bit):
    return (lax.axis_index(BOTH) // bit) % 2


def masks_of(bits):
    masks = [0]
    for bit in bits:
        masks = masks + [m | bit for m in masks]
    return masks


def groups_of(bits):
    return [bits[i : i + 2] for i in range(0, len(bits), 2)]


def absolute(pieces, bits):
    for i, bit in enumerate(bits):
        same = own_bit(bit) == 0
        pieces = [jnp.where(same, p, pieces[k ^ (1 << i)]) for k, p in enumerate(pieces)]
    return pieces


def gather_rows(rows):
    for bit in reversed(seq_bits()):
        rows = jnp.concatenate([rows, swap(rows, bit)], axis=0)
    return rows


def relative():
    return masks_of(seq_bits()[::-1])


def segment_of(places, seq_lengths):
    count = seq_lengths.shape[0]
    before = jnp.arange(count)[None, :] <= jnp.arange(count)[:, None]
    boundary = jnp.sum(jnp.where(before, seq_lengths[None, :], 0), axis=1)
    return jnp.sum((places[:, None] >= boundary[None, :]).astype(jnp.int32), axis=1)


def from_sequence(mine):
    bits = seq_bits()
    return absolute([mine if m == 0 else swap(mine, m) for m in masks_of(bits)], bits)


def halve(total, bit, near, done):
    low_bits = 1 if len(near) - done == 1 else 1 << near.index(bit)
    values = total.reshape((total.shape[0] // (2 * low_bits), 2, low_bits) + total.shape[1:])
    own = own_bit(bit)
    arrived = swap(lax.dynamic_index_in_dim(values, 1 - own, 1, keepdims=False), bit)
    kept = lax.dynamic_index_in_dim(values, own, 1, keepdims=False)
    result = low(kept.astype(jnp.float32) + arrived.astype(jnp.float32))
    return result.reshape((-1,) + total.shape[1:])


def share_low(total, group, width):
    values = total.reshape((total.shape[0] // width, width) + total.shape[1:])
    own = lax.axis_index(BOTH)
    pieces = []
    for m in masks_of(group):
        place = ((own ^ m) // group[0]) % width
        piece = lax.dynamic_index_in_dim(values, place, 1, keepdims=False)
        pieces.append(piece if m == 0 else swap(piece, m))
    return sum(p.astype(jnp.float32) for p in pieces).astype(total.dtype)


BLOCKS = 16
PIECE = 48
TALL = 192
TN = (((0,), (0,)), ((), ()))


def cheap(rows):
    return pl.CostEstimate(flops=rows, bytes_accessed=rows, transcendentals=0)


def dot_nn(left, right):
    return lax.dot_general(left, right, NN, preferred_element_type=jnp.float32)


def dot_nt(left, right):
    return lax.dot_general(left, right, NT, preferred_element_type=jnp.float32)


def mat(chunk):
    return chunk.reshape(-1, WIDE)


def columns(c):
    return slice(c * WIDE, (c + 1) * WIDE)


def joined(chunk):
    return jnp.concatenate([mat(chunk[:, 0]), mat(chunk[:, 1])], axis=1)


def gelu_parts(u):
    root = math.sqrt(2.0 / math.pi)
    t = jnp.tanh(root * (u + 0.044715 * (u * u * u)))
    return 0.5 * (1.0 + t), 0.5 * u * (1.0 - t * t) * (root * (1.0 + (3 * 0.044715) * (u * u)))


def qkv_kernel(rows_ref, w_ref, kv_ref, q_ref):
    step = pl.program_id(0)
    weight = joined(w_ref[...])

    @pl.when(step < 2)
    def _():
        kv_ref[...] = dot_nn(rows_ref[...], weight).astype(kv_ref.dtype)

    @pl.when(step == 2)
    def _():
        q_ref[...] = dot_nn(rows_ref[: q_ref.shape[0]], weight).astype(q_ref.dtype)


def project(rows_all, own, weights, first):
    count = rows_all.shape[0]
    return pl.pallas_call(
        qkv_kernel,
        grid=(3,),
        in_specs=[
            pl.BlockSpec((count, D), lambda t: (0, 0)),
            pl.BlockSpec((BLOCKS, 2, PIECE, WIDE), lambda t: (0, 0, jnp.where(t < 2, first + 1 + t, first), 0)),
        ],
        out_specs=[
            pl.BlockSpec((count, D), lambda t: (0, jnp.minimum(t, 1))),
            pl.BlockSpec((own, D), lambda t: (0, 0)),
        ],
        out_shape=[
            jax.ShapeDtypeStruct((count, 2 * D), jnp.bfloat16),
            jax.ShapeDtypeStruct((own, D), jnp.bfloat16),
        ],
        compiler_params=pltpu.CompilerParams(vmem_limit_bytes=60 << 20),
        cost_estimate=cheap(own),
        name="project",
    )(rows_all, weights)


def halves(ref):
    half = ref.shape[0] // 2
    return (slice(0, half), slice(half, 2 * half))


def mlp_kernel(h_ref, o_ref, gain_ref, next_ref, wo_ref, wu_ref, wd_ref, mid_ref, sec_ref, u_ref, act_ref, res_ref, nrm_ref):
    step = pl.program_id(0)

    @pl.when(step == 0)
    def _():
        middle = h_ref[...].astype(jnp.float32) + dot_nn(o_ref[...], joined(wo_ref[...]))
        mid_ref[...] = middle
        sec_ref[...] = norm_rows(middle, gain_ref[...]).astype(sec_ref.dtype)
        res_ref[...] = middle

    up = jnp.concatenate([mat(wu_ref[:, 0, :PIECE]), mat(wu_ref[:, 0, PIECE:])], axis=1)
    down = joined(wd_ref[...])
    for part in halves(sec_ref):
        u = dot_nn(sec_ref[part], up)
        u_ref[part] = u.astype(u_ref.dtype)
        active_part = (u * gelu_parts(u)[0]).astype(act_ref.dtype)
        act_ref[part] = active_part
        res_ref[part] += dot_nn(active_part, down)

    @pl.when(step == 3)
    def _():
        nrm_ref[...] = norm_rows(res_ref[...], next_ref[...]).astype(nrm_ref.dtype)


def mlp_specs(out_piece):
    return [
        pl.BlockSpec((BLOCKS, 2, PIECE, WIDE), lambda t: (0, 0, out_piece, 0)),
        pl.BlockSpec((BLOCKS, 1, 2 * PIECE, WIDE), lambda t: (0, t // 2, 2 + t % 2, 0)),
        pl.BlockSpec((BLOCKS // 4, 2, TALL, WIDE), lambda t: (t, 0, 0, 0)),
    ]


def whole(shape):
    return pl.BlockSpec(shape, lambda t: (0,) * len(shape))


def feed_forward(hidden, attended, gain, next_gain, w_out, out_piece, w_mlp):
    rows = hidden.shape[0]
    full, tile = (rows, D), pl.BlockSpec((rows, D), lambda t: (0, t))
    return pl.pallas_call(
        mlp_kernel,
        grid=(4,),
        in_specs=[whole(full), whole(full), whole((1, D)), whole((1, D)), *mlp_specs(out_piece)],
        out_specs=[whole(full), whole(full), tile, tile, whole(full), whole(full)],
        out_shape=[
            jax.ShapeDtypeStruct(full, jnp.float32),
            jax.ShapeDtypeStruct(full, jnp.bfloat16),
            jax.ShapeDtypeStruct((rows, 4 * D), jnp.bfloat16),
            jax.ShapeDtypeStruct((rows, 4 * D), jnp.bfloat16),
            jax.ShapeDtypeStruct(full, jnp.float32),
            jax.ShapeDtypeStruct(full, jnp.bfloat16),
        ],
        compiler_params=pltpu.CompilerParams(vmem_limit_bytes=60 << 20),
        cost_estimate=cheap(rows),
        name="feed_forward",
    )(hidden, attended, gain[None], next_gain[None], w_out, w_mlp, w_mlp)


def norm_back(grad, values, gain):
    centre = values - jnp.mean(values, axis=-1, keepdims=True)
    scale = lax.rsqrt(jnp.mean(centre * centre, axis=-1, keepdims=True) + 1e-06)
    unit = centre * scale
    inner = grad * gain
    inner = inner - jnp.mean(inner, axis=-1, keepdims=True) - unit * jnp.mean(inner * unit, axis=-1, keepdims=True)
    return inner * scale, grad * unit


def mlp_back_kernel(g_ref, u_ref, mid_ref, gain_ref, wo_ref, wu_ref, wd_ref, gb_ref, gu_ref, gm_ref, ga_ref, gat_ref, gg_ref, acc):
    step = pl.program_id(0)

    @pl.when(step == 0)
    def _():
        gb_ref[...] = g_ref[...].astype(gb_ref.dtype)
        acc[...] = jnp.zeros(acc.shape, jnp.float32)

    up = jnp.concatenate([mat(wu_ref[:, 0, :PIECE]), mat(wu_ref[:, 0, PIECE:])], axis=1)
    down = joined(wd_ref[...])
    for part in halves(gb_ref):
        grad = dot_nt(gb_ref[part], down)
        gu = (grad * sum(gelu_parts(u_ref[part].astype(jnp.float32)))).astype(gu_ref.dtype)
        gu_ref[part] = gu
        acc[part] += dot_nt(gu, up)

    @pl.when(step == 3)
    def _():
        back, gain_rows = norm_back(acc[...], mid_ref[...], gain_ref[...])
        middle = back + g_ref[...]
        gm_ref[...] = middle
        gg_ref[...] = jnp.sum(gain_rows, axis=0, keepdims=True)
        low_middle = middle.astype(ga_ref.dtype)
        ga_ref[...] = low_middle
        gat_ref[...] = dot_nt(low_middle, joined(wo_ref[...])).astype(gat_ref.dtype)


def feed_forward_back(grad, upward, middle, gain, w_out, out_piece, w_mlp):
    rows = grad.shape[0]
    full, tile = (rows, D), pl.BlockSpec((rows, D), lambda t: (0, t))
    return pl.pallas_call(
        mlp_back_kernel,
        grid=(4,),
        in_specs=[whole(full), tile, whole(full), whole((1, D)), *mlp_specs(out_piece)],
        out_specs=[whole(full), tile, whole(full), whole(full), whole(full), whole((1, D))],
        out_shape=[
            jax.ShapeDtypeStruct(full, jnp.bfloat16),
            jax.ShapeDtypeStruct((rows, 4 * D), jnp.bfloat16),
            jax.ShapeDtypeStruct(full, jnp.float32),
            jax.ShapeDtypeStruct(full, jnp.bfloat16),
            jax.ShapeDtypeStruct(full, jnp.bfloat16),
            jax.ShapeDtypeStruct((1, D), jnp.float32),
        ],
        scratch_shapes=[pltpu.VMEM(full, jnp.float32)],
        compiler_params=pltpu.CompilerParams(vmem_limit_bytes=60 << 20),
        cost_estimate=cheap(rows),
        name="feed_forward_back",
    )(grad, upward, middle, gain[None], w_out, w_mlp, w_mlp)


def rows_back_kernel(steps, half, dk0, dk1, dv0, dv1, dq0, dq1, wq_ref, wk_ref, wv_ref, near_ref, far_ref, full):
    step = pl.program_id(0)

    @pl.when(step == 0)
    def _():
        full[:, :D] = joined(wk_ref[...])
        full[:, D:] = joined(wv_ref[...])

    rows = jnp.concatenate([dk0[...], dk1[...], dv0[...], dv1[...]], axis=1)
    total = dot_nt(rows, full[...])
    away = (step >= half) & (step < 2 * half)

    @pl.when(away)
    def _():
        far_ref[...] = total.astype(far_ref.dtype)

    @pl.when(jnp.logical_not(away))
    def _():
        near_ref[...] = total

    @pl.when(step < steps)
    def _():
        near_ref[...] += dot_nt(jnp.concatenate([dq0[...], dq1[...]], axis=1), joined(wq_ref[...]))


def rows_back(one, two, weights, first):
    count, size = one[1].shape[0], one[0].shape[0]
    tokens = count // size * size
    if count != tokens:
        size = math.gcd(count, size)
    steps, half = one[0].shape[0] // size, tokens // (2 * size)
    tile = pl.BlockSpec((size, WIDE), lambda t: (t, 0))
    query = pl.BlockSpec((size, WIDE), lambda t: (jnp.minimum(t, steps - 1), 0))
    piece = lambda i: pl.BlockSpec((BLOCKS, 2, PIECE, WIDE), lambda t: (0, 0, first + i, 0))
    near = lambda t: (jnp.where(t < half, t, jnp.where(t < 2 * half, half, t - half)), 0)
    far = lambda t: (jnp.clip(t - half, 0, half - 1), 0)
    rest = count - half * size
    spare = rest + size if count == tokens else rest
    return pl.pallas_call(
        functools.partial(rows_back_kernel, steps, half),
        grid=(count // size,),
        in_specs=[tile, tile, tile, tile, query, query, piece(0), piece(1), piece(2)],
        out_specs=[pl.BlockSpec((size, D), near), pl.BlockSpec((size, D), far)],
        out_shape=[
            jax.ShapeDtypeStruct((spare, D), jnp.float32),
            jax.ShapeDtypeStruct((half * size, D), jnp.bfloat16),
        ],
        scratch_shapes=[pltpu.VMEM((D, 2 * D), jnp.bfloat16)],
        compiler_params=pltpu.CompilerParams(vmem_limit_bytes=60 << 20),
        cost_estimate=cheap(size),
        name="rows_back",
    )(one[1], two[1], one[2], two[2], one[0], two[0], weights, weights, weights)


def products_kernel(plan, count_in, outs, *refs):
    ins, turned = refs[outs - 1 : outs - 1 + count_in], refs[-1]
    out_refs = refs[-1 - outs : -1]
    step = pl.program_id(0)
    for left, rights, begin, tiles, tall in plan:
        count = ins[left].shape[0]

        @pl.when(step == begin)
        def _():
            for i in range(0, ins[left].shape[1], D):
                part = ins[left][:, i : i + D].T
                if tall:
                    turned[i // TALL : (i + D) // TALL, :, :count] = part.reshape(D // TALL, TALL, count)
                else:
                    turned[:, :PIECE, :count] = part.reshape(BLOCKS, PIECE, count)

        @pl.when((step >= begin) & (step < begin + tiles))
        def _():
            n = step - begin
            if tall:
                at = pl.multiple_of(n * PIECE, PIECE)
                rows = turned[:, pl.ds(at, PIECE), :count].reshape(D, count)
            else:
                rows = turned[:, :PIECE, :count].reshape(D, count)
            if len(rights) == 2:
                right = jnp.concatenate([ins[r][...] for r in rights], axis=1)
            elif tall or tiles == 1:
                right = ins[rights[0]][...]
            else:
                half = tiles * WIDE
                parts = [
                    ins[rights[0]][:, pl.ds(pl.multiple_of(n * WIDE + c * half, WIDE), WIDE)] for c in range(2)
                ]
                right = jnp.concatenate(parts, axis=1)
            part = dot_nn(rows, right).astype(jnp.bfloat16)
            chunk = [part[:, columns(c)].reshape(BLOCKS, PIECE, WIDE) for c in range(2)]
            if outs == 1:
                for c in range(2):
                    out_refs[0][:, c] = chunk[c]
            else:
                for core in range(2):

                    @pl.when(refs[0][0] == core)
                    def _():
                        out_refs[0][...] = chunk[1 - core]
                        out_refs[1][...] = chunk[core]


def products(wanted, core=None, into=(), first=0, pieces=None):
    arrays, plan, steps = [], [], 0

    def place(array):
        for i, known in enumerate(arrays):
            if known is array:
                return i
        arrays.append(array)
        return len(arrays) - 1

    for left, rights in wanted:
        tall = left.shape[1] != D
        tiles = left.shape[1] // D if tall else sum(r.shape[1] for r in rights) // D
        plan.append((place(left), [place(r) for r in rights], steps, tiles, tall))
        steps += tiles
    longest = max(left.shape[0] for left, _ in wanted)
    height = TALL if any(p[4] for p in plan) else PIECE
    rows = (pieces or steps) * PIECE
    outs = 1 if core is None else 2
    if core is None:
        block, shape = (BLOCKS, 2, PIECE, WIDE), (BLOCKS, 2, rows, WIDE)
        where = lambda t: (0, 0, first + t, 0)
    else:
        block, shape = (BLOCKS, PIECE, WIDE), (BLOCKS, rows, WIDE)
        where = lambda t, _: (0, first + t, 0)
    spec = pltpu.PrefetchScalarGridSpec(
        num_scalar_prefetch=outs - 1,
        grid=(steps,),
        in_specs=[pl.BlockSpec(a.shape, lambda t, *_: (0, 0), pipeline_mode=pl.Buffered(1)) for a in arrays]
        + [pl.BlockSpec(memory_space=pl.ANY)] * len(into),
        out_specs=[pl.BlockSpec(block, where)] * outs,
        scratch_shapes=[pltpu.VMEM((BLOCKS, height, longest), jnp.bfloat16)],
    )
    result = pl.pallas_call(
        functools.partial(products_kernel, plan, len(arrays), outs),
        grid_spec=spec,
        out_shape=[jax.ShapeDtypeStruct(shape, jnp.bfloat16)] * outs,
        input_output_aliases={outs - 1 + len(arrays) + i: i for i in range(len(into))},
        compiler_params=pltpu.CompilerParams(vmem_limit_bytes=60 << 20),
        cost_estimate=cheap(longest),
        name="products",
    )(*([] if core is None else [core.reshape(1)]), *arrays, *into)
    return result[0] if core is None else result


def to_blocks(gathered, sizes):
    places = gathered.shape[0] // 2
    chunks = gathered.reshape(places, 2, -1, WIDE)
    if places == BLOCKS:
        return chunks
    pieces, at = [], 0
    for size in sizes:
        rows = size * BLOCKS // places
        part = chunks[:, :, at : at + rows].reshape(BLOCKS, -1, 2, rows, WIDE)
        pieces.append(part.transpose(0, 2, 1, 3, 4).reshape(BLOCKS, 2, size, WIDE))
        at += rows
    return jnp.concatenate(pieces, axis=2)


def from_blocks(chunks, sizes):
    places = 1 << len(chip_bits())
    if places == BLOCKS:
        return chunks
    pieces, at = [], 0
    for size in sizes:
        rows = size * BLOCKS // places
        part = chunks[:, :, at : at + size].reshape(BLOCKS, 2, -1, rows, WIDE)
        pieces.append(part.transpose(0, 2, 1, 3, 4).reshape(places, 2, rows, WIDE))
        at += size
    return jnp.concatenate(pieces, axis=2)


def bundle(shards):
    chips, index = lax.axis_size("seq") // 2, lax.axis_index("seq")
    pieces = []
    for shard in shards:
        rows, half = shard.shape[0] // chips, shard.shape[1] // 2
        part = lax.dynamic_slice(shard, (index // 2 * rows, index % 2 * half), (rows, half))
        pieces += [part[:, i : i + WIDE] for i in range(0, half, WIDE)]
    return jnp.concatenate(pieces, axis=0)


def sizes_of(shards):
    tall = lambda s: s.shape[0] * lax.axis_size("dp") // BLOCKS
    return [tall(s) for s in shards for _ in range(0, s.shape[1] // 2, WIDE)]


def thirds_of(shard):
    return [shard[:, i : i + D] for i in range(0, 3 * D, D)]


def gather_weights(shards):
    return lax.all_gather(bundle(shards), BOTH, axis=0)


def gather_first(shards, after):
    values = bundle(shards)
    rows = values.shape[0]
    values = values[None]
    for step, group in enumerate(reversed(groups_of(chip_bits()))):
        pieces = [values if m == 0 else swap(values, m) for m in masks_of(group)]
        if step == 0:
            pieces, after = lax.optimization_barrier((pieces, after))
        values = jnp.stack(absolute(pieces, group), axis=1).reshape(-1, rows, WIDE)
    values = jnp.stack(absolute([values, swap(values, 1)], [1]), axis=1)
    return to_blocks(values.reshape(-1, rows, WIDE), sizes_of(shards)), after


def collect_kernel(plan, own_ref, *refs):
    count = len(refs) - len({p[3] for p in plan})
    ins, outs = refs[:count], refs[count:]
    for own in range(count):

        @pl.when(own_ref[0] == own)
        def _():
            for device in range(count):
                y, core = device // 2, device % 2
                for half, at, rows, out, column in plan:
                    if half == core:
                        part = ins[device ^ own][at : at + rows].astype(jnp.float32)
                        outs[out][y * rows : (y + 1) * rows, column : column + WIDE] = part


def collect(mine, wanted, outs):
    bits = seq_bits()
    held = {0: mine}
    for bit in reversed(bits):
        held.update({m | bit: swap(t, bit) for m, t in list(held.items())})
    pieces = [held[m] for m in masks_of(bits)]
    places = 1 << len(chip_bits())
    plan, shapes, at = [], {}, 0
    for (height, width), out in zip(wanted, outs):
        rows, half = height // places, width // 2
        begin = shapes.get(out, (0, 0))[1]
        for i in range(0, half, WIDE):
            plan += [(core, at, rows, out, begin + core * half + i) for core in range(2)]
            at += rows
        shapes[out] = (height // lax.axis_size("dp"), begin + width)
    if any(p[2] % 16 for p in plan):
        shares = absolute(pieces, bits)
        results = [jnp.zeros(shape, jnp.float32) for shape in shapes.values()]
        for core, at, rows, out, column in plan:
            for y, share in enumerate(shares[core::2]):
                part = share[at : at + rows].astype(jnp.float32)
                results[out] = results[out].at[y * rows : (y + 1) * rows, column : column + WIDE].set(part)
        return results, pieces
    spec = pltpu.PrefetchScalarGridSpec(
        num_scalar_prefetch=1,
        grid=(1,),
        in_specs=[pl.BlockSpec(mine.shape, lambda t, own: (0, 0)) for _ in pieces],
        out_specs=[pl.BlockSpec(shape, lambda t, own: (0, 0)) for shape in shapes.values()],
    )
    results = pl.pallas_call(
        functools.partial(collect_kernel, plan),
        grid_spec=spec,
        out_shape=[jax.ShapeDtypeStruct(shape, jnp.float32) for shape in shapes.values()],
        compiler_params=pltpu.CompilerParams(vmem_limit_bytes=40 << 20),
        cost_estimate=cheap(D),
        name="collect",
    )(lax.axis_index("seq").reshape(1), *pieces)
    return results, pieces


def across(pieces):
    shares = absolute(pieces, seq_bits())
    rows = jnp.concatenate([jnp.concatenate(shares[i : i + 2], axis=1) for i in range(0, len(shares), 2)], axis=0)
    total = rows[None]
    for group in groups_of(chip_bits()[len(seq_bits()) - 1 :]):
        total = jnp.stack(absolute([total if m == 0 else swap(total, m) for m in masks_of(group)], group), axis=0)
        total = total.reshape((-1,) + rows.shape)
    return total.reshape(-1, rows.shape[1])


def scatter_sums(chunks):
    return lax.psum_scatter(chunks.reshape((-1,) + chunks.shape[2:]), BOTH, scatter_dimension=0)


def stepped_sums(send, keep, sizes, classes):
    if 1 << len(chip_bits()) != BLOCKS:
        chunks = from_blocks(jnp.stack([send, keep], axis=1), sizes)
        send, keep = chunks[:, 0], chunks[:, 1]
    arrived = swap(send, 1)
    total = low(keep.astype(jnp.float32) + arrived.astype(jnp.float32))
    bits = chip_bits()
    if classes == 2:
        near, bits = bits[:2], bits[2:]
        cut = total.shape[1] // 2
        parts = yield [total[:, :cut], total[:, cut:]]
        for i in range(2):
            parts = yield [halve(t, bit, near, i) for t, bit in zip(parts, (near[i], near[1 - i]))]
        total = jnp.concatenate(parts, axis=1)
    else:
        total = (yield [total])[0]
    for group in groups_of(bits):
        total = (yield [share_low(total, group, 1 << len(group))])[0]
    return total[0]


def everywhere(values):
    for group in groups_of([1] + chip_bits()):
        values = sum(values if m == 0 else swap(values, m) for m in masks_of(group))
        values = (yield [values])[0]
    return values


def waited(values):
    return (yield [values])[0]


class Running:
    def __init__(self, steps):
        self.steps, self.values, self.result = steps, None, None
        self.go(None)

    def go(self, values):
        try:
            self.values = self.steps.send(values)
        except StopIteration as end:
            self.values, self.result = [], end.value

    def finish(self):
        while self.result is None:
            self.go(self.values)
        return self.result


def tie(values, *running):
    values, held = lax.optimization_barrier((values, [r.values for r in running]))
    for r, h in zip(running, held):
        if r.result is None:
            r.go(h)
    return values


def attention_backward(grad_attended, kept, mask, between):
    feature_k = mask[1]
    keyval, attended, kept_q = kept
    pairs = HEADS // 2
    cut = pairs // 2
    one = attend_back(kept_q, keyval, feature_k, grad_attended, attended, 0, cut)
    one, grad_attended = between((one, grad_attended))
    two = attend_back(kept_q, keyval, feature_k, grad_attended, attended, cut, pairs - cut)
    return one, two


def summed_rows(near, far):
    rows = near[: far.shape[0]] + swap(far, 1).astype(jnp.float32)
    for bit in seq_bits()[1:-1]:
        half = rows.shape[0] // 2
        rows = rows[:half] + swap(low(rows[half:]), bit).astype(jnp.float32)
    half = rows.shape[0] // 2
    return rows[:half], low(rows[half:])


def local(
    tokens,
    lengths,
    classes,
    norm_gains,
    mask_gain,
    enc_qkv,
    enc_out,
    enc_up,
    enc_down,
    dec_qkv,
    dec_out,
    dec_up,
    dec_down,
    patch_proj,
    class_proj,
    mask_cot,
):
    w_first, (tokens, lengths) = gather_first(thirds_of(enc_qkv), (tokens, lengths))
    middle_shards = (enc_down, enc_up, enc_out, *thirds_of(dec_qkv), dec_out)
    last_shards = (dec_down, dec_up, patch_proj, class_proj)
    w_middle = to_blocks(gather_weights(middle_shards), sizes_of(middle_shards))
    gathered_last = gather_weights(last_shards)
    core = own_bit(1)
    row_count = tokens.shape[1]
    index = lax.axis_index("seq")
    seq_lengths = lengths[0]
    inputs_f = tokens[0].astype(jnp.float32)
    gains_f = norm_gains.astype(jnp.float32)
    classes_f = classes.astype(jnp.float32)
    class_count = classes.shape[0]
    mask_gain_f = mask_gain.astype(jnp.float32)
    steps = jnp.arange(row_count, dtype=jnp.int32)
    seg_query = segment_of(index * row_count + steps, seq_lengths)
    starts = jnp.stack([(index ^ r) * row_count for r in relative()])
    seg_rows = segment_of((starts[:, None] + steps[None, :]).reshape(-1), seq_lengths)
    class_slots = jnp.arange(CLASS_ROWS, dtype=jnp.int32)
    seg_key = jnp.concatenate([seg_rows, jnp.where(class_slots < class_count, -1, IMGS + 1)])
    feature_q, feature_k = features(seg_query, seg_key)
    enc_mask = (feature_q, feature_k[: seg_rows.shape[0]])
    dec_mask = (feature_q, feature_k)
    valid_rows = (seg_query < IMGS).astype(jnp.float32)[:, None]
    enc_normed = low(norm_rows(inputs_f, gains_f[0]))
    enc_rows = gather_rows(enc_normed)
    keyval, queries = project(enc_rows, row_count, w_first, 0)
    attended, attended_low, kept_q = attend(queries, keyval, *enc_mask)
    enc_attn = (keyval, attended, kept_q)
    enc_low = attended_low
    enc_middle, enc_second, enc_upward, enc_active, encoded, dec_normed = feed_forward(
        tokens[0], attended_low, gains_f[1], gains_f[2], w_middle, 8, w_middle
    )
    class_normed = low(norm_rows(classes_f, gains_f[2]))
    class_padded = jnp.pad(class_normed, ((0, CLASS_ROWS - class_count), (0, 0)))
    dec_rows = jnp.concatenate([gather_rows(dec_normed), class_padded], axis=0)
    keyval, queries = project(dec_rows, row_count, w_middle, 9)
    attended, dec_low, kept_q = attend(queries, keyval, *dec_mask)
    dec_attn = (keyval, attended, kept_q)
    gathered_last, dec_low = lax.optimization_barrier((gathered_last, dec_low))
    w_last = to_blocks(gathered_last, sizes_of(last_shards))
    dec_middle, dec_second, dec_upward, dec_active, decoded, final_normed = feed_forward(
        encoded, dec_low, gains_f[3], gains_f[4], w_middle, 12, w_last
    )
    w_patch, w_class = (
        jnp.concatenate([w_last[:, c, at : at + PIECE].reshape(D, WIDE) for c in range(2)], axis=1)
        for at in (2 * TALL, 2 * TALL + PIECE)
    )
    patch_rows = low(dot(final_normed, w_patch))
    class_rows = dot(classes, w_class)
    class_unit = low(unit_rows(class_rows))
    logits = dot_turned(patch_rows, class_unit)
    mask_out = class_norm(logits, mask_gain_f) * valid_rows
    _, head_back = jax.vjp(class_norm, logits, mask_gain_f)
    grad_logits, grad_mask_gain = head_back(mask_cot[0] * valid_rows)
    grad_logits_low = low(grad_logits)
    grad_patch_rows = low(dot(grad_logits_low, class_unit))
    grad_unit = dot_rows(grad_logits_low, patch_rows)
    grad_final = dot_turned(grad_patch_rows, w_patch)
    _, final_back = jax.vjp(norm_rows, decoded, gains_f[4])
    grad_decoded, grad_gain_last = final_back(grad_final)
    _, unit_back = jax.vjp(unit_rows, class_rows)
    grad_class_rows = low(unit_back(grad_unit)[0])
    grad_classes = dot_turned(grad_class_rows, w_class)
    grad_branch, grad_upward, grad_middle, grad_attn, grad_attended, grad_gain_three = feed_forward_back(
        grad_decoded, dec_upward, dec_middle, gains_f[3], w_middle, 12, w_last
    )
    pad_classes = ((0, CLASS_ROWS - class_count), (0, 0))
    dec_chunks = products(
        [
            (dec_active, [grad_branch]),
            (dec_second, [grad_upward]),
            (dec_low, [grad_attn]),
            (final_normed, [grad_patch_rows]),
            (jnp.pad(classes, pad_classes), [jnp.pad(grad_class_rows, pad_classes)]),
        ]
    )
    dec_chunks, grad_attended = lax.optimization_barrier((dec_chunks, grad_attended))
    dec_sum = scatter_sums(from_blocks(dec_chunks, [TALL] + 7 * [PIECE]))
    one, two = attention_backward(grad_attended, dec_attn, dec_mask, lambda v: v)
    near, far = rows_back(one, two, w_middle, 9)
    here, going = summed_rows(near, far)
    going, one, two = lax.optimization_barrier((going, one, two))
    coming = swap(going, seq_bits()[-1])
    dec_qkv_chunks = products(
        [(dec_normed, [one[0], two[0]]), (dec_rows, [one[1], two[1]]), (dec_rows, [one[2], two[2]])],
        core,
        first=9,
        pieces=12,
    )
    _, class_back = jax.vjp(norm_rows, classes_f, gains_f[2])
    grad_classes_kv, grad_gain_class = class_back(near[far.shape[0] : far.shape[0] + class_count])
    coming, dec_qkv_chunks = lax.optimization_barrier((coming, dec_qkv_chunks))
    back, gain_rows = norm_back(here + coming.astype(jnp.float32), encoded, gains_f[2])
    grad_encoded = back + grad_middle
    padded_mask_gain = jnp.pad(grad_mask_gain, (0, D - class_count))
    shared = jnp.concatenate(
        [
            grad_classes + grad_classes_kv,
            jnp.stack(
                [jnp.sum(gain_rows, axis=0) + grad_gain_class, grad_gain_three[0], grad_gain_last, padded_mask_gain]
            ),
        ],
        axis=0,
    )
    per_block = CLASS_ROWS // BLOCKS
    shared = low(jnp.pad(shared, ((0, CLASS_ROWS - shared.shape[0]), (0, 0))))
    shared = shared.reshape(BLOCKS, per_block, 2, WIDE).transpose(0, 2, 1, 3)
    grad_branch, grad_upward, grad_middle, grad_attn, grad_attended, grad_gain_one = feed_forward_back(
        grad_encoded, enc_upward, enc_middle, gains_f[1], w_middle, 8, w_middle
    )
    enc_chunks = products(
        [(enc_active, [grad_branch]), (enc_second, [grad_upward]), (enc_low, [grad_attn])],
        core,
        into=dec_qkv_chunks,
        pieces=12,
    )
    enc_chunks, grad_attended = lax.optimization_barrier((enc_chunks, grad_attended))
    enc_sum = Running(stepped_sums(*enc_chunks, [TALL] + 8 * [PIECE], 2))
    dec_sum = Running(waited(dec_sum))
    one, two = attention_backward(grad_attended, enc_attn, enc_mask, lambda v: tie(v, enc_sum))
    one, two = tie((one, two), dec_sum)
    here, going = summed_rows(*rows_back(one, two, w_first, 0))
    going, one, two = tie((going, one, two), enc_sum)
    coming = swap(going, seq_bits()[-1])
    enc_qkv_chunks = products(
        [(enc_normed, [one[0], two[0]]), (enc_rows, [one[1], two[1]]), (enc_rows, [one[2], two[2]])],
        core,
    )
    enc_qkv_chunks, coming, enc_sum.values = lax.optimization_barrier((enc_qkv_chunks, coming, enc_sum.values))
    enc_qkv_chunks = [
        jnp.concatenate([t, lax.dynamic_index_in_dim(shared, c, 1, keepdims=False)], axis=1)
        for t, c in zip(enc_qkv_chunks, (1 - core, core))
    ]
    enc_proj = Running(stepped_sums(*enc_qkv_chunks, 3 * [PIECE] + [per_block], 1))
    here, coming = tie((here, coming), enc_proj, enc_sum)
    back, gain_rows = norm_back(here + coming.astype(jnp.float32), inputs_f, gains_f[0])
    grad_inputs = back + grad_middle
    gain_rows, dec_sum = tie((gain_rows, dec_sum.finish()), enc_proj, enc_sum)
    late = Running(everywhere(jnp.stack([jnp.sum(gain_rows, axis=0), grad_gain_one[0]])))
    square, wide, tall = (D, D), (D, 4 * D), (4 * D, D)
    qkv = [square, square, square]
    (out_enc_qkv,), shares = collect(enc_proj.finish(), qkv, [0, 0, 0])
    shared = across([t[-(per_block * BLOCKS >> len(chip_bits())) :] for t in shares]).astype(jnp.float32)
    late = late.finish()
    out_dec, _ = collect(dec_sum, [tall, wide, square, square, square], range(5))
    out_enc, _ = collect(enc_sum.finish(), [tall, wide, square] + qkv, [0, 1, 2, 3, 3, 3])
    out_dec_qkv = out_enc[3]
    gain_sums = jnp.concatenate([late, shared[class_count : class_count + 3]], axis=0)
    return (
        mask_out[None],
        grad_inputs[None],
        shared[:class_count],
        gain_sums,
        shared[class_count + 3, :class_count],
        out_enc_qkv,
        out_enc[2],
        out_enc[1],
        out_enc[0],
        out_dec_qkv,
        out_dec[2],
        out_dec[1],
        out_dec[0],
        out_dec[3],
        out_dec[4],
    )


def solution(mesh):
    placed = (
        P("dp", "seq", None),
        P("dp", None),
        P(),
        P(),
        P(),
        P("dp", None),
        P("dp", None),
        P("dp", None),
        P("dp", None),
        P("dp", None),
        P("dp", None),
        P("dp", None),
        P("dp", None),
        P("dp", None),
        P("dp", None),
        P("dp", "seq", None),
    )
    return jax.shard_map(
        local,
        mesh=mesh,
        in_specs=placed,
        out_specs=(
            P("dp", "seq", None),
            P("dp", "seq", None),
            P(),
            P(),
            P(),
            P("dp", None),
            P("dp", None),
            P("dp", None),
            P("dp", None),
            P("dp", None),
            P("dp", None),
            P("dp", None),
            P("dp", None),
            P("dp", None),
            P("dp", None),
        ),
        check_vma=False,
    )
```

```python
import functools
import math

import jax
import jax.numpy as jnp
from jax import lax
from jax.experimental import pallas as pl
from jax.experimental.pallas import tpu as pltpu
from jax.sharding import PartitionSpec as P
HD=64
KB=256
LSE_LANE=10
NEG=-1e30
NT=(((1,),(1,)),((),()))
NN=(((1,),(0,)),((),()))

def split3(v):
    hi=v.astype(jnp.bfloat16).astype(jnp.float32)
    mid=(v-hi).astype(jnp.bfloat16).astype(jnp.float32)
    return hi,mid,v-hi-mid

def fwd_kernel(q_ref, k_ref, v_ref, fq_ref, fk_ref, o_ref, ol_ref, qa_ref):
    lane = lax.broadcasted_iota(jnp.int32, (1, 128), 1)
    low = lane < HD
    fk, k2, v2 = fk_ref[...], k_ref[...], v_ref[...]
    keys = (jnp.where(low, k2, fk), jnp.where(low, fk, k2))
    values = (jnp.where(low, v2, fk), jnp.where(low, fk, v2))
    size = q_ref.shape[0] // 2
    for t in range(2):
        r = slice(t * size, (t + 1) * size)
        q2, fq = q_ref[r] * jnp.bfloat16(0.125), fq_ref[r]
        outs = []
        for h, qs in enumerate((jnp.where(low, q2, fq), jnp.where(low, fq, q2))):
            s = lax.dot_general(qs, keys[h], NT, preferred_element_type=jnp.float32)
            top = jnp.max(s, axis=1, keepdims=True)
            p = jnp.exp(s - top).astype(jnp.bfloat16)
            acc = lax.dot_general(p, values[h], NN, preferred_element_type=jnp.float32)
            base = HD + LSE_LANE if h == 0 else LSE_LANE
            total = acc[:, base : base + 1]
            outs.append(acc / total)
            qa = qs.astype(jnp.float32)
            for j, x in enumerate(split3(-(top + jnp.log(total)))):
                qa = jnp.where(lane == base + j, x, qa)
            qa_ref[h, r] = qa.astype(jnp.bfloat16)
        o = jnp.where(low, outs[0], outs[1])
        o_ref[r] = o
        ol_ref[r] = o.astype(jnp.bfloat16)


def attend(q, kv, fq, fk, heads=12):
    rows, d = q.shape
    nk, pairs = kv.shape[0], heads // 2
    row = pl.BlockSpec((rows, 128), lambda p: (0, p))
    return pl.pallas_call(
        fwd_kernel,
        grid=(pairs,),
        in_specs=[
            row,
            pl.BlockSpec((nk, 128), lambda p: (0, p)),
            pl.BlockSpec((nk, 128), lambda p: (0, p + pairs)),
            pl.BlockSpec((rows, 128), lambda p: (0, 0)),
            pl.BlockSpec((nk, 128), lambda p: (0, 0)),
        ],
        out_specs=[row, row, pl.BlockSpec((2, rows, 128), lambda p: (p, 0, 0))],
        out_shape=[
            jax.ShapeDtypeStruct((rows, d), jnp.float32),
            jax.ShapeDtypeStruct((rows, d), jnp.bfloat16),
            jax.ShapeDtypeStruct((heads, rows, 128), jnp.bfloat16),
        ],
        compiler_params=pltpu.CompilerParams(vmem_limit_bytes=60 << 20),
        cost_estimate=pl.CostEstimate(flops=rows, bytes_accessed=rows, transcendentals=0),
        name="attend",
    )(q, kv, kv, fq, fk)


def bwd_kernel(qa_ref, k_ref, v_ref, fk_ref, g_ref, o_ref, dq_ref, dk_ref, dv_ref, ds_ref):
    nk = k_ref.shape[0]
    lane = lax.broadcasted_iota(jnp.int32, (1, 128), 1)
    low = lane < HD
    g = g_ref[...].astype(jnp.float32)
    prod = g * o_ref[...]
    gs = []
    for h in range(2):
        own = low if h == 0 else jnp.logical_not(low)
        base = HD + LSE_LANE if h == 0 else LSE_LANE
        delta = jnp.sum(jnp.where(own, prod, 0.0), axis=1, keepdims=True)
        ga = jnp.where(own, g, 0.0)
        for j, t in enumerate(split3(-delta)):
            ga = jnp.where(lane == base + j, t, ga)
        gs.append(ga.astype(jnp.bfloat16))
    for at in range(0, nk, 3 * KB):
        r = slice(at, min(at + 3 * KB, nk))
        k2, v2, fk = k_ref[r], v_ref[r], fk_ref[r]
        dks, dvs = [], []
        for h in range(2):
            ka = jnp.where(low, k2, fk) if h == 0 else jnp.where(low, fk, k2)
            va = jnp.where(low, v2, fk) if h == 0 else jnp.where(low, fk, v2)
            pt = jnp.exp(lax.dot_general(ka, qa_ref[h], NT, preferred_element_type=jnp.float32))
            dpt = lax.dot_general(va, gs[h], NT, preferred_element_type=jnp.float32)
            ds = (pt * dpt).astype(jnp.bfloat16)
            ds_ref[h, r] = ds
            dvs.append(lax.dot_general(pt.astype(jnp.bfloat16), gs[h], NN, preferred_element_type=jnp.float32))
            dks.append(lax.dot_general(ds, qa_ref[h], NN, preferred_element_type=jnp.float32))
        dk_ref[r] = jnp.where(low, dks[0], dks[1]).astype(dk_ref.dtype)
        dv_ref[r] = jnp.where(low, dvs[0], dvs[1]).astype(dv_ref.dtype)
    kt = k_ref[...].T
    dqs = [lax.dot_general(kt, ds_ref[h], NN, preferred_element_type=jnp.float32) for h in range(2)]
    top = lax.broadcasted_iota(jnp.int32, (128, 1), 0) < HD
    dq_ref[...] = (jnp.where(top, dqs[0], dqs[1]).T * 0.125).astype(dq_ref.dtype)


def attend_back(qa, kv, fk, g, o, first, count, heads=12):
    rows, nk, pairs = g.shape[0], kv.shape[0], heads // 2
    row = pl.BlockSpec((rows, 128), lambda p: (0, p + first))
    key = pl.BlockSpec((nk, 128), lambda p: (0, p))
    return pl.pallas_call(
        bwd_kernel,
        grid=(count,),
        in_specs=[
            pl.BlockSpec((2, rows, 128), lambda p: (p + first, 0, 0)),
            pl.BlockSpec((nk, 128), lambda p: (0, p + first)),
            pl.BlockSpec((nk, 128), lambda p: (0, p + first + pairs)),
            pl.BlockSpec((nk, 128), lambda p: (0, 0)),
            row,
            row,
        ],
        out_specs=[pl.BlockSpec((rows, 128), lambda p: (0, p)), key, key],
        out_shape=[jax.ShapeDtypeStruct((n, 128 * count), jnp.bfloat16) for n in (rows, nk, nk)],
        scratch_shapes=[pltpu.VMEM((2, nk, rows), jnp.bfloat16)],
        compiler_params=pltpu.CompilerParams(vmem_limit_bytes=60 << 20),
        cost_estimate=pl.CostEstimate(flops=rows, bytes_accessed=rows, transcendentals=0),
        name="attend_back",
    )(qa, kv, kv, fk, g, o)


def features(seg_query,seg_key):
    j=jnp.arange(128,dtype=jnp.int32)[None,:]%HD
    fq=jnp.where((j<10)&(j!=seg_query[:,None]),NEG,0.0).astype(jnp.bfloat16)
    fk=(((j<10)&(j==seg_key[:,None]))|((j>=LSE_LANE)&(j<LSE_LANE+3))).astype(jnp.bfloat16)
    return fq,fk


D = 768
HEADS = 12
IMGS = 8
CLASS_ROWS = 256
WIDE = 384


def norm_rows(values, gain_row):
    centre = values - jnp.mean(values, axis=-1, keepdims=True)
    return centre * lax.rsqrt(jnp.mean(centre * centre, axis=-1, keepdims=True) + 1e-06) * gain_row


def class_norm(logits, gain_row):
    centre = logits - jnp.mean(logits, axis=-1, keepdims=True)
    return centre * lax.rsqrt(jnp.mean(centre * centre, axis=-1, keepdims=True) + 1e-05) * gain_row


def unit_rows(values):
    return values * lax.rsqrt(jnp.sum(values * values, axis=-1, keepdims=True) + 1e-06)


def dot(left, right):
    return jnp.dot(left, right, preferred_element_type=jnp.float32)


def dot_rows(left, right):
    return lax.dot_general(left, right, (((0,), (0,)), ((), ())), preferred_element_type=jnp.float32)


def dot_turned(left, right):
    return lax.dot_general(left, right, (((1,), (1,)), ((), ())), preferred_element_type=jnp.float32)


def low(values):
    return values.astype(jnp.bfloat16)


BOTH = ("dp", "seq")


def bits_of(count):
    return [1 << i for i in range(count.bit_length() - 1)]


def seq_bits():
    return bits_of(lax.axis_size("seq"))


def chip_bits():
    return bits_of(lax.axis_size("seq") * lax.axis_size("dp"))[1:]


def swap(values, mask):
    inner, outer = lax.axis_size("seq"), lax.axis_size("dp")
    place = [(i % inner) * outer + i // inner for i in range(inner * outer)]
    pairs = [(place[i], place[i ^ mask]) for i in range(inner * outer)]
    return lax.ppermute(values, ("seq", "dp"), pairs)


def own_bit(bit):
    return (lax.axis_index(BOTH) // bit) % 2


def masks_of(bits):
    masks = [0]
    for bit in bits:
        masks = masks + [m | bit for m in masks]
    return masks


def groups_of(bits):
    return [bits[i : i + 2] for i in range(0, len(bits), 2)]


def absolute(pieces, bits):
    for i, bit in enumerate(bits):
        same = own_bit(bit) == 0
        pieces = [jnp.where(same, p, pieces[k ^ (1 << i)]) for k, p in enumerate(pieces)]
    return pieces


def gather_rows(rows):
    for bit in reversed(seq_bits()):
        rows = jnp.concatenate([rows, swap(rows, bit)], axis=0)
    return rows


def relative():
    return masks_of(seq_bits()[::-1])


def segment_of(places, seq_lengths):
    count = seq_lengths.shape[0]
    before = jnp.arange(count)[None, :] <= jnp.arange(count)[:, None]
    boundary = jnp.sum(jnp.where(before, seq_lengths[None, :], 0), axis=1)
    return jnp.sum((places[:, None] >= boundary[None, :]).astype(jnp.int32), axis=1)


def from_sequence(mine):
    bits = seq_bits()
    return absolute([mine if m == 0 else swap(mine, m) for m in masks_of(bits)], bits)


def halve(total, bit, near, done):
    low_bits = 1 if len(near) - done == 1 else 1 << near.index(bit)
    values = total.reshape((total.shape[0] // (2 * low_bits), 2, low_bits) + total.shape[1:])
    own = own_bit(bit)
    arrived = swap(lax.dynamic_index_in_dim(values, 1 - own, 1, keepdims=False), bit)
    kept = lax.dynamic_index_in_dim(values, own, 1, keepdims=False)
    result = low(kept.astype(jnp.float32) + arrived.astype(jnp.float32))
    return result.reshape((-1,) + total.shape[1:])


def share_low(total, group, width):
    values = total.reshape((total.shape[0] // width, width) + total.shape[1:])
    own = lax.axis_index(BOTH)
    pieces = []
    for m in masks_of(group):
        place = ((own ^ m) // group[0]) % width
        piece = lax.dynamic_index_in_dim(values, place, 1, keepdims=False)
        pieces.append(piece if m == 0 else swap(piece, m))
    return sum(p.astype(jnp.float32) for p in pieces).astype(total.dtype)


BLOCKS = 16
PIECE = 48
TALL = 192
TN = (((0,), (0,)), ((), ()))


def cheap(rows):
    return pl.CostEstimate(flops=rows, bytes_accessed=rows, transcendentals=0)


def dot_nn(left, right):
    return lax.dot_general(left, right, NN, preferred_element_type=jnp.float32)


def dot_nt(left, right):
    return lax.dot_general(left, right, NT, preferred_element_type=jnp.float32)


def mat(chunk):
    return chunk.reshape(-1, WIDE)


def columns(c):
    return slice(c * WIDE, (c + 1) * WIDE)


def joined(chunk):
    return jnp.concatenate([mat(chunk[:, 0]), mat(chunk[:, 1])], axis=1)


def gelu_parts(u):
    root = math.sqrt(2.0 / math.pi)
    t = jnp.tanh(root * (u + 0.044715 * (u * u * u)))
    return 0.5 * (1.0 + t), 0.5 * u * (1.0 - t * t) * (root * (1.0 + (3 * 0.044715) * (u * u)))


def qkv_kernel(rows_ref, w_ref, kv_ref, q_ref):
    step = pl.program_id(0)
    weight = joined(w_ref[...])

    @pl.when(step < 2)
    def _():
        kv_ref[...] = dot_nn(rows_ref[...], weight).astype(kv_ref.dtype)

    @pl.when(step == 2)
    def _():
        q_ref[...] = dot_nn(rows_ref[: q_ref.shape[0]], weight).astype(q_ref.dtype)


def project(rows_all, own, weights, first):
    count = rows_all.shape[0]
    return pl.pallas_call(
        qkv_kernel,
        grid=(3,),
        in_specs=[
            pl.BlockSpec((count, D), lambda t: (0, 0)),
            pl.BlockSpec((BLOCKS, 2, PIECE, WIDE), lambda t: (0, 0, jnp.where(t < 2, first + 1 + t, first), 0)),
        ],
        out_specs=[
            pl.BlockSpec((count, D), lambda t: (0, jnp.minimum(t, 1))),
            pl.BlockSpec((own, D), lambda t: (0, 0)),
        ],
        out_shape=[
            jax.ShapeDtypeStruct((count, 2 * D), jnp.bfloat16),
            jax.ShapeDtypeStruct((own, D), jnp.bfloat16),
        ],
        compiler_params=pltpu.CompilerParams(vmem_limit_bytes=60 << 20),
        cost_estimate=cheap(own),
        name="project",
    )(rows_all, weights)


def halves(ref):
    half = ref.shape[0] // 2
    return (slice(0, half), slice(half, 2 * half))


def mlp_kernel(h_ref, o_ref, gain_ref, next_ref, wo_ref, wu_ref, wd_ref, mid_ref, sec_ref, u_ref, act_ref, res_ref, nrm_ref):
    step = pl.program_id(0)

    @pl.when(step == 0)
    def _():
        middle = h_ref[...].astype(jnp.float32) + dot_nn(o_ref[...], joined(wo_ref[...]))
        mid_ref[...] = middle
        sec_ref[...] = norm_rows(middle, gain_ref[...]).astype(sec_ref.dtype)
        res_ref[...] = middle

    up = jnp.concatenate([mat(wu_ref[:, 0, :PIECE]), mat(wu_ref[:, 0, PIECE:])], axis=1)
    down = joined(wd_ref[...])
    for part in halves(sec_ref):
        u = dot_nn(sec_ref[part], up)
        u_ref[part] = u.astype(u_ref.dtype)
        active_part = (u * gelu_parts(u)[0]).astype(act_ref.dtype)
        act_ref[part] = active_part
        res_ref[part] += dot_nn(active_part, down)

    @pl.when(step == 3)
    def _():
        nrm_ref[...] = norm_rows(res_ref[...], next_ref[...]).astype(nrm_ref.dtype)


def mlp_specs(out_piece):
    return [
        pl.BlockSpec((BLOCKS, 2, PIECE, WIDE), lambda t: (0, 0, out_piece, 0)),
        pl.BlockSpec((BLOCKS, 1, 2 * PIECE, WIDE), lambda t: (0, t // 2, 2 + t % 2, 0)),
        pl.BlockSpec((BLOCKS // 4, 2, TALL, WIDE), lambda t: (t, 0, 0, 0)),
    ]


def whole(shape):
    return pl.BlockSpec(shape, lambda t: (0,) * len(shape))


def feed_forward(hidden, attended, gain, next_gain, w_out, out_piece, w_mlp):
    rows = hidden.shape[0]
    full, tile = (rows, D), pl.BlockSpec((rows, D), lambda t: (0, t))
    return pl.pallas_call(
        mlp_kernel,
        grid=(4,),
        in_specs=[whole(full), whole(full), whole((1, D)), whole((1, D)), *mlp_specs(out_piece)],
        out_specs=[whole(full), whole(full), tile, tile, whole(full), whole(full)],
        out_shape=[
            jax.ShapeDtypeStruct(full, jnp.float32),
            jax.ShapeDtypeStruct(full, jnp.bfloat16),
            jax.ShapeDtypeStruct((rows, 4 * D), jnp.bfloat16),
            jax.ShapeDtypeStruct((rows, 4 * D), jnp.bfloat16),
            jax.ShapeDtypeStruct(full, jnp.float32),
            jax.ShapeDtypeStruct(full, jnp.bfloat16),
        ],
        compiler_params=pltpu.CompilerParams(vmem_limit_bytes=60 << 20),
        cost_estimate=cheap(rows),
        name="feed_forward",
    )(hidden, attended, gain[None], next_gain[None], w_out, w_mlp, w_mlp)


def norm_back(grad, values, gain):
    centre = values - jnp.mean(values, axis=-1, keepdims=True)
    scale = lax.rsqrt(jnp.mean(centre * centre, axis=-1, keepdims=True) + 1e-06)
    unit = centre * scale
    inner = grad * gain
    inner = inner - jnp.mean(inner, axis=-1, keepdims=True) - unit * jnp.mean(inner * unit, axis=-1, keepdims=True)
    return inner * scale, grad * unit


def mlp_back_kernel(g_ref, u_ref, mid_ref, gain_ref, wo_ref, wu_ref, wd_ref, gb_ref, gu_ref, gm_ref, ga_ref, gat_ref, gg_ref, acc):
    step = pl.program_id(0)

    @pl.when(step == 0)
    def _():
        gb_ref[...] = g_ref[...].astype(gb_ref.dtype)
        acc[...] = jnp.zeros(acc.shape, jnp.float32)

    up = jnp.concatenate([mat(wu_ref[:, 0, :PIECE]), mat(wu_ref[:, 0, PIECE:])], axis=1)
    down = joined(wd_ref[...])
    for part in halves(gb_ref):
        grad = dot_nt(gb_ref[part], down)
        gu = (grad * sum(gelu_parts(u_ref[part].astype(jnp.float32)))).astype(gu_ref.dtype)
        gu_ref[part] = gu
        acc[part] += dot_nt(gu, up)

    @pl.when(step == 3)
    def _():
        back, gain_rows = norm_back(acc[...], mid_ref[...], gain_ref[...])
        middle = back + g_ref[...]
        gm_ref[...] = middle
        gg_ref[...] = jnp.sum(gain_rows, axis=0, keepdims=True)
        low_middle = middle.astype(ga_ref.dtype)
        ga_ref[...] = low_middle
        gat_ref[...] = dot_nt(low_middle, joined(wo_ref[...])).astype(gat_ref.dtype)


def feed_forward_back(grad, upward, middle, gain, w_out, out_piece, w_mlp):
    rows = grad.shape[0]
    full, tile = (rows, D), pl.BlockSpec((rows, D), lambda t: (0, t))
    return pl.pallas_call(
        mlp_back_kernel,
        grid=(4,),
        in_specs=[whole(full), tile, whole(full), whole((1, D)), *mlp_specs(out_piece)],
        out_specs=[whole(full), tile, whole(full), whole(full), whole(full), whole((1, D))],
        out_shape=[
            jax.ShapeDtypeStruct(full, jnp.bfloat16),
            jax.ShapeDtypeStruct((rows, 4 * D), jnp.bfloat16),
            jax.ShapeDtypeStruct(full, jnp.float32),
            jax.ShapeDtypeStruct(full, jnp.bfloat16),
            jax.ShapeDtypeStruct(full, jnp.bfloat16),
            jax.ShapeDtypeStruct((1, D), jnp.float32),
        ],
        scratch_shapes=[pltpu.VMEM(full, jnp.float32)],
        compiler_params=pltpu.CompilerParams(vmem_limit_bytes=60 << 20),
        cost_estimate=cheap(rows),
        name="feed_forward_back",
    )(grad, upward, middle, gain[None], w_out, w_mlp, w_mlp)


def rows_back_kernel(steps, half, dk0, dk1, dv0, dv1, dq0, dq1, wq_ref, wk_ref, wv_ref, near_ref, far_ref, full):
    step = pl.program_id(0)

    @pl.when(step == 0)
    def _():
        full[:, :D] = joined(wk_ref[...])
        full[:, D:] = joined(wv_ref[...])

    rows = jnp.concatenate([dk0[...], dk1[...], dv0[...], dv1[...]], axis=1)
    total = dot_nt(rows, full[...])
    away = (step >= half) & (step < 2 * half)

    @pl.when(away)
    def _():
        far_ref[...] = total.astype(far_ref.dtype)

    @pl.when(jnp.logical_not(away))
    def _():
        near_ref[...] = total

    @pl.when(step < steps)
    def _():
        near_ref[...] += dot_nt(jnp.concatenate([dq0[...], dq1[...]], axis=1), joined(wq_ref[...]))


def rows_back(one, two, weights, first):
    count, size = one[1].shape[0], one[0].shape[0]
    tokens = count // size * size
    if count != tokens:
        size = math.gcd(count, size)
    steps, half = one[0].shape[0] // size, tokens // (2 * size)
    tile = pl.BlockSpec((size, WIDE), lambda t: (t, 0))
    query = pl.BlockSpec((size, WIDE), lambda t: (jnp.minimum(t, steps - 1), 0))
    piece = lambda i: pl.BlockSpec((BLOCKS, 2, PIECE, WIDE), lambda t: (0, 0, first + i, 0))
    near = lambda t: (jnp.where(t < half, t, jnp.where(t < 2 * half, half, t - half)), 0)
    far = lambda t: (jnp.clip(t - half, 0, half - 1), 0)
    rest = count - half * size
    spare = rest + size if count == tokens else rest
    return pl.pallas_call(
        functools.partial(rows_back_kernel, steps, half),
        grid=(count // size,),
        in_specs=[tile, tile, tile, tile, query, query, piece(0), piece(1), piece(2)],
        out_specs=[pl.BlockSpec((size, D), near), pl.BlockSpec((size, D), far)],
        out_shape=[
            jax.ShapeDtypeStruct((spare, D), jnp.float32),
            jax.ShapeDtypeStruct((half * size, D), jnp.bfloat16),
        ],
        scratch_shapes=[pltpu.VMEM((D, 2 * D), jnp.bfloat16)],
        compiler_params=pltpu.CompilerParams(vmem_limit_bytes=60 << 20),
        cost_estimate=cheap(size),
        name="rows_back",
    )(one[1], two[1], one[2], two[2], one[0], two[0], weights, weights, weights)


def products_kernel(plan, count_in, outs, *refs):
    ins, turned = refs[outs - 1 : outs - 1 + count_in], refs[-1]
    out_refs = refs[-1 - outs : -1]
    step = pl.program_id(0)
    for left, rights, begin, tiles, tall in plan:
        count = ins[left].shape[0]

        @pl.when(step == begin)
        def _():
            for i in range(0, ins[left].shape[1], D):
                part = ins[left][:, i : i + D].T
                if tall:
                    turned[i // TALL : (i + D) // TALL, :, :count] = part.reshape(D // TALL, TALL, count)
                else:
                    turned[:, :PIECE, :count] = part.reshape(BLOCKS, PIECE, count)

        @pl.when((step >= begin) & (step < begin + tiles))
        def _():
            n = step - begin
            if tall:
                at = pl.multiple_of(n * PIECE, PIECE)
                rows = turned[:, pl.ds(at, PIECE), :count].reshape(D, count)
            else:
                rows = turned[:, :PIECE, :count].reshape(D, count)
            if len(rights) == 2:
                right = jnp.concatenate([ins[r][...] for r in rights], axis=1)
            elif tall or tiles == 1:
                right = ins[rights[0]][...]
            else:
                half = tiles * WIDE
                parts = [
                    ins[rights[0]][:, pl.ds(pl.multiple_of(n * WIDE + c * half, WIDE), WIDE)] for c in range(2)
                ]
                right = jnp.concatenate(parts, axis=1)
            part = dot_nn(rows, right).astype(jnp.bfloat16)
            chunk = [part[:, columns(c)].reshape(BLOCKS, PIECE, WIDE) for c in range(2)]
            if outs == 1:
                for c in range(2):
                    out_refs[0][:, c] = chunk[c]
            else:
                for core in range(2):

                    @pl.when(refs[0][0] == core)
                    def _():
                        out_refs[0][...] = chunk[1 - core]
                        out_refs[1][...] = chunk[core]


def products(wanted, core=None, into=(), first=0, pieces=None):
    arrays, plan, steps = [], [], 0

    def place(array):
        for i, known in enumerate(arrays):
            if known is array:
                return i
        arrays.append(array)
        return len(arrays) - 1

    for left, rights in wanted:
        tall = left.shape[1] != D
        tiles = left.shape[1] // D if tall else sum(r.shape[1] for r in rights) // D
        plan.append((place(left), [place(r) for r in rights], steps, tiles, tall))
        steps += tiles
    longest = max(left.shape[0] for left, _ in wanted)
    height = TALL if any(p[4] for p in plan) else PIECE
    rows = (pieces or steps) * PIECE
    outs = 1 if core is None else 2
    if core is None:
        block, shape = (BLOCKS, 2, PIECE, WIDE), (BLOCKS, 2, rows, WIDE)
        where = lambda t: (0, 0, first + t, 0)
    else:
        block, shape = (BLOCKS, PIECE, WIDE), (BLOCKS, rows, WIDE)
        where = lambda t, _: (0, first + t, 0)
    spec = pltpu.PrefetchScalarGridSpec(
        num_scalar_prefetch=outs - 1,
        grid=(steps,),
        in_specs=[pl.BlockSpec(a.shape, lambda t, *_: (0, 0), pipeline_mode=pl.Buffered(1)) for a in arrays]
        + [pl.BlockSpec(memory_space=pl.ANY)] * len(into),
        out_specs=[pl.BlockSpec(block, where)] * outs,
        scratch_shapes=[pltpu.VMEM((BLOCKS, height, longest), jnp.bfloat16)],
    )
    result = pl.pallas_call(
        functools.partial(products_kernel, plan, len(arrays), outs),
        grid_spec=spec,
        out_shape=[jax.ShapeDtypeStruct(shape, jnp.bfloat16)] * outs,
        input_output_aliases={outs - 1 + len(arrays) + i: i for i in range(len(into))},
        compiler_params=pltpu.CompilerParams(vmem_limit_bytes=60 << 20),
        cost_estimate=cheap(longest),
        name="products",
    )(*([] if core is None else [core.reshape(1)]), *arrays, *into)
    return result[0] if core is None else result


def to_blocks(gathered, sizes):
    places = gathered.shape[0] // 2
    chunks = gathered.reshape(places, 2, -1, WIDE)
    if places == BLOCKS:
        return chunks
    pieces, at = [], 0
    for size in sizes:
        rows = size * BLOCKS // places
        part = chunks[:, :, at : at + rows].reshape(BLOCKS, -1, 2, rows, WIDE)
        pieces.append(part.transpose(0, 2, 1, 3, 4).reshape(BLOCKS, 2, size, WIDE))
        at += rows
    return jnp.concatenate(pieces, axis=2)


def from_blocks(chunks, sizes):
    places = 1 << len(chip_bits())
    if places == BLOCKS:
        return chunks
    pieces, at = [], 0
    for size in sizes:
        rows = size * BLOCKS // places
        part = chunks[:, :, at : at + size].reshape(BLOCKS, 2, -1, rows, WIDE)
        pieces.append(part.transpose(0, 2, 1, 3, 4).reshape(places, 2, rows, WIDE))
        at += size
    return jnp.concatenate(pieces, axis=2)


def bundle(shards):
    chips, index = lax.axis_size("seq") // 2, lax.axis_index("seq")
    pieces = []
    for shard in shards:
        rows, half = shard.shape[0] // chips, shard.shape[1] // 2
        part = lax.dynamic_slice(shard, (index // 2 * rows, index % 2 * half), (rows, half))
        pieces += [part[:, i : i + WIDE] for i in range(0, half, WIDE)]
    return jnp.concatenate(pieces, axis=0)


def sizes_of(shards):
    tall = lambda s: s.shape[0] * lax.axis_size("dp") // BLOCKS
    return [tall(s) for s in shards for _ in range(0, s.shape[1] // 2, WIDE)]


def thirds_of(shard):
    return [shard[:, i : i + D] for i in range(0, 3 * D, D)]


def gather_weights(shards):
    return lax.all_gather(bundle(shards), BOTH, axis=0)


def gather_first(shards, after):
    values = bundle(shards)
    rows = values.shape[0]
    values = values[None]
    for step, group in enumerate(reversed(groups_of(chip_bits()))):
        pieces = [values if m == 0 else swap(values, m) for m in masks_of(group)]
        if step == 0:
            pieces, after = lax.optimization_barrier((pieces, after))
        values = jnp.stack(absolute(pieces, group), axis=1).reshape(-1, rows, WIDE)
    values = jnp.stack(absolute([values, swap(values, 1)], [1]), axis=1)
    return to_blocks(values.reshape(-1, rows, WIDE), sizes_of(shards)), after


def collect_kernel(plan, own_ref, *refs):
    count = len(refs) - len({p[3] for p in plan})
    ins, outs = refs[:count], refs[count:]
    for own in range(count):

        @pl.when(own_ref[0] == own)
        def _():
            for device in range(count):
                y, core = device // 2, device % 2
                for half, at, rows, out, column in plan:
                    if half == core:
                        part = ins[device ^ own][at : at + rows].astype(jnp.float32)
                        outs[out][y * rows : (y + 1) * rows, column : column + WIDE] = part


def collect(mine, wanted, outs):
    bits = seq_bits()
    held = {0: mine}
    for bit in reversed(bits):
        held.update({m | bit: swap(t, bit) for m, t in list(held.items())})
    pieces = [held[m] for m in masks_of(bits)]
    places = 1 << len(chip_bits())
    plan, shapes, at = [], {}, 0
    for (height, width), out in zip(wanted, outs):
        rows, half = height // places, width // 2
        begin = shapes.get(out, (0, 0))[1]
        for i in range(0, half, WIDE):
            plan += [(core, at, rows, out, begin + core * half + i) for core in range(2)]
            at += rows
        shapes[out] = (height // lax.axis_size("dp"), begin + width)
    if any(p[2] % 16 for p in plan):
        shares = absolute(pieces, bits)
        results = [jnp.zeros(shape, jnp.float32) for shape in shapes.values()]
        for core, at, rows, out, column in plan:
            for y, share in enumerate(shares[core::2]):
                part = share[at : at + rows].astype(jnp.float32)
                results[out] = results[out].at[y * rows : (y + 1) * rows, column : column + WIDE].set(part)
        return results, pieces
    spec = pltpu.PrefetchScalarGridSpec(
        num_scalar_prefetch=1,
        grid=(1,),
        in_specs=[pl.BlockSpec(mine.shape, lambda t, own: (0, 0)) for _ in pieces],
        out_specs=[pl.BlockSpec(shape, lambda t, own: (0, 0)) for shape in shapes.values()],
    )
    results = pl.pallas_call(
        functools.partial(collect_kernel, plan),
        grid_spec=spec,
        out_shape=[jax.ShapeDtypeStruct(shape, jnp.float32) for shape in shapes.values()],
        compiler_params=pltpu.CompilerParams(vmem_limit_bytes=40 << 20),
        cost_estimate=cheap(D),
        name="collect",
    )(lax.axis_index("seq").reshape(1), *pieces)
    return results, pieces


def across(pieces):
    shares = absolute(pieces, seq_bits())
    rows = jnp.concatenate([jnp.concatenate(shares[i : i + 2], axis=1) for i in range(0, len(shares), 2)], axis=0)
    total = rows[None]
    for group in groups_of(chip_bits()[len(seq_bits()) - 1 :]):
        total = jnp.stack(absolute([total if m == 0 else swap(total, m) for m in masks_of(group)], group), axis=0)
        total = total.reshape((-1,) + rows.shape)
    return total.reshape(-1, rows.shape[1])


def scatter_sums(chunks):
    return lax.psum_scatter(chunks.reshape((-1,) + chunks.shape[2:]), BOTH, scatter_dimension=0)


def add_and_part_kernel(cut, own_ref, keep_ref, arrived_ref, *outs):
    def total(index, rows):
        return (keep_ref[index, rows].astype(jnp.float32) + arrived_ref[index, rows].astype(jnp.float32)).astype(jnp.bfloat16)

    first, second = slice(0, cut), slice(cut, None)
    y, x = own_ref[0], own_ref[1]
    for i in range(2):
        outs[0][i] = total(2 * i + 1 - y, first)
        outs[1][i] = total(2 * i + y, first)
        outs[2][i] = total(2 - 2 * x + i, second)
        outs[3][i] = total(2 * x + i, second)


def add_and_part(keep, arrived, cut):
    places, rows, _ = keep.shape
    bits = chip_bits()
    four = pl.BlockSpec((4, rows, WIDE), lambda t, _: (t, 0, 0))
    heights = (cut, cut, rows - cut, rows - cut)
    spec = pltpu.PrefetchScalarGridSpec(
        num_scalar_prefetch=1,
        grid=(places // 4,),
        in_specs=[four, four],
        out_specs=[pl.BlockSpec((2, h, WIDE), lambda t, _: (t, 0, 0)) for h in heights],
    )
    return pl.pallas_call(
        functools.partial(add_and_part_kernel, cut),
        grid_spec=spec,
        out_shape=[jax.ShapeDtypeStruct((places // 2, h, WIDE), jnp.bfloat16) for h in heights],
        compiler_params=pltpu.CompilerParams(vmem_limit_bytes=40 << 20),
        cost_estimate=cheap(D),
        name="add_and_part",
    )(jnp.stack([own_bit(bits[0]), own_bit(bits[1])]), keep, arrived)


def add_and_halve_kernel(own_ref, keep_ref, arrived_ref, going_ref, kept_ref):
    own = own_ref[0]
    for ref, index in ((going_ref, 1 - own), (kept_ref, own)):
        ref[0] = (keep_ref[index].astype(jnp.float32) + arrived_ref[index].astype(jnp.float32)).astype(jnp.bfloat16)


def add_and_halve(keep, arrived, own):
    places, rows, _ = keep.shape
    pair = pl.BlockSpec((2, rows, WIDE), lambda t, _: (t, 0, 0))
    one = pl.BlockSpec((1, rows, WIDE), lambda t, _: (t, 0, 0))
    spec = pltpu.PrefetchScalarGridSpec(
        num_scalar_prefetch=1, grid=(places // 2,), in_specs=[pair, pair], out_specs=[one, one]
    )
    return pl.pallas_call(
        add_and_halve_kernel,
        grid_spec=spec,
        out_shape=[jax.ShapeDtypeStruct((places // 2, rows, WIDE), jnp.bfloat16)] * 2,
        compiler_params=pltpu.CompilerParams(vmem_limit_bytes=40 << 20),
        cost_estimate=cheap(D),
        name="add_and_halve",
    )(own.reshape(1), keep, arrived)


def stepped_sums(send, keep, sizes, classes):
    if classes == 2 and 1 << len(chip_bits()) == BLOCKS:
        bits = chip_bits()
        cut = keep.shape[1] // 2
        parts = yield add_and_part(keep, swap(send, 1), cut)
        ways = (bits[0], bits[1])
        parts = yield [
            part
            for way, other, (going, kept) in zip(ways, ways[::-1], (parts[:2], parts[2:]))
            for part in add_and_halve(kept, swap(going, way), own_bit(other))
        ]
        total = [
            low(kept.astype(jnp.float32) + swap(going, way).astype(jnp.float32))
            for way, (going, kept) in zip(ways[::-1], (parts[:2], parts[2:]))
        ]
        total = (yield [jnp.concatenate(total, axis=1)])[0]
        for group in groups_of(bits[2:]):
            total = (yield [share_low(total, group, 1 << len(group))])[0]
        return total[0]
    if 1 << len(chip_bits()) != BLOCKS:
        chunks = from_blocks(jnp.stack([send, keep], axis=1), sizes)
        send, keep = chunks[:, 0], chunks[:, 1]
    arrived = swap(send, 1)
    total = low(keep.astype(jnp.float32) + arrived.astype(jnp.float32))
    bits = chip_bits()
    if classes == 2:
        near, bits = bits[:2], bits[2:]
        cut = total.shape[1] // 2
        parts = yield [total[:, :cut], total[:, cut:]]
        for i in range(2):
            parts = yield [halve(t, bit, near, i) for t, bit in zip(parts, (near[i], near[1 - i]))]
        total = jnp.concatenate(parts, axis=1)
    else:
        total = (yield [total])[0]
    for group in groups_of(bits):
        total = (yield [share_low(total, group, 1 << len(group))])[0]
    return total[0]


def everywhere(values):
    for group in groups_of([1] + chip_bits()):
        values = sum(values if m == 0 else swap(values, m) for m in masks_of(group))
        values = (yield [values])[0]
    return values


def waited(values):
    return (yield [values])[0]


class Running:
    def __init__(self, steps):
        self.steps, self.values, self.result = steps, None, None
        self.go(None)

    def go(self, values):
        try:
            self.values = self.steps.send(values)
        except StopIteration as end:
            self.values, self.result = [], end.value

    def finish(self):
        while self.result is None:
            self.go(self.values)
        return self.result


def tie(values, *running):
    values, held = lax.optimization_barrier((values, [r.values for r in running]))
    for r, h in zip(running, held):
        if r.result is None:
            r.go(h)
    return values


def attention_backward(grad_attended, kept, mask, between):
    feature_k = mask[1]
    keyval, attended, kept_q = kept
    pairs = HEADS // 2
    cut = pairs // 2
    one = attend_back(kept_q, keyval, feature_k, grad_attended, attended, 0, cut)
    one, grad_attended = between((one, grad_attended))
    two = attend_back(kept_q, keyval, feature_k, grad_attended, attended, cut, pairs - cut)
    return one, two


def summed_rows(near, far):
    rows = near[: far.shape[0]] + swap(far, 1).astype(jnp.float32)
    for bit in seq_bits()[1:-1]:
        half = rows.shape[0] // 2
        rows = rows[:half] + swap(low(rows[half:]), bit).astype(jnp.float32)
    half = rows.shape[0] // 2
    return rows[:half], low(rows[half:])


def local(
    tokens,
    lengths,
    classes,
    norm_gains,
    mask_gain,
    enc_qkv,
    enc_out,
    enc_up,
    enc_down,
    dec_qkv,
    dec_out,
    dec_up,
    dec_down,
    patch_proj,
    class_proj,
    mask_cot,
):
    w_first, (tokens, lengths) = gather_first(thirds_of(enc_qkv), (tokens, lengths))
    middle_shards = (enc_down, enc_up, enc_out, *thirds_of(dec_qkv), dec_out)
    last_shards = (dec_down, dec_up, patch_proj, class_proj)
    w_middle = to_blocks(gather_weights(middle_shards), sizes_of(middle_shards))
    gathered_last = gather_weights(last_shards)
    core = own_bit(1)
    row_count = tokens.shape[1]
    index = lax.axis_index("seq")
    seq_lengths = lengths[0]
    inputs_f = tokens[0].astype(jnp.float32)
    gains_f = norm_gains.astype(jnp.float32)
    classes_f = classes.astype(jnp.float32)
    class_count = classes.shape[0]
    mask_gain_f = mask_gain.astype(jnp.float32)
    steps = jnp.arange(row_count, dtype=jnp.int32)
    seg_query = segment_of(index * row_count + steps, seq_lengths)
    starts = jnp.stack([(index ^ r) * row_count for r in relative()])
    seg_rows = segment_of((starts[:, None] + steps[None, :]).reshape(-1), seq_lengths)
    class_slots = jnp.arange(CLASS_ROWS, dtype=jnp.int32)
    seg_key = jnp.concatenate([seg_rows, jnp.where(class_slots < class_count, -1, IMGS + 1)])
    feature_q, feature_k = features(seg_query, seg_key)
    enc_mask = (feature_q, feature_k[: seg_rows.shape[0]])
    dec_mask = (feature_q, feature_k)
    valid_rows = (seg_query < IMGS).astype(jnp.float32)[:, None]
    enc_normed = low(norm_rows(inputs_f, gains_f[0]))
    enc_rows = gather_rows(enc_normed)
    keyval, queries = project(enc_rows, row_count, w_first, 0)
    attended, attended_low, kept_q = attend(queries, keyval, *enc_mask)
    enc_attn = (keyval, attended, kept_q)
    enc_low = attended_low
    enc_middle, enc_second, enc_upward, enc_active, encoded, dec_normed = feed_forward(
        tokens[0], attended_low, gains_f[1], gains_f[2], w_middle, 8, w_middle
    )
    class_normed = low(norm_rows(classes_f, gains_f[2]))
    class_padded = jnp.pad(class_normed, ((0, CLASS_ROWS - class_count), (0, 0)))
    dec_rows = jnp.concatenate([gather_rows(dec_normed), class_padded], axis=0)
    keyval, queries = project(dec_rows, row_count, w_middle, 9)
    attended, dec_low, kept_q = attend(queries, keyval, *dec_mask)
    dec_attn = (keyval, attended, kept_q)
    gathered_last, dec_low = lax.optimization_barrier((gathered_last, dec_low))
    w_last = to_blocks(gathered_last, sizes_of(last_shards))
    dec_middle, dec_second, dec_upward, dec_active, decoded, final_normed = feed_forward(
        encoded, dec_low, gains_f[3], gains_f[4], w_middle, 12, w_last
    )
    w_patch, w_class = (
        jnp.concatenate([w_last[:, c, at : at + PIECE].reshape(D, WIDE) for c in range(2)], axis=1)
        for at in (2 * TALL, 2 * TALL + PIECE)
    )
    patch_rows = low(dot(final_normed, w_patch))
    class_rows = dot(classes, w_class)
    class_unit = low(unit_rows(class_rows))
    logits = dot_turned(patch_rows, class_unit)
    mask_out = class_norm(logits, mask_gain_f) * valid_rows
    _, head_back = jax.vjp(class_norm, logits, mask_gain_f)
    grad_logits, grad_mask_gain = head_back(mask_cot[0] * valid_rows)
    grad_logits_low = low(grad_logits)
    grad_patch_rows = low(dot(grad_logits_low, class_unit))
    grad_unit = dot_rows(grad_logits_low, patch_rows)
    grad_final = dot_turned(grad_patch_rows, w_patch)
    _, final_back = jax.vjp(norm_rows, decoded, gains_f[4])
    grad_decoded, grad_gain_last = final_back(grad_final)
    _, unit_back = jax.vjp(unit_rows, class_rows)
    grad_class_rows = low(unit_back(grad_unit)[0])
    grad_classes = dot_turned(grad_class_rows, w_class)
    grad_branch, grad_upward, grad_middle, grad_attn, grad_attended, grad_gain_three = feed_forward_back(
        grad_decoded, dec_upward, dec_middle, gains_f[3], w_middle, 12, w_last
    )
    pad_classes = ((0, CLASS_ROWS - class_count), (0, 0))
    dec_chunks = products(
        [
            (dec_active, [grad_branch]),
            (dec_second, [grad_upward]),
            (dec_low, [grad_attn]),
            (final_normed, [grad_patch_rows]),
            (jnp.pad(classes, pad_classes), [jnp.pad(grad_class_rows, pad_classes)]),
        ]
    )
    dec_chunks, grad_attended = lax.optimization_barrier((dec_chunks, grad_attended))
    dec_sum = scatter_sums(from_blocks(dec_chunks, [TALL] + 7 * [PIECE]))
    one, two = attention_backward(grad_attended, dec_attn, dec_mask, lambda v: v)
    near, far = rows_back(one, two, w_middle, 9)
    here, going = summed_rows(near, far)
    going, one, two = lax.optimization_barrier((going, one, two))
    coming = swap(going, seq_bits()[-1])
    dec_qkv_chunks = products(
        [(dec_normed, [one[0], two[0]]), (dec_rows, [one[1], two[1]]), (dec_rows, [one[2], two[2]])],
        core,
        first=9,
        pieces=12,
    )
    _, class_back = jax.vjp(norm_rows, classes_f, gains_f[2])
    grad_classes_kv, grad_gain_class = class_back(near[far.shape[0] : far.shape[0] + class_count])
    coming, dec_qkv_chunks = lax.optimization_barrier((coming, dec_qkv_chunks))
    back, gain_rows = norm_back(here + coming.astype(jnp.float32), encoded, gains_f[2])
    grad_encoded = back + grad_middle
    padded_mask_gain = jnp.pad(grad_mask_gain, (0, D - class_count))
    shared = jnp.concatenate(
        [
            grad_classes + grad_classes_kv,
            jnp.stack(
                [jnp.sum(gain_rows, axis=0) + grad_gain_class, grad_gain_three[0], grad_gain_last, padded_mask_gain]
            ),
        ],
        axis=0,
    )
    per_block = CLASS_ROWS // BLOCKS
    shared = low(jnp.pad(shared, ((0, CLASS_ROWS - shared.shape[0]), (0, 0))))
    shared = shared.reshape(BLOCKS, per_block, 2, WIDE).transpose(0, 2, 1, 3)
    grad_branch, grad_upward, grad_middle, grad_attn, grad_attended, grad_gain_one = feed_forward_back(
        grad_encoded, enc_upward, enc_middle, gains_f[1], w_middle, 8, w_middle
    )
    enc_chunks = products(
        [(enc_active, [grad_branch]), (enc_second, [grad_upward]), (enc_low, [grad_attn])],
        core,
        into=dec_qkv_chunks,
        pieces=12,
    )
    enc_chunks, grad_attended = lax.optimization_barrier((enc_chunks, grad_attended))
    enc_sum = Running(stepped_sums(*enc_chunks, [TALL] + 8 * [PIECE], 2))
    dec_sum = Running(waited(dec_sum))
    one, two = attention_backward(grad_attended, enc_attn, enc_mask, lambda v: tie(v, enc_sum))
    one, two = tie((one, two), dec_sum)
    here, going = summed_rows(*rows_back(one, two, w_first, 0))
    going, one, two = tie((going, one, two), enc_sum)
    coming = swap(going, seq_bits()[-1])
    enc_qkv_chunks = products(
        [(enc_normed, [one[0], two[0]]), (enc_rows, [one[1], two[1]]), (enc_rows, [one[2], two[2]])],
        core,
    )
    enc_qkv_chunks, coming, enc_sum.values = lax.optimization_barrier((enc_qkv_chunks, coming, enc_sum.values))
    enc_qkv_chunks = [
        jnp.concatenate([t, lax.dynamic_index_in_dim(shared, c, 1, keepdims=False)], axis=1)
        for t, c in zip(enc_qkv_chunks, (1 - core, core))
    ]
    enc_proj = Running(stepped_sums(*enc_qkv_chunks, 3 * [PIECE] + [per_block], 1))
    here, coming = tie((here, coming), enc_proj, enc_sum)
    back, gain_rows = norm_back(here + coming.astype(jnp.float32), inputs_f, gains_f[0])
    grad_inputs = back + grad_middle
    gain_rows, dec_sum = tie((gain_rows, dec_sum.finish()), enc_proj, enc_sum)
    late = Running(everywhere(jnp.stack([jnp.sum(gain_rows, axis=0), grad_gain_one[0]])))
    square, wide, tall = (D, D), (D, 4 * D), (4 * D, D)
    qkv = [square, square, square]
    (out_enc_qkv,), shares = collect(enc_proj.finish(), qkv, [0, 0, 0])
    shared = across([t[-(per_block * BLOCKS >> len(chip_bits())) :] for t in shares]).astype(jnp.float32)
    late = late.finish()
    out_dec, _ = collect(dec_sum, [tall, wide, square, square, square], range(5))
    out_enc, _ = collect(enc_sum.finish(), [tall, wide, square] + qkv, [0, 1, 2, 3, 3, 3])
    out_dec_qkv = out_enc[3]
    gain_sums = jnp.concatenate([late, shared[class_count : class_count + 3]], axis=0)
    return (
        mask_out[None],
        grad_inputs[None],
        shared[:class_count],
        gain_sums,
        shared[class_count + 3, :class_count],
        out_enc_qkv,
        out_enc[2],
        out_enc[1],
        out_enc[0],
        out_dec_qkv,
        out_dec[2],
        out_dec[1],
        out_dec[0],
        out_dec[3],
        out_dec[4],
    )


def solution(mesh):
    placed = (
        P("dp", "seq", None),
        P("dp", None),
        P(),
        P(),
        P(),
        P("dp", None),
        P("dp", None),
        P("dp", None),
        P("dp", None),
        P("dp", None),
        P("dp", None),
        P("dp", None),
        P("dp", None),
        P("dp", None),
        P("dp", None),
        P("dp", "seq", None),
    )
    return jax.shard_map(
        local,
        mesh=mesh,
        in_specs=placed,
        out_specs=(
            P("dp", "seq", None),
            P("dp", "seq", None),
            P(),
            P(),
            P(),
            P("dp", None),
            P("dp", None),
            P("dp", None),
            P("dp", None),
            P("dp", None),
            P("dp", None),
            P("dp", None),
            P("dp", None),
            P("dp", None),
            P("dp", None),
        ),
        check_vma=False,
    )
```

```python
import functools
import math

import jax
import jax.numpy as jnp
from jax import lax
from jax.experimental import pallas as pl
from jax.experimental.pallas import tpu as pltpu
from jax.sharding import PartitionSpec as P
HD=64
KB=256
LSE_LANE=10
NEG=-1e30
NT=(((1,),(1,)),((),()))
NN=(((1,),(0,)),((),()))

def split3(v):
    hi=v.astype(jnp.bfloat16).astype(jnp.float32)
    mid=(v-hi).astype(jnp.bfloat16).astype(jnp.float32)
    return hi,mid,v-hi-mid

def fwd_kernel(q_ref, k_ref, v_ref, fq_ref, fk_ref, o_ref, ol_ref, qa_ref):
    lane = lax.broadcasted_iota(jnp.int32, (1, 128), 1)
    low = lane < HD
    fk, k2, v2 = fk_ref[...], k_ref[...], v_ref[...]
    keys = (jnp.where(low, k2, fk), jnp.where(low, fk, k2))
    values = (jnp.where(low, v2, fk), jnp.where(low, fk, v2))
    size = q_ref.shape[0] // 2
    for t in range(2):
        r = slice(t * size, (t + 1) * size)
        q2, fq = q_ref[r] * jnp.bfloat16(0.125), fq_ref[r]
        outs = []
        for h, qs in enumerate((jnp.where(low, q2, fq), jnp.where(low, fq, q2))):
            s = lax.dot_general(qs, keys[h], NT, preferred_element_type=jnp.float32)
            top = jnp.max(s, axis=1, keepdims=True)
            p = jnp.exp(s - top).astype(jnp.bfloat16)
            acc = lax.dot_general(p, values[h], NN, preferred_element_type=jnp.float32)
            base = HD + LSE_LANE if h == 0 else LSE_LANE
            total = acc[:, base : base + 1]
            outs.append(acc / total)
            qa = qs.astype(jnp.float32)
            for j, x in enumerate(split3(-(top + jnp.log(total)))):
                qa = jnp.where(lane == base + j, x, qa)
            qa_ref[h, r] = qa.astype(jnp.bfloat16)
        o = jnp.where(low, outs[0], outs[1])
        o_ref[r] = o
        ol_ref[r] = o.astype(jnp.bfloat16)


def attend(q, kv, fq, fk, heads=12):
    rows, d = q.shape
    nk, pairs = kv.shape[0], heads // 2
    row = pl.BlockSpec((rows, 128), lambda p: (0, p))
    return pl.pallas_call(
        fwd_kernel,
        grid=(pairs,),
        in_specs=[
            row,
            pl.BlockSpec((nk, 128), lambda p: (0, p)),
            pl.BlockSpec((nk, 128), lambda p: (0, p + pairs)),
            pl.BlockSpec((rows, 128), lambda p: (0, 0)),
            pl.BlockSpec((nk, 128), lambda p: (0, 0)),
        ],
        out_specs=[row, row, pl.BlockSpec((2, rows, 128), lambda p: (p, 0, 0))],
        out_shape=[
            jax.ShapeDtypeStruct((rows, d), jnp.float32),
            jax.ShapeDtypeStruct((rows, d), jnp.bfloat16),
            jax.ShapeDtypeStruct((heads, rows, 128), jnp.bfloat16),
        ],
        compiler_params=pltpu.CompilerParams(vmem_limit_bytes=60 << 20),
        cost_estimate=pl.CostEstimate(flops=rows, bytes_accessed=rows, transcendentals=0),
        name="attend",
    )(q, kv, kv, fq, fk)


def bwd_kernel(qa_ref, k_ref, v_ref, fk_ref, g_ref, o_ref, dq_ref, dk_ref, dv_ref, ds_ref):
    nk = k_ref.shape[0]
    lane = lax.broadcasted_iota(jnp.int32, (1, 128), 1)
    low = lane < HD
    g = g_ref[...].astype(jnp.float32)
    prod = g * o_ref[...]
    gs = []
    for h in range(2):
        own = low if h == 0 else jnp.logical_not(low)
        base = HD + LSE_LANE if h == 0 else LSE_LANE
        delta = jnp.sum(jnp.where(own, prod, 0.0), axis=1, keepdims=True)
        ga = jnp.where(own, g, 0.0)
        for j, t in enumerate(split3(-delta)):
            ga = jnp.where(lane == base + j, t, ga)
        gs.append(ga.astype(jnp.bfloat16))
    for at in range(0, nk, 3 * KB):
        r = slice(at, min(at + 3 * KB, nk))
        k2, v2, fk = k_ref[r], v_ref[r], fk_ref[r]
        dks, dvs = [], []
        for h in range(2):
            ka = jnp.where(low, k2, fk) if h == 0 else jnp.where(low, fk, k2)
            va = jnp.where(low, v2, fk) if h == 0 else jnp.where(low, fk, v2)
            pt = jnp.exp(lax.dot_general(ka, qa_ref[h], NT, preferred_element_type=jnp.float32))
            dpt = lax.dot_general(va, gs[h], NT, preferred_element_type=jnp.float32)
            ds = (pt * dpt).astype(jnp.bfloat16)
            ds_ref[h, r] = ds
            dvs.append(lax.dot_general(pt.astype(jnp.bfloat16), gs[h], NN, preferred_element_type=jnp.float32))
            dks.append(lax.dot_general(ds, qa_ref[h], NN, preferred_element_type=jnp.float32))
        dk_ref[r] = jnp.where(low, dks[0], dks[1]).astype(dk_ref.dtype)
        dv_ref[r] = jnp.where(low, dvs[0], dvs[1]).astype(dv_ref.dtype)
    kt = k_ref[...].T
    dqs = [lax.dot_general(kt, ds_ref[h], NN, preferred_element_type=jnp.float32) for h in range(2)]
    top = lax.broadcasted_iota(jnp.int32, (128, 1), 0) < HD
    dq_ref[...] = (jnp.where(top, dqs[0], dqs[1]).T * 0.125).astype(dq_ref.dtype)


def attend_back(qa, kv, fk, g, o, first, count, heads=12):
    rows, nk, pairs = g.shape[0], kv.shape[0], heads // 2
    row = pl.BlockSpec((rows, 128), lambda p: (0, p + first))
    key = pl.BlockSpec((nk, 128), lambda p: (0, p))
    return pl.pallas_call(
        bwd_kernel,
        grid=(count,),
        in_specs=[
            pl.BlockSpec((2, rows, 128), lambda p: (p + first, 0, 0)),
            pl.BlockSpec((nk, 128), lambda p: (0, p + first)),
            pl.BlockSpec((nk, 128), lambda p: (0, p + first + pairs)),
            pl.BlockSpec((nk, 128), lambda p: (0, 0)),
            row,
            row,
        ],
        out_specs=[pl.BlockSpec((rows, 128), lambda p: (0, p)), key, key],
        out_shape=[jax.ShapeDtypeStruct((n, 128 * count), jnp.bfloat16) for n in (rows, nk, nk)],
        scratch_shapes=[pltpu.VMEM((2, nk, rows), jnp.bfloat16)],
        compiler_params=pltpu.CompilerParams(vmem_limit_bytes=60 << 20),
        cost_estimate=pl.CostEstimate(flops=rows, bytes_accessed=rows, transcendentals=0),
        name="attend_back",
    )(qa, kv, kv, fk, g, o)


def features(seg_query,seg_key):
    j=jnp.arange(128,dtype=jnp.int32)[None,:]%HD
    fq=jnp.where((j<10)&(j!=seg_query[:,None]),NEG,0.0).astype(jnp.bfloat16)
    fk=(((j<10)&(j==seg_key[:,None]))|((j>=LSE_LANE)&(j<LSE_LANE+3))).astype(jnp.bfloat16)
    return fq,fk


D = 768
HEADS = 12
IMGS = 8
CLASS_ROWS = 256
WIDE = 384


def norm_rows(values, gain_row):
    centre = values - jnp.mean(values, axis=-1, keepdims=True)
    return centre * lax.rsqrt(jnp.mean(centre * centre, axis=-1, keepdims=True) + 1e-06) * gain_row


def class_norm(logits, gain_row):
    centre = logits - jnp.mean(logits, axis=-1, keepdims=True)
    return centre * lax.rsqrt(jnp.mean(centre * centre, axis=-1, keepdims=True) + 1e-05) * gain_row


def unit_rows(values):
    return values * lax.rsqrt(jnp.sum(values * values, axis=-1, keepdims=True) + 1e-06)


def dot(left, right):
    return jnp.dot(left, right, preferred_element_type=jnp.float32)


def dot_rows(left, right):
    return lax.dot_general(left, right, (((0,), (0,)), ((), ())), preferred_element_type=jnp.float32)


def dot_turned(left, right):
    return lax.dot_general(left, right, (((1,), (1,)), ((), ())), preferred_element_type=jnp.float32)


def low(values):
    return values.astype(jnp.bfloat16)


BOTH = ("dp", "seq")


def bits_of(count):
    return [1 << i for i in range(count.bit_length() - 1)]


def seq_bits():
    return bits_of(lax.axis_size("seq"))


def chip_bits():
    return bits_of(lax.axis_size("seq") * lax.axis_size("dp"))[1:]


def swap(values, mask):
    inner, outer = lax.axis_size("seq"), lax.axis_size("dp")
    place = [(i % inner) * outer + i // inner for i in range(inner * outer)]
    pairs = [(place[i], place[i ^ mask]) for i in range(inner * outer)]
    return lax.ppermute(values, ("seq", "dp"), pairs)


def own_bit(bit):
    return (lax.axis_index(BOTH) // bit) % 2


def masks_of(bits):
    masks = [0]
    for bit in bits:
        masks = masks + [m | bit for m in masks]
    return masks


def groups_of(bits):
    return [bits[i : i + 2] for i in range(0, len(bits), 2)]


def absolute(pieces, bits):
    for i, bit in enumerate(bits):
        same = own_bit(bit) == 0
        pieces = [jnp.where(same, p, pieces[k ^ (1 << i)]) for k, p in enumerate(pieces)]
    return pieces


def gather_rows(rows):
    for bit in reversed(seq_bits()):
        rows = jnp.concatenate([rows, swap(rows, bit)], axis=0)
    return rows


def relative():
    return masks_of(seq_bits()[::-1])


def segment_of(places, seq_lengths):
    count = seq_lengths.shape[0]
    before = jnp.arange(count)[None, :] <= jnp.arange(count)[:, None]
    boundary = jnp.sum(jnp.where(before, seq_lengths[None, :], 0), axis=1)
    return jnp.sum((places[:, None] >= boundary[None, :]).astype(jnp.int32), axis=1)


def from_sequence(mine):
    bits = seq_bits()
    return absolute([mine if m == 0 else swap(mine, m) for m in masks_of(bits)], bits)


def halve(total, bit, near, done):
    low_bits = 1 if len(near) - done == 1 else 1 << near.index(bit)
    values = total.reshape((total.shape[0] // (2 * low_bits), 2, low_bits) + total.shape[1:])
    own = own_bit(bit)
    arrived = swap(lax.dynamic_index_in_dim(values, 1 - own, 1, keepdims=False), bit)
    kept = lax.dynamic_index_in_dim(values, own, 1, keepdims=False)
    result = low(kept.astype(jnp.float32) + arrived.astype(jnp.float32))
    return result.reshape((-1,) + total.shape[1:])


def share_low(total, group, width):
    values = total.reshape((total.shape[0] // width, width) + total.shape[1:])
    own = lax.axis_index(BOTH)
    pieces = []
    for m in masks_of(group):
        place = ((own ^ m) // group[0]) % width
        piece = lax.dynamic_index_in_dim(values, place, 1, keepdims=False)
        pieces.append(piece if m == 0 else swap(piece, m))
    return sum(p.astype(jnp.float32) for p in pieces).astype(total.dtype)


BLOCKS = 16
PIECE = 48
TALL = 192
TN = (((0,), (0,)), ((), ()))


def cheap(rows):
    return pl.CostEstimate(flops=rows, bytes_accessed=rows, transcendentals=0)


def dot_nn(left, right):
    return lax.dot_general(left, right, NN, preferred_element_type=jnp.float32)


def dot_nt(left, right):
    return lax.dot_general(left, right, NT, preferred_element_type=jnp.float32)


def mat(chunk):
    return chunk.reshape(-1, WIDE)


def columns(c):
    return slice(c * WIDE, (c + 1) * WIDE)


def joined(chunk):
    return jnp.concatenate([mat(chunk[:, 0]), mat(chunk[:, 1])], axis=1)


def gelu_parts(u):
    root = math.sqrt(2.0 / math.pi)
    t = jnp.tanh(root * (u + 0.044715 * (u * u * u)))
    return 0.5 * (1.0 + t), 0.5 * u * (1.0 - t * t) * (root * (1.0 + (3 * 0.044715) * (u * u)))


def qkv_kernel(rows_ref, w_ref, kv_ref, q_ref):
    step = pl.program_id(0)
    weight = joined(w_ref[...])

    @pl.when(step < 2)
    def _():
        kv_ref[...] = dot_nn(rows_ref[...], weight).astype(kv_ref.dtype)

    @pl.when(step == 2)
    def _():
        q_ref[...] = dot_nn(rows_ref[: q_ref.shape[0]], weight).astype(q_ref.dtype)


def project(rows_all, own, weights, first):
    count = rows_all.shape[0]
    return pl.pallas_call(
        qkv_kernel,
        grid=(3,),
        in_specs=[
            pl.BlockSpec((count, D), lambda t: (0, 0)),
            pl.BlockSpec((BLOCKS, 2, PIECE, WIDE), lambda t: (0, 0, jnp.where(t < 2, first + 1 + t, first), 0)),
        ],
        out_specs=[
            pl.BlockSpec((count, D), lambda t: (0, jnp.minimum(t, 1))),
            pl.BlockSpec((own, D), lambda t: (0, 0)),
        ],
        out_shape=[
            jax.ShapeDtypeStruct((count, 2 * D), jnp.bfloat16),
            jax.ShapeDtypeStruct((own, D), jnp.bfloat16),
        ],
        compiler_params=pltpu.CompilerParams(vmem_limit_bytes=60 << 20),
        cost_estimate=cheap(own),
        name="project",
    )(rows_all, weights)


def halves(ref):
    half = ref.shape[0] // 2
    return (slice(0, half), slice(half, 2 * half))


def mlp_kernel(h_ref, o_ref, gain_ref, next_ref, wo_ref, wu_ref, wd_ref, mid_ref, sec_ref, u_ref, act_ref, res_ref, nrm_ref):
    step = pl.program_id(0)

    @pl.when(step == 0)
    def _():
        middle = h_ref[...].astype(jnp.float32) + dot_nn(o_ref[...], joined(wo_ref[...]))
        mid_ref[...] = middle
        sec_ref[...] = norm_rows(middle, gain_ref[...]).astype(sec_ref.dtype)
        res_ref[...] = middle

    up = jnp.concatenate([mat(wu_ref[:, 0, :PIECE]), mat(wu_ref[:, 0, PIECE:])], axis=1)
    down = joined(wd_ref[...])
    for part in halves(sec_ref):
        u = dot_nn(sec_ref[part], up)
        u_ref[part] = u.astype(u_ref.dtype)
        active_part = (u * gelu_parts(u)[0]).astype(act_ref.dtype)
        act_ref[part] = active_part
        res_ref[part] += dot_nn(active_part, down)

    @pl.when(step == 3)
    def _():
        nrm_ref[...] = norm_rows(res_ref[...], next_ref[...]).astype(nrm_ref.dtype)


def mlp_specs(out_piece):
    return [
        pl.BlockSpec((BLOCKS, 2, PIECE, WIDE), lambda t: (0, 0, out_piece, 0)),
        pl.BlockSpec((BLOCKS, 1, 2 * PIECE, WIDE), lambda t: (0, t // 2, 2 + t % 2, 0)),
        pl.BlockSpec((BLOCKS // 4, 2, TALL, WIDE), lambda t: (t, 0, 0, 0)),
    ]


def whole(shape):
    return pl.BlockSpec(shape, lambda t: (0,) * len(shape))


def feed_forward(hidden, attended, gain, next_gain, w_out, out_piece, w_mlp):
    rows = hidden.shape[0]
    full, tile = (rows, D), pl.BlockSpec((rows, D), lambda t: (0, t))
    return pl.pallas_call(
        mlp_kernel,
        grid=(4,),
        in_specs=[whole(full), whole(full), whole((1, D)), whole((1, D)), *mlp_specs(out_piece)],
        out_specs=[whole(full), whole(full), tile, tile, whole(full), whole(full)],
        out_shape=[
            jax.ShapeDtypeStruct(full, jnp.float32),
            jax.ShapeDtypeStruct(full, jnp.bfloat16),
            jax.ShapeDtypeStruct((rows, 4 * D), jnp.bfloat16),
            jax.ShapeDtypeStruct((rows, 4 * D), jnp.bfloat16),
            jax.ShapeDtypeStruct(full, jnp.float32),
            jax.ShapeDtypeStruct(full, jnp.bfloat16),
        ],
        compiler_params=pltpu.CompilerParams(vmem_limit_bytes=60 << 20),
        cost_estimate=cheap(rows),
        name="feed_forward",
    )(hidden, attended, gain[None], next_gain[None], w_out, w_mlp, w_mlp)


def norm_back(grad, values, gain):
    centre = values - jnp.mean(values, axis=-1, keepdims=True)
    scale = lax.rsqrt(jnp.mean(centre * centre, axis=-1, keepdims=True) + 1e-06)
    unit = centre * scale
    inner = grad * gain
    inner = inner - jnp.mean(inner, axis=-1, keepdims=True) - unit * jnp.mean(inner * unit, axis=-1, keepdims=True)
    return inner * scale, grad * unit


def mlp_back_kernel(g_ref, u_ref, mid_ref, gain_ref, wo_ref, wu_ref, wd_ref, gb_ref, gu_ref, gm_ref, ga_ref, gat_ref, gg_ref, acc):
    step = pl.program_id(0)

    @pl.when(step == 0)
    def _():
        gb_ref[...] = g_ref[...].astype(gb_ref.dtype)
        acc[...] = jnp.zeros(acc.shape, jnp.float32)

    up = jnp.concatenate([mat(wu_ref[:, 0, :PIECE]), mat(wu_ref[:, 0, PIECE:])], axis=1)
    down = joined(wd_ref[...])
    for part in halves(gb_ref):
        grad = dot_nt(gb_ref[part], down)
        gu = (grad * sum(gelu_parts(u_ref[part].astype(jnp.float32)))).astype(gu_ref.dtype)
        gu_ref[part] = gu
        acc[part] += dot_nt(gu, up)

    @pl.when(step == 3)
    def _():
        back, gain_rows = norm_back(acc[...], mid_ref[...], gain_ref[...])
        middle = back + g_ref[...]
        gm_ref[...] = middle
        gg_ref[...] = jnp.sum(gain_rows, axis=0, keepdims=True)
        low_middle = middle.astype(ga_ref.dtype)
        ga_ref[...] = low_middle
        gat_ref[...] = dot_nt(low_middle, joined(wo_ref[...])).astype(gat_ref.dtype)


def feed_forward_back(grad, upward, middle, gain, w_out, out_piece, w_mlp):
    rows = grad.shape[0]
    full, tile = (rows, D), pl.BlockSpec((rows, D), lambda t: (0, t))
    return pl.pallas_call(
        mlp_back_kernel,
        grid=(4,),
        in_specs=[whole(full), tile, whole(full), whole((1, D)), *mlp_specs(out_piece)],
        out_specs=[whole(full), tile, whole(full), whole(full), whole(full), whole((1, D))],
        out_shape=[
            jax.ShapeDtypeStruct(full, jnp.bfloat16),
            jax.ShapeDtypeStruct((rows, 4 * D), jnp.bfloat16),
            jax.ShapeDtypeStruct(full, jnp.float32),
            jax.ShapeDtypeStruct(full, jnp.bfloat16),
            jax.ShapeDtypeStruct(full, jnp.bfloat16),
            jax.ShapeDtypeStruct((1, D), jnp.float32),
        ],
        scratch_shapes=[pltpu.VMEM(full, jnp.float32)],
        compiler_params=pltpu.CompilerParams(vmem_limit_bytes=60 << 20),
        cost_estimate=cheap(rows),
        name="feed_forward_back",
    )(grad, upward, middle, gain[None], w_out, w_mlp, w_mlp)


def rows_back_kernel(steps, half, dk0, dk1, dv0, dv1, dq0, dq1, wq_ref, wk_ref, wv_ref, near_ref, far_ref, full):
    step = pl.program_id(0)

    @pl.when(step == 0)
    def _():
        full[:, :D] = joined(wk_ref[...])
        full[:, D:] = joined(wv_ref[...])

    rows = jnp.concatenate([dk0[...], dk1[...], dv0[...], dv1[...]], axis=1)
    total = dot_nt(rows, full[...])
    away = (step >= half) & (step < 2 * half)

    @pl.when(away)
    def _():
        far_ref[...] = total.astype(far_ref.dtype)

    @pl.when(jnp.logical_not(away))
    def _():
        near_ref[...] = total

    @pl.when(step < steps)
    def _():
        near_ref[...] += dot_nt(jnp.concatenate([dq0[...], dq1[...]], axis=1), joined(wq_ref[...]))


def rows_back(one, two, weights, first):
    count, size = one[1].shape[0], one[0].shape[0]
    tokens = count // size * size
    if count != tokens:
        size = math.gcd(count, size)
    steps, half = one[0].shape[0] // size, tokens // (2 * size)
    tile = pl.BlockSpec((size, WIDE), lambda t: (t, 0))
    query = pl.BlockSpec((size, WIDE), lambda t: (jnp.minimum(t, steps - 1), 0))
    piece = lambda i: pl.BlockSpec((BLOCKS, 2, PIECE, WIDE), lambda t: (0, 0, first + i, 0))
    near = lambda t: (jnp.where(t < half, t, jnp.where(t < 2 * half, half, t - half)), 0)
    far = lambda t: (jnp.clip(t - half, 0, half - 1), 0)
    rest = count - half * size
    spare = rest + size if count == tokens else rest
    return pl.pallas_call(
        functools.partial(rows_back_kernel, steps, half),
        grid=(count // size,),
        in_specs=[tile, tile, tile, tile, query, query, piece(0), piece(1), piece(2)],
        out_specs=[pl.BlockSpec((size, D), near), pl.BlockSpec((size, D), far)],
        out_shape=[
            jax.ShapeDtypeStruct((spare, D), jnp.float32),
            jax.ShapeDtypeStruct((half * size, D), jnp.bfloat16),
        ],
        scratch_shapes=[pltpu.VMEM((D, 2 * D), jnp.bfloat16)],
        compiler_params=pltpu.CompilerParams(vmem_limit_bytes=60 << 20),
        cost_estimate=cheap(size),
        name="rows_back",
    )(one[1], two[1], one[2], two[2], one[0], two[0], weights, weights, weights)


def products_kernel(plan, count_in, outs, *refs):
    ins, turned = refs[outs - 1 : outs - 1 + count_in], refs[-1]
    out_refs = refs[-1 - outs : -1]
    step = pl.program_id(0)
    for left, rights, begin, tiles, tall in plan:
        count = ins[left].shape[0]

        @pl.when(step == begin)
        def _():
            for i in range(0, ins[left].shape[1], D):
                part = ins[left][:, i : i + D].T
                if tall:
                    turned[i // TALL : (i + D) // TALL, :, :count] = part.reshape(D // TALL, TALL, count)
                else:
                    turned[:, :PIECE, :count] = part.reshape(BLOCKS, PIECE, count)

        @pl.when((step >= begin) & (step < begin + tiles))
        def _():
            n = step - begin
            if tall:
                at = pl.multiple_of(n * PIECE, PIECE)
                rows = turned[:, pl.ds(at, PIECE), :count].reshape(D, count)
            else:
                rows = turned[:, :PIECE, :count].reshape(D, count)
            if len(rights) == 2:
                right = jnp.concatenate([ins[r][...] for r in rights], axis=1)
            elif tall or tiles == 1:
                right = ins[rights[0]][...]
            else:
                half = tiles * WIDE
                parts = [
                    ins[rights[0]][:, pl.ds(pl.multiple_of(n * WIDE + c * half, WIDE), WIDE)] for c in range(2)
                ]
                right = jnp.concatenate(parts, axis=1)
            part = dot_nn(rows, right).astype(jnp.bfloat16)
            chunk = [part[:, columns(c)].reshape(BLOCKS, PIECE, WIDE) for c in range(2)]
            if outs == 1:
                for c in range(2):
                    out_refs[0][:, c] = chunk[c]
            else:
                for core in range(2):

                    @pl.when(refs[0][0] == core)
                    def _():
                        out_refs[0][...] = chunk[1 - core]
                        out_refs[1][...] = chunk[core]


def products(wanted, core=None, into=(), first=0, pieces=None):
    arrays, plan, steps = [], [], 0

    def place(array):
        for i, known in enumerate(arrays):
            if known is array:
                return i
        arrays.append(array)
        return len(arrays) - 1

    for left, rights in wanted:
        tall = left.shape[1] != D
        tiles = left.shape[1] // D if tall else sum(r.shape[1] for r in rights) // D
        plan.append((place(left), [place(r) for r in rights], steps, tiles, tall))
        steps += tiles
    longest = max(left.shape[0] for left, _ in wanted)
    height = TALL if any(p[4] for p in plan) else PIECE
    rows = (pieces or steps) * PIECE
    outs = 1 if core is None else 2
    if core is None:
        block, shape = (BLOCKS, 2, PIECE, WIDE), (BLOCKS, 2, rows, WIDE)
        where = lambda t: (0, 0, first + t, 0)
    else:
        block, shape = (BLOCKS, PIECE, WIDE), (BLOCKS, rows, WIDE)
        where = lambda t, _: (0, first + t, 0)
    spec = pltpu.PrefetchScalarGridSpec(
        num_scalar_prefetch=outs - 1,
        grid=(steps,),
        in_specs=[pl.BlockSpec(a.shape, lambda t, *_: (0, 0), pipeline_mode=pl.Buffered(1)) for a in arrays]
        + [pl.BlockSpec(memory_space=pl.ANY)] * len(into),
        out_specs=[pl.BlockSpec(block, where)] * outs,
        scratch_shapes=[pltpu.VMEM((BLOCKS, height, longest), jnp.bfloat16)],
    )
    result = pl.pallas_call(
        functools.partial(products_kernel, plan, len(arrays), outs),
        grid_spec=spec,
        out_shape=[jax.ShapeDtypeStruct(shape, jnp.bfloat16)] * outs,
        input_output_aliases={outs - 1 + len(arrays) + i: i for i in range(len(into))},
        compiler_params=pltpu.CompilerParams(vmem_limit_bytes=60 << 20),
        cost_estimate=cheap(longest),
        name="products",
    )(*([] if core is None else [core.reshape(1)]), *arrays, *into)
    return result[0] if core is None else result


def to_blocks(gathered, sizes):
    places = gathered.shape[0] // 2
    chunks = gathered.reshape(places, 2, -1, WIDE)
    if places == BLOCKS:
        return chunks
    pieces, at = [], 0
    for size in sizes:
        rows = size * BLOCKS // places
        part = chunks[:, :, at : at + rows].reshape(BLOCKS, -1, 2, rows, WIDE)
        pieces.append(part.transpose(0, 2, 1, 3, 4).reshape(BLOCKS, 2, size, WIDE))
        at += rows
    return jnp.concatenate(pieces, axis=2)


def from_blocks(chunks, sizes):
    places = 1 << len(chip_bits())
    if places == BLOCKS:
        return chunks
    pieces, at = [], 0
    for size in sizes:
        rows = size * BLOCKS // places
        part = chunks[:, :, at : at + size].reshape(BLOCKS, 2, -1, rows, WIDE)
        pieces.append(part.transpose(0, 2, 1, 3, 4).reshape(places, 2, rows, WIDE))
        at += size
    return jnp.concatenate(pieces, axis=2)


def bundle(shards):
    chips, index = lax.axis_size("seq") // 2, lax.axis_index("seq")
    pieces = []
    for shard in shards:
        rows, half = shard.shape[0] // chips, shard.shape[1] // 2
        part = lax.dynamic_slice(shard, (index // 2 * rows, index % 2 * half), (rows, half))
        pieces += [part[:, i : i + WIDE] for i in range(0, half, WIDE)]
    return jnp.concatenate(pieces, axis=0)


def sizes_of(shards):
    tall = lambda s: s.shape[0] * lax.axis_size("dp") // BLOCKS
    return [tall(s) for s in shards for _ in range(0, s.shape[1] // 2, WIDE)]


def thirds_of(shard):
    return [shard[:, i : i + D] for i in range(0, 3 * D, D)]


def gather_weights(shards):
    return lax.all_gather(bundle(shards), BOTH, axis=0)


def gather_first(shards, after):
    values = bundle(shards)
    rows = values.shape[0]
    values = values[None]
    for step, group in enumerate(reversed(groups_of(chip_bits()))):
        pieces = [values if m == 0 else swap(values, m) for m in masks_of(group)]
        if step == 0:
            pieces, after = lax.optimization_barrier((pieces, after))
        values = jnp.stack(absolute(pieces, group), axis=1).reshape(-1, rows, WIDE)
    values = jnp.stack(absolute([values, swap(values, 1)], [1]), axis=1)
    return to_blocks(values.reshape(-1, rows, WIDE), sizes_of(shards)), after


def collect_kernel(plan, own_ref, *refs):
    count = len(refs) - len({p[3] for p in plan})
    ins, outs = refs[:count], refs[count:]
    for own in range(count):

        @pl.when(own_ref[0] == own)
        def _():
            for device in range(count):
                y, core = device // 2, device % 2
                for half, at, rows, out, column in plan:
                    if half == core:
                        part = ins[device ^ own][at : at + rows].astype(jnp.float32)
                        outs[out][y * rows : (y + 1) * rows, column : column + WIDE] = part


def collect(mine, wanted, outs):
    bits = seq_bits()
    held = {0: mine}
    for bit in reversed(bits):
        held.update({m | bit: swap(t, bit) for m, t in list(held.items())})
    pieces = [held[m] for m in masks_of(bits)]
    places = 1 << len(chip_bits())
    plan, shapes, at = [], {}, 0
    for (height, width), out in zip(wanted, outs):
        rows, half = height // places, width // 2
        begin = shapes.get(out, (0, 0))[1]
        for i in range(0, half, WIDE):
            plan += [(core, at, rows, out, begin + core * half + i) for core in range(2)]
            at += rows
        shapes[out] = (height // lax.axis_size("dp"), begin + width)
    if any(p[2] % 16 for p in plan):
        shares = absolute(pieces, bits)
        results = [jnp.zeros(shape, jnp.float32) for shape in shapes.values()]
        for core, at, rows, out, column in plan:
            for y, share in enumerate(shares[core::2]):
                part = share[at : at + rows].astype(jnp.float32)
                results[out] = results[out].at[y * rows : (y + 1) * rows, column : column + WIDE].set(part)
        return results, pieces
    spec = pltpu.PrefetchScalarGridSpec(
        num_scalar_prefetch=1,
        grid=(1,),
        in_specs=[pl.BlockSpec(mine.shape, lambda t, own: (0, 0)) for _ in pieces],
        out_specs=[pl.BlockSpec(shape, lambda t, own: (0, 0)) for shape in shapes.values()],
    )
    results = pl.pallas_call(
        functools.partial(collect_kernel, plan),
        grid_spec=spec,
        out_shape=[jax.ShapeDtypeStruct(shape, jnp.float32) for shape in shapes.values()],
        compiler_params=pltpu.CompilerParams(vmem_limit_bytes=60 << 20),
        cost_estimate=cheap(D),
        name="collect",
    )(lax.axis_index("seq").reshape(1), *pieces)
    return results, pieces


def across(pieces):
    shares = absolute(pieces, seq_bits())
    rows = jnp.concatenate([jnp.concatenate(shares[i : i + 2], axis=1) for i in range(0, len(shares), 2)], axis=0)
    total = rows[None]
    for group in groups_of(chip_bits()[len(seq_bits()) - 1 :]):
        total = jnp.stack(absolute([total if m == 0 else swap(total, m) for m in masks_of(group)], group), axis=0)
        total = total.reshape((-1,) + rows.shape)
    return total.reshape(-1, rows.shape[1])


def scatter_sums(chunks):
    return lax.psum_scatter(chunks.reshape((-1,) + chunks.shape[2:]), BOTH, scatter_dimension=0)


def add_and_part_kernel(cut, own_ref, keep_ref, arrived_ref, *outs):
    def total(index, rows):
        return (keep_ref[index, rows].astype(jnp.float32) + arrived_ref[index, rows].astype(jnp.float32)).astype(jnp.bfloat16)

    first, second = slice(0, cut), slice(cut, None)
    y, x = own_ref[0], own_ref[1]
    for i in range(2):
        outs[0][i] = total(2 * i + 1 - y, first)
        outs[1][i] = total(2 * i + y, first)
        outs[2][i] = total(2 - 2 * x + i, second)
        outs[3][i] = total(2 * x + i, second)


def add_and_part(keep, arrived, cut):
    places, rows, _ = keep.shape
    bits = chip_bits()
    four = pl.BlockSpec((4, rows, WIDE), lambda t, _: (t, 0, 0))
    heights = (cut, cut, rows - cut, rows - cut)
    spec = pltpu.PrefetchScalarGridSpec(
        num_scalar_prefetch=1,
        grid=(places // 4,),
        in_specs=[four, four],
        out_specs=[pl.BlockSpec((2, h, WIDE), lambda t, _: (t, 0, 0)) for h in heights],
    )
    return pl.pallas_call(
        functools.partial(add_and_part_kernel, cut),
        grid_spec=spec,
        out_shape=[jax.ShapeDtypeStruct((places // 2, h, WIDE), jnp.bfloat16) for h in heights],
        compiler_params=pltpu.CompilerParams(vmem_limit_bytes=40 << 20),
        cost_estimate=cheap(D),
        name="add_and_part",
    )(jnp.stack([own_bit(bits[0]), own_bit(bits[1])]), keep, arrived)


def add_and_halve_kernel(own_ref, keep_ref, arrived_ref, going_ref, kept_ref):
    own = own_ref[0]
    for ref, index in ((going_ref, 1 - own), (kept_ref, own)):
        ref[0] = (keep_ref[index].astype(jnp.float32) + arrived_ref[index].astype(jnp.float32)).astype(jnp.bfloat16)


def add_and_halve(keep, arrived, own):
    places, rows, _ = keep.shape
    pair = pl.BlockSpec((2, rows, WIDE), lambda t, _: (t, 0, 0))
    one = pl.BlockSpec((1, rows, WIDE), lambda t, _: (t, 0, 0))
    spec = pltpu.PrefetchScalarGridSpec(
        num_scalar_prefetch=1, grid=(places // 2,), in_specs=[pair, pair], out_specs=[one, one]
    )
    return pl.pallas_call(
        add_and_halve_kernel,
        grid_spec=spec,
        out_shape=[jax.ShapeDtypeStruct((places // 2, rows, WIDE), jnp.bfloat16)] * 2,
        compiler_params=pltpu.CompilerParams(vmem_limit_bytes=40 << 20),
        cost_estimate=cheap(D),
        name="add_and_halve",
    )(own.reshape(1), keep, arrived)


def stepped_sums(send, keep, sizes, classes):
    if classes == 2 and 1 << len(chip_bits()) == BLOCKS:
        bits = chip_bits()
        cut = keep.shape[1] // 2
        parts = yield add_and_part(keep, swap(send, 1), cut)
        ways = (bits[0], bits[1])
        parts = yield [
            part
            for way, other, (going, kept) in zip(ways, ways[::-1], (parts[:2], parts[2:]))
            for part in add_and_halve(kept, swap(going, way), own_bit(other))
        ]
        total = [
            low(kept.astype(jnp.float32) + swap(going, way).astype(jnp.float32))
            for way, (going, kept) in zip(ways[::-1], (parts[:2], parts[2:]))
        ]
        total = (yield [jnp.concatenate(total, axis=1)])[0]
        for group in groups_of(bits[2:]):
            total = (yield [share_low(total, group, 1 << len(group))])[0]
        return total[0]
    if 1 << len(chip_bits()) != BLOCKS:
        chunks = from_blocks(jnp.stack([send, keep], axis=1), sizes)
        send, keep = chunks[:, 0], chunks[:, 1]
    arrived = swap(send, 1)
    total = low(keep.astype(jnp.float32) + arrived.astype(jnp.float32))
    bits = chip_bits()
    if classes == 2:
        near, bits = bits[:2], bits[2:]
        cut = total.shape[1] // 2
        parts = yield [total[:, :cut], total[:, cut:]]
        for i in range(2):
            parts = yield [halve(t, bit, near, i) for t, bit in zip(parts, (near[i], near[1 - i]))]
        total = jnp.concatenate(parts, axis=1)
    else:
        total = (yield [total])[0]
    for group in groups_of(bits):
        total = (yield [share_low(total, group, 1 << len(group))])[0]
    return total[0]


def everywhere(values):
    for group in groups_of([1] + chip_bits()):
        values = sum(values if m == 0 else swap(values, m) for m in masks_of(group))
        values = (yield [values])[0]
    return values


def waited(values):
    return (yield [values])[0]


class Running:
    def __init__(self, steps):
        self.steps, self.values, self.result = steps, None, None
        self.go(None)

    def go(self, values):
        try:
            self.values = self.steps.send(values)
        except StopIteration as end:
            self.values, self.result = [], end.value

    def finish(self):
        while self.result is None:
            self.go(self.values)
        return self.result


def tie(values, *running):
    values, held = lax.optimization_barrier((values, [r.values for r in running]))
    for r, h in zip(running, held):
        if r.result is None:
            r.go(h)
    return values


def attention_backward(grad_attended, kept, mask, between):
    feature_k = mask[1]
    keyval, attended, kept_q = kept
    pairs = HEADS // 2
    cut = pairs // 2
    one = attend_back(kept_q, keyval, feature_k, grad_attended, attended, 0, cut)
    one, grad_attended = between((one, grad_attended))
    two = attend_back(kept_q, keyval, feature_k, grad_attended, attended, cut, pairs - cut)
    return one, two


def summed_rows(near, far):
    rows = near[: far.shape[0]] + swap(far, 1).astype(jnp.float32)
    for bit in seq_bits()[1:-1]:
        half = rows.shape[0] // 2
        rows = rows[:half] + swap(low(rows[half:]), bit).astype(jnp.float32)
    half = rows.shape[0] // 2
    return rows[:half], low(rows[half:])


def local(
    tokens,
    lengths,
    classes,
    norm_gains,
    mask_gain,
    enc_qkv,
    enc_out,
    enc_up,
    enc_down,
    dec_qkv,
    dec_out,
    dec_up,
    dec_down,
    patch_proj,
    class_proj,
    mask_cot,
):
    w_first, (tokens, lengths) = gather_first(thirds_of(enc_qkv), (tokens, lengths))
    middle_shards = (enc_down, enc_up, enc_out, *thirds_of(dec_qkv), dec_out)
    last_shards = (dec_down, dec_up, patch_proj, class_proj)
    w_middle = to_blocks(gather_weights(middle_shards), sizes_of(middle_shards))
    gathered_last = gather_weights(last_shards)
    core = own_bit(1)
    row_count = tokens.shape[1]
    index = lax.axis_index("seq")
    seq_lengths = lengths[0]
    inputs_f = tokens[0].astype(jnp.float32)
    gains_f = norm_gains.astype(jnp.float32)
    classes_f = classes.astype(jnp.float32)
    class_count = classes.shape[0]
    mask_gain_f = mask_gain.astype(jnp.float32)
    steps = jnp.arange(row_count, dtype=jnp.int32)
    seg_query = segment_of(index * row_count + steps, seq_lengths)
    starts = jnp.stack([(index ^ r) * row_count for r in relative()])
    seg_rows = segment_of((starts[:, None] + steps[None, :]).reshape(-1), seq_lengths)
    class_slots = jnp.arange(CLASS_ROWS, dtype=jnp.int32)
    seg_key = jnp.concatenate([seg_rows, jnp.where(class_slots < class_count, -1, IMGS + 1)])
    feature_q, feature_k = features(seg_query, seg_key)
    enc_mask = (feature_q, feature_k[: seg_rows.shape[0]])
    dec_mask = (feature_q, feature_k)
    valid_rows = (seg_query < IMGS).astype(jnp.float32)[:, None]
    enc_normed = low(norm_rows(inputs_f, gains_f[0]))
    enc_rows = gather_rows(enc_normed)
    keyval, queries = project(enc_rows, row_count, w_first, 0)
    attended, attended_low, kept_q = attend(queries, keyval, *enc_mask)
    enc_attn = (keyval, attended, kept_q)
    enc_low = attended_low
    enc_middle, enc_second, enc_upward, enc_active, encoded, dec_normed = feed_forward(
        tokens[0], attended_low, gains_f[1], gains_f[2], w_middle, 8, w_middle
    )
    class_normed = low(norm_rows(classes_f, gains_f[2]))
    class_padded = jnp.pad(class_normed, ((0, CLASS_ROWS - class_count), (0, 0)))
    dec_rows = jnp.concatenate([gather_rows(dec_normed), class_padded], axis=0)
    keyval, queries = project(dec_rows, row_count, w_middle, 9)
    attended, dec_low, kept_q = attend(queries, keyval, *dec_mask)
    dec_attn = (keyval, attended, kept_q)
    gathered_last, dec_low = lax.optimization_barrier((gathered_last, dec_low))
    w_last = to_blocks(gathered_last, sizes_of(last_shards))
    dec_middle, dec_second, dec_upward, dec_active, decoded, final_normed = feed_forward(
        encoded, dec_low, gains_f[3], gains_f[4], w_middle, 12, w_last
    )
    w_patch, w_class = (
        jnp.concatenate([w_last[:, c, at : at + PIECE].reshape(D, WIDE) for c in range(2)], axis=1)
        for at in (2 * TALL, 2 * TALL + PIECE)
    )
    patch_rows = low(dot(final_normed, w_patch))
    class_rows = dot(classes, w_class)
    class_unit = low(unit_rows(class_rows))
    logits = dot_turned(patch_rows, class_unit)
    mask_out = class_norm(logits, mask_gain_f) * valid_rows
    _, head_back = jax.vjp(class_norm, logits, mask_gain_f)
    grad_logits, grad_mask_gain = head_back(mask_cot[0] * valid_rows)
    grad_logits_low = low(grad_logits)
    grad_patch_rows = low(dot(grad_logits_low, class_unit))
    grad_unit = dot_rows(grad_logits_low, patch_rows)
    grad_final = dot_turned(grad_patch_rows, w_patch)
    _, final_back = jax.vjp(norm_rows, decoded, gains_f[4])
    grad_decoded, grad_gain_last = final_back(grad_final)
    _, unit_back = jax.vjp(unit_rows, class_rows)
    grad_class_rows = low(unit_back(grad_unit)[0])
    grad_classes = dot_turned(grad_class_rows, w_class)
    grad_branch, grad_upward, grad_middle, grad_attn, grad_attended, grad_gain_three = feed_forward_back(
        grad_decoded, dec_upward, dec_middle, gains_f[3], w_middle, 12, w_last
    )
    pad_classes = ((0, CLASS_ROWS - class_count), (0, 0))
    dec_chunks = products(
        [
            (dec_active, [grad_branch]),
            (dec_second, [grad_upward]),
            (dec_low, [grad_attn]),
            (final_normed, [grad_patch_rows]),
            (jnp.pad(classes, pad_classes), [jnp.pad(grad_class_rows, pad_classes)]),
        ]
    )
    dec_chunks, grad_attended = lax.optimization_barrier((dec_chunks, grad_attended))
    dec_sum = scatter_sums(from_blocks(dec_chunks, [TALL] + 7 * [PIECE]))
    one, two = attention_backward(grad_attended, dec_attn, dec_mask, lambda v: v)
    near, far = rows_back(one, two, w_middle, 9)
    here, going = summed_rows(near, far)
    going, one, two = lax.optimization_barrier((going, one, two))
    coming = swap(going, seq_bits()[-1])
    dec_qkv_chunks = products(
        [(dec_normed, [one[0], two[0]]), (dec_rows, [one[1], two[1]]), (dec_rows, [one[2], two[2]])],
        core,
        first=9,
        pieces=12,
    )
    _, class_back = jax.vjp(norm_rows, classes_f, gains_f[2])
    grad_classes_kv, grad_gain_class = class_back(near[far.shape[0] : far.shape[0] + class_count])
    coming, dec_qkv_chunks = lax.optimization_barrier((coming, dec_qkv_chunks))
    back, gain_rows = norm_back(here + coming.astype(jnp.float32), encoded, gains_f[2])
    grad_encoded = back + grad_middle
    padded_mask_gain = jnp.pad(grad_mask_gain, (0, D - class_count))
    shared = jnp.concatenate(
        [
            grad_classes + grad_classes_kv,
            jnp.stack(
                [jnp.sum(gain_rows, axis=0) + grad_gain_class, grad_gain_three[0], grad_gain_last, padded_mask_gain]
            ),
        ],
        axis=0,
    )
    per_block = CLASS_ROWS // BLOCKS
    shared = low(jnp.pad(shared, ((0, CLASS_ROWS - shared.shape[0]), (0, 0))))
    shared = shared.reshape(BLOCKS, per_block, 2, WIDE).transpose(0, 2, 1, 3)
    grad_branch, grad_upward, grad_middle, grad_attn, grad_attended, grad_gain_one = feed_forward_back(
        grad_encoded, enc_upward, enc_middle, gains_f[1], w_middle, 8, w_middle
    )
    enc_chunks = products(
        [(enc_active, [grad_branch]), (enc_second, [grad_upward]), (enc_low, [grad_attn])],
        core,
        into=dec_qkv_chunks,
        pieces=12,
    )
    enc_chunks, grad_attended = lax.optimization_barrier((enc_chunks, grad_attended))
    enc_sum = Running(stepped_sums(*enc_chunks, [TALL] + 8 * [PIECE], 2))
    dec_sum = Running(waited(dec_sum))
    one, two = attention_backward(grad_attended, enc_attn, enc_mask, lambda v: tie(v, enc_sum))
    one, two = tie((one, two), dec_sum)
    here, going = summed_rows(*rows_back(one, two, w_first, 0))
    going, one, two = tie((going, one, two), enc_sum)
    coming = swap(going, seq_bits()[-1])
    enc_qkv_chunks = products(
        [(enc_normed, [one[0], two[0]]), (enc_rows, [one[1], two[1]]), (enc_rows, [one[2], two[2]])],
        core,
    )
    enc_qkv_chunks, coming, enc_sum.values = lax.optimization_barrier((enc_qkv_chunks, coming, enc_sum.values))
    enc_qkv_chunks = [
        jnp.concatenate([t, lax.dynamic_index_in_dim(shared, c, 1, keepdims=False)], axis=1)
        for t, c in zip(enc_qkv_chunks, (1 - core, core))
    ]
    enc_proj = Running(stepped_sums(*enc_qkv_chunks, 3 * [PIECE] + [per_block], 1))
    here, coming = tie((here, coming), enc_proj, enc_sum)
    back, gain_rows = norm_back(here + coming.astype(jnp.float32), inputs_f, gains_f[0])
    grad_inputs = back + grad_middle
    gain_rows, dec_sum = tie((gain_rows, dec_sum.finish()), enc_proj, enc_sum)
    late = Running(everywhere(jnp.stack([jnp.sum(gain_rows, axis=0), grad_gain_one[0]])))
    square, wide, tall = (D, D), (D, 4 * D), (4 * D, D)
    qkv = [square, square, square]
    (out_enc_qkv,), shares = collect(enc_proj.finish(), qkv, [0, 0, 0])
    shared = across([t[-(per_block * BLOCKS >> len(chip_bits())) :] for t in shares]).astype(jnp.float32)
    late = late.finish()
    outs, _ = collect(
        jnp.concatenate([dec_sum, enc_sum.finish()], axis=0),
        [tall, wide, square, square, square, tall, wide, square] + qkv,
        [0, 1, 2, 3, 4, 5, 6, 7, 8, 8, 8],
    )
    out_dec, out_enc = outs[:5], outs[5:]
    out_dec_qkv = out_enc[3]
    gain_sums = jnp.concatenate([late, shared[class_count : class_count + 3]], axis=0)
    return (
        mask_out[None],
        grad_inputs[None],
        shared[:class_count],
        gain_sums,
        shared[class_count + 3, :class_count],
        out_enc_qkv,
        out_enc[2],
        out_enc[1],
        out_enc[0],
        out_dec_qkv,
        out_dec[2],
        out_dec[1],
        out_dec[0],
        out_dec[3],
        out_dec[4],
    )


def solution(mesh):
    placed = (
        P("dp", "seq", None),
        P("dp", None),
        P(),
        P(),
        P(),
        P("dp", None),
        P("dp", None),
        P("dp", None),
        P("dp", None),
        P("dp", None),
        P("dp", None),
        P("dp", None),
        P("dp", None),
        P("dp", None),
        P("dp", None),
        P("dp", "seq", None),
    )
    return jax.shard_map(
        local,
        mesh=mesh,
        in_specs=placed,
        out_specs=(
            P("dp", "seq", None),
            P("dp", "seq", None),
            P(),
            P(),
            P(),
            P("dp", None),
            P("dp", None),
            P("dp", None),
            P("dp", None),
            P("dp", None),
            P("dp", None),
            P("dp", None),
            P("dp", None),
            P("dp", None),
            P("dp", None),
        ),
        check_vma=False,
    )
```
